32 devices in a mesh: dp: 8 (over y, x, core), tensor: 4 (over z).
Axes of the slice: x: 2, y: 2, z: 4, core: 2. Of those that a mesh axis runs over, the one named last changes fastest.
Arguments:
- hidden_in: float32 [4096, 1024], P('dp'), may hold values from -6 to 6
- doc_ids: int32 [4096], P('dp'), may hold values from 0 to 7, never falling along the last dimension, each value on 1 to 1024 neighbouring positions
- attend_weight: bfloat16 [2, 1024, 3, 1024], P(None, 'dp', None, 'tensor'), may hold values from -0.1875 to 0.1875
- attend_bias: bfloat16 [2, 2, 1024], P(None, None, ('tensor', 'dp')), may hold values from -3 to 3
- output_weight: bfloat16 [2, 1024, 1024], P(None, ('tensor', 'dp')), may hold values from -0.75 to 0.75
- branch_bias: bfloat16 [2, 2, 1024], P(None, None, 'dp'), may hold values from -3 to 3
- expand_weight: bfloat16 [2, 1024, 4096], P(None, 'dp', 'tensor'), may hold values from -0.1875 to 0.1875
- expand_bias: bfloat16 [2, 4096], P(None, ('tensor', 'dp')), may hold values from -3 to 3
- reduce_weight: bfloat16 [2, 4096, 1024], P(None, ('tensor', 'dp')), may hold values from -0.125 to 0.125
- norm_gain: bfloat16 [2, 2, 1024], P(None, None, 'dp'), may hold values from 0.5 to 1.5
- norm_bias: bfloat16 [2, 2, 1024], P(None, None, 'dp'), may hold values from -2 to 2
- out_grad: float32 [4096, 1024], P('dp'), may hold values from -6 to 6
Outputs:
- hidden_out: float32 [4096, 1024], P('dp')
- in_grad: float32 [4096, 1024], P('dp')
- attend_wgrad: float32 [2, 1024, 3, 1024], P(None, 'dp', None, 'tensor')
- attend_bgrad: float32 [2, 2, 1024], P(None, None, ('tensor', 'dp'))
- output_wgrad: float32 [2, 1024, 1024], P(None, ('tensor', 'dp'))
- branch_bgrad: float32 [2, 2, 1024], P(None, None, 'dp')
- expand_wgrad: float32 [2, 1024, 4096], P(None, 'dp', 'tensor')
- expand_bgrad: float32 [2, 4096], P(None, ('tensor', 'dp'))
- reduce_wgrad: float32 [2, 4096, 1024], P(None, ('tensor', 'dp'))
- gain_grad: float32 [2, 2, 1024], P(None, None, 'dp')
- offset_grad: float32 [2, 2, 1024], P(None, None, 'dp')
The draws below stay inside these ranges and needn't reach their ends.
Inputs may be any that keep to these rules, and one draw needn't show every extreme that they name: doc_ids never falls from one token to the next; each of the 8 documents holds 1 to 1024 consecutive tokens, and some document exactly 1024.
All inputs are finite; a program needn't handle non-finite values.
Results may differ from the reference program's by a relative error of at most 0.025.
Values may be sent and summed in bfloat16 or wider, within the bound.
A program may use at most 192 MiB of HBM per device.

```python
import math
import jax
import jax.numpy as jnp
import numpy as np
from jax import lax

D = 1024
HEADS = 16
HEAD_DIM = 64
FF = 4096
CTX = 1024
LAYERS = 2
TOK_DEV = 512
TOKENS = 4096
BACK = 2
DOCS = 8
N_TENSOR = 4


def steps_of(own_key, dims, split, smallest, top_value):
    factor_of, own = 1.0, jax.random.fold_in(own_key, 6)
    for dim, blocks in split:
        heights = jnp.exp(jax.random.uniform(jax.random.fold_in(own, dim), (blocks,), jnp.float32, smallest / len(split), top_value / len(split)))
        factor_of = factor_of * jnp.repeat(heights, dims[dim] // blocks).reshape([-1 if axis == dim else 1 for axis in range(len(dims))])
    return factor_of


def split_up(number_of, total, most, slope):
    weights = [(1 << 20) // math.isqrt(standing ** slope) + 1 for standing in range(2, number_of + 1)]
    surplus, counts = total - most - (number_of - 1), [1] * (number_of - 1)
    while surplus > 0:
        candidates = [i for i in range(number_of - 1) if counts[i] < most]
        pool, left = sum([weights[i] for i in candidates]), surplus
        for i in candidates:
            extra = min(most - counts[i], max(1, left * weights[i] // pool), surplus)
            counts[i] = counts[i] + extra
            surplus = surplus - extra
    return np.array([most] + counts)


def uneven_parts(rng, number_of, total, bound, slope):
    if number_of == 2:
        one = jax.random.randint(rng, (), max(1, total - bound), min(bound, total - 1) + 1)
        return jnp.stack([one, total - one])
    lengths = jnp.asarray(split_up(number_of, total, bound, slope), jnp.int32)
    twos = (number_of - 1) // 2
    giver, sink = lengths[1:1 + 2 * twos:2], lengths[2:2 + 2 * twos:2]
    room = jnp.minimum(giver - 1, bound - sink)
    moved = jax.random.randint(jax.random.fold_in(rng, 1), (twos,), 0, 1 << 20) % (room + 1)
    lengths = lengths.at[1:1 + 2 * twos:2].set(giver - moved).at[2:2 + 2 * twos:2].set(sink + moved)
    return lengths[jax.random.permutation(jax.random.fold_in(rng, 2), number_of)]


def gaussian(own_key, dims, deviation, limit, cuts=(), kind=jnp.bfloat16):
    entries = deviation * jax.random.normal(own_key, dims, jnp.float32)
    if cuts:
        entries = entries * steps_of(own_key, dims, cuts, -0.22, 0.18)
    return jnp.clip(entries, -limit, limit).astype(kind)


def setup_inputs(seed: int = 0) -> dict:
    seeds = jax.random.split(jax.random.key(seed), 13)
    hidden_in = gaussian(seeds[0], (TOKENS, D), 1.0, 6.0, ((0, 8),), jnp.float32)
    doc_ids = jnp.searchsorted(jnp.cumsum(uneven_parts(seeds[1], DOCS, TOKENS, CTX, 1)), jnp.arange(TOKENS), side="right").astype(jnp.int32)
    attend_weight = gaussian(seeds[2], (LAYERS, D, 3, D), D ** -0.5, 0.1875, ((1, 8), (3, 4)))
    attend_bias = gaussian(seeds[3], (LAYERS, 2, D), 0.5, 3.0, ((2, 32),))
    output_weight = gaussian(seeds[4], (LAYERS, D, D), (D // 16) ** -0.5, 0.75, ((1, 32),))
    branch_bias = gaussian(seeds[5], (LAYERS, 2, D), 0.5, 3.0, ((2, 8),))
    expand_weight = gaussian(seeds[6], (LAYERS, D, FF), D ** -0.5, 0.1875, ((1, 8), (2, 4)))
    expand_bias = gaussian(seeds[7], (LAYERS, FF), 0.5, 3.0, ((1, 32),))
    reduce_weight = gaussian(seeds[8], (LAYERS, FF, D), (FF // 2) ** -0.5, 0.125, ((1, 32),))
    norm_gain = jnp.clip(1.0 + 0.1 * jax.random.normal(seeds[9], (LAYERS, 2, D), jnp.float32), 0.5, 1.5).astype(jnp.bfloat16)
    norm_bias = gaussian(seeds[10], (LAYERS, 2, D), 0.3, 2.0, ((2, 8),))
    out_grad = gaussian(seeds[11], (TOKENS, D), 1.0, 6.0, ((0, 8),), jnp.float32)
    return dict(hidden_in=hidden_in, doc_ids=doc_ids, attend_weight=attend_weight, attend_bias=attend_bias, output_weight=output_weight, branch_bias=branch_bias, expand_weight=expand_weight, expand_bias=expand_bias, reduce_weight=reduce_weight, norm_gain=norm_gain, norm_bias=norm_bias, out_grad=out_grad)


def contract(pattern, left_side, right_side):
    return jnp.einsum(pattern, left_side.astype(jnp.float32), right_side.astype(jnp.float32), precision=lax.Precision.HIGHEST)

def layer_norm(values, gain_row, offset_row):
    center = values - lax.optimization_barrier(jnp.mean(values, axis=-1, keepdims=True))
    spread = lax.optimization_barrier(jnp.mean(center * center, axis=-1, keepdims=True))
    return center * lax.rsqrt(spread + 1e-05) * gain_row + offset_row

def gelu_tanh(values):
    return 0.5 * values * (1.0 + jnp.tanh(0.7978845608028654 * (values + 0.044715 * values * values * values)))

def attend_forward(queries, key_block, value_block, allowed):
    factor = 1.0 / math.sqrt(queries.shape[-1])
    scores = contract('qhe,khe->hqk', queries, key_block) * factor
    unnormed = jnp.where(allowed[None], jnp.exp(scores), 0.0)
    totals = lax.optimization_barrier(jnp.sum(unnormed, axis=-1))
    probabilities = (unnormed / totals[..., None]).astype(jnp.bfloat16)
    context = contract('hqk,khe->qhe', probabilities, value_block)
    return (context.astype(jnp.bfloat16), jnp.log(totals))

def attend_backward(queries, key_block, value_block, log_totals, out_cot, allowed):
    factor = 1.0 / math.sqrt(queries.shape[-1])
    scores = contract('qhe,khe->hqk', queries, key_block) * factor
    probabilities = jnp.where(allowed[None], jnp.exp(scores - log_totals[..., None]), 0.0)
    rounded = probabilities.astype(jnp.bfloat16)
    value_cot = contract('hqk,qhe->khe', rounded, out_cot)
    prob_cot = contract('qhe,khe->hqk', out_cot, value_block)
    row_inner = lax.optimization_barrier(jnp.sum(probabilities * prob_cot, axis=-1, keepdims=True))
    score_cot = (probabilities * (prob_cot - row_inner) * factor).astype(jnp.bfloat16)
    query_cot = contract('hqk,khe->qhe', score_cot, key_block)
    key_cot = contract('hqk,qhe->khe', score_cot, queries)
    return (query_cot, key_cot, value_cot)

def group_total(partials):
    rounded = lax.optimization_barrier(partials.astype(jnp.bfloat16))
    return lax.optimization_barrier(jnp.sum(rounded.astype(jnp.float32), axis=0))

def reference(hidden_in, doc_ids, attend_weight, attend_bias, output_weight, branch_bias, expand_weight, expand_bias, reduce_weight, norm_gain, norm_bias, out_grad):
    groups = N_TENSOR
    reach_back = BACK
    block_rows = TOK_DEV
    count_blocks = TOKENS // TOK_DEV
    window_rows = (reach_back + 1) * block_rows
    head_count = HEADS
    doc_marks = doc_ids.astype(jnp.int32) + 1
    padded_marks = jnp.concatenate([jnp.zeros((reach_back * block_rows,), jnp.int32), doc_marks])
    row_ids = jnp.arange(block_rows, dtype=jnp.int32)[:, None]
    col_ids = jnp.arange(window_rows, dtype=jnp.int32)[None, :]
    causal = col_ids - reach_back * block_rows <= row_ids
    block_ids = jnp.arange(count_blocks, dtype=jnp.int32)

    def mask_of(block_index):
        own_marks = lax.dynamic_slice_in_dim(doc_marks, (block_index * block_rows).astype(jnp.int32), block_rows)
        window_marks = lax.dynamic_slice_in_dim(padded_marks, (block_index * block_rows).astype(jnp.int32), window_rows)
        return (window_marks[None, :] == own_marks[:, None]) & causal

    def pad_rows(values):
        return jnp.concatenate([jnp.zeros((reach_back * block_rows,) + values.shape[1:], values.dtype), values])

    def slice_rows(values, block_index, length):
        return lax.dynamic_slice_in_dim(values, (block_index * block_rows).astype(jnp.int32), length)
    kept_states = []
    current = hidden_in
    for layer_index in range(LAYERS):
        gain_pair = norm_gain[layer_index].astype(jnp.float32)
        offset_pair = norm_bias[layer_index].astype(jnp.float32)
        normed_one = layer_norm(current, gain_pair[0], offset_pair[0]).astype(jnp.bfloat16)
        projected = jnp.dot(normed_one, attend_weight[layer_index].reshape(D, 3 * D), preferred_element_type=jnp.float32).reshape(TOKENS, 3, D)
        bias_pair = attend_bias[layer_index].astype(jnp.float32)
        queries = (projected[:, 0] + bias_pair[0]).astype(jnp.bfloat16).reshape(TOKENS, head_count, HEAD_DIM)
        key_all = projected[:, 1].astype(jnp.bfloat16).reshape(TOKENS, head_count, HEAD_DIM)
        value_all = (projected[:, 2] + bias_pair[1]).astype(jnp.bfloat16).reshape(TOKENS, head_count, HEAD_DIM)
        key_pad = pad_rows(key_all)
        value_pad = pad_rows(value_all)

        def one_block(block_index):
            return attend_forward(slice_rows(queries, block_index, block_rows), slice_rows(key_pad, block_index, window_rows), slice_rows(value_pad, block_index, window_rows), mask_of(block_index))
        context, log_totals = lax.map(one_block, block_ids)
        flat_context = context.reshape(TOKENS, D)
        attended = group_total(contract('tgk,gkn->gtn', flat_context.reshape(TOKENS, groups, D // groups), output_weight[layer_index].reshape(groups, D // groups, D)))
        branch_pair = branch_bias[layer_index].astype(jnp.float32)
        middle = current + (attended + branch_pair[0])
        normed_two = layer_norm(middle, gain_pair[1], offset_pair[1]).astype(jnp.bfloat16)
        pre_act = jnp.dot(normed_two, expand_weight[layer_index], preferred_element_type=jnp.float32) + expand_bias[layer_index].astype(jnp.float32)
        activated = gelu_tanh(pre_act).astype(jnp.bfloat16)
        reduced = group_total(contract('tgk,gkn->gtn', activated.reshape(TOKENS, groups, FF // groups), reduce_weight[layer_index].reshape(groups, FF // groups, D)))
        output = middle + (reduced + branch_pair[1])
        kept_states.append((current, normed_one, queries, key_pad, value_pad, flat_context, log_totals, middle, normed_two, pre_act, activated))
        current = output
    hidden_out = current
    grad_now = out_grad
    layer_grads = [None] * LAYERS
    for layer_index in reversed(range(LAYERS)):
        hidden, normed_one, queries, key_pad, value_pad, flat_context, log_totals, middle, normed_two, pre_act, activated = kept_states[layer_index]
        gain_pair = norm_gain[layer_index].astype(jnp.float32)
        offset_pair = norm_bias[layer_index].astype(jnp.float32)
        bias_two = lax.optimization_barrier(jnp.sum(grad_now, axis=0))
        grad_rounded = grad_now.astype(jnp.bfloat16)
        reduce_grad = jnp.dot(activated.T, grad_rounded, preferred_element_type=jnp.float32)
        act_cot = jnp.dot(grad_rounded, reduce_weight[layer_index].T, preferred_element_type=jnp.float32)
        unused, gelu_pull = jax.vjp(gelu_tanh, pre_act)
        pre_cot = gelu_pull(act_cot)[0]
        expand_bias_grad = lax.optimization_barrier(jnp.sum(pre_cot, axis=0))
        pre_rounded = pre_cot.astype(jnp.bfloat16)
        expand_grad = jnp.dot(normed_two.T, pre_rounded, preferred_element_type=jnp.float32)
        normed_cot = group_total(contract('tgk,dgk->gtd', pre_rounded.reshape(TOKENS, groups, FF // groups), expand_weight[layer_index].reshape(D, groups, FF // groups)))
        unused, norm_pull = jax.vjp(layer_norm, middle, gain_pair[1], offset_pair[1])
        mid_part, gain_two, offset_two = norm_pull(normed_cot)
        mid_cot = grad_now + mid_part
        bias_one = lax.optimization_barrier(jnp.sum(mid_cot, axis=0))
        mid_rounded = mid_cot.astype(jnp.bfloat16)
        output_grad = jnp.dot(flat_context.T, mid_rounded, preferred_element_type=jnp.float32)
        context_cot = jnp.dot(mid_rounded, output_weight[layer_index].T, preferred_element_type=jnp.float32).astype(jnp.bfloat16).reshape(TOKENS, head_count, HEAD_DIM)

        def one_back(block_index):
            return attend_backward(slice_rows(queries, block_index, block_rows), slice_rows(key_pad, block_index, window_rows), slice_rows(value_pad, block_index, window_rows), lax.dynamic_index_in_dim(log_totals, block_index, 0, keepdims=False), slice_rows(context_cot, block_index, block_rows), mask_of(block_index))
        query_cot, key_cot, value_cot = lax.map(one_back, block_ids)
        query_cot = query_cot.reshape(TOKENS, head_count, HEAD_DIM)
        key_cot = key_cot.reshape(count_blocks, reach_back + 1, block_rows, head_count, HEAD_DIM)
        value_cot = value_cot.reshape(count_blocks, reach_back + 1, block_rows, head_count, HEAD_DIM)
        key_acc = jnp.zeros((count_blocks + reach_back, block_rows, head_count, HEAD_DIM), jnp.float32)
        value_acc = jnp.zeros((count_blocks + reach_back, block_rows, head_count, HEAD_DIM), jnp.float32)
        for hop_index in range(reach_back + 1):
            key_acc = key_acc.at[hop_index:hop_index + count_blocks].add(key_cot[:, hop_index])
            value_acc = value_acc.at[hop_index:hop_index + count_blocks].add(value_cot[:, hop_index])
        key_total = key_acc[reach_back:].reshape(TOKENS, D)
        value_total = value_acc[reach_back:].reshape(TOKENS, D)
        proj_cot = jnp.stack([query_cot.reshape(TOKENS, D), key_total, value_total], axis=1)
        attend_bias_grad = jnp.stack([lax.optimization_barrier(jnp.sum(proj_cot[:, 0], axis=0)), lax.optimization_barrier(jnp.sum(proj_cot[:, 2], axis=0))])
        proj_rounded = proj_cot.astype(jnp.bfloat16)
        attend_grad = jnp.dot(normed_one.T, proj_rounded.reshape(TOKENS, 3 * D), preferred_element_type=jnp.float32).reshape(D, 3, D)
        normed_cot_one = group_total(contract('tcgk,dcgk->gtd', proj_rounded.reshape(TOKENS, 3, groups, D // groups), attend_weight[layer_index].reshape(D, 3, groups, D // groups)))
        unused, first_pull = jax.vjp(layer_norm, hidden, gain_pair[0], offset_pair[0])
        hid_part, gain_one, offset_one = first_pull(normed_cot_one)
        grad_now = mid_cot + hid_part
        layer_grads[layer_index] = (attend_grad, attend_bias_grad, output_grad, jnp.stack([bias_one, bias_two]), expand_grad, expand_bias_grad, reduce_grad, jnp.stack([gain_one, gain_two]), jnp.stack([offset_one, offset_two]))
    stacked = [jnp.stack([entry[member] for entry in layer_grads]) for member in range(9)]
    return (hidden_out, grad_now, stacked[0], stacked[1], stacked[2], stacked[3], stacked[4], stacked[5], stacked[6], stacked[7], stacked[8])
```

```python
import functools
import math

import jax
import jax.numpy as jnp
from jax import lax
from jax.experimental import pallas as pl
from jax.experimental.pallas import tpu as pltpu
from jax.sharding import PartitionSpec as P

HEAD_DIM = 64
CTX = 1024
LANES = 128
ROW_TILE = 256


def passed_along(block, axis, distance):
    devices = range(lax.axis_size(axis))
    route = [(i - distance, i) for i in devices if i - distance in devices]
    return lax.ppermute(block, axis, route)


def contract(pattern, left_side, right_side):
    return jnp.einsum(pattern, left_side, right_side, preferred_element_type=jnp.float32)


def layer_norm(values, gain_row, offset_row):
    center = values - jnp.mean(values, axis=-1, keepdims=True)
    spread = jnp.mean(center * center, axis=-1, keepdims=True)
    return center * lax.rsqrt(spread + 1e-05) * gain_row + offset_row


def gelu_tanh(values):
    return (
        0.5
        * values
        * (1.0 + jnp.tanh(0.7978845608028654 * (values + 0.044715 * values * values * values)))
    )


def dot_rows(left_side, right_side):
    return lax.dot_general(
        left_side, right_side, (((1,), (1,)), ((), ())), preferred_element_type=jnp.float32
    )


def dot_tokens(left_side, right_side):
    return lax.dot_general(
        left_side, right_side, (((0,), (0,)), ((), ())), preferred_element_type=jnp.float32
    )


def row_tiles(rows, window_rows):
    tile = min(ROW_TILE, rows)
    back = window_rows - rows
    for start in range(0, rows, tile):
        low = max(0, (back + start - CTX + 1) // LANES * LANES)
        yield start, tile, low, back + start + tile


def tile_mask(own_ref, window_ref, start, tile, low, high, back):
    own = own_ref[start : start + tile, :]
    window = window_ref[:, low:high]
    row = lax.broadcasted_iota(jnp.int32, (tile, high - low), 0) + (start + back)
    col = lax.broadcasted_iota(jnp.int32, (tile, high - low), 1) + low
    return (window == own) & (col <= row)


def head_parts(width):
    group = min(LANES, width)
    for base in range(0, width, group):
        for inner in range(0, group, HEAD_DIM):
            yield base, group, inner


def pick(block, inner):
    lane = lax.broadcasted_iota(jnp.int32, block.shape, 1)
    return jnp.where((lane >= inner) & (lane < inner + HEAD_DIM), block, jnp.zeros_like(block))


def forward_kernel(q_ref, kv_ref, own_ref, window_ref, o_ref, lse_ref):
    rows, width = q_ref.shape
    window_rows = kv_ref.shape[0]
    back = window_rows - rows
    factor = 1.0 / math.sqrt(HEAD_DIM)
    for start, tile, low, high in row_tiles(rows, window_rows):
        allowed = tile_mask(own_ref, window_ref, start, tile, low, high, back)
        held = None
        logs = []
        for base, group, inner in head_parts(width):
            queries = pick(q_ref[start : start + tile, base : base + group], inner)
            keys = kv_ref[low:high, base : base + group]
            values = kv_ref[low:high, width + base : width + base + group]
            unnormed = jnp.where(allowed, jnp.exp(dot_rows(queries, keys) * factor), 0.0)
            totals = jnp.sum(unnormed, axis=-1, keepdims=True)
            probabilities = (unnormed * (1.0 / totals)).astype(jnp.bfloat16)
            context = pick(
                jnp.dot(probabilities, values, preferred_element_type=jnp.float32), inner
            )
            held = context if inner == 0 else held + context
            logs.append(jnp.log(totals))
            if inner + HEAD_DIM == group:
                o_ref[start : start + tile, base : base + group] = held.astype(jnp.bfloat16)
        for index, entry in enumerate(logs):
            lse_ref[start : start + tile, index : index + 1] = entry


def backward_kernel(
    q_ref, kv_ref, lse_ref, cot_ref, own_ref, window_ref, dq_ref, own_out, back_out, acc
):
    rows, width = q_ref.shape
    window_rows = kv_ref.shape[0]
    back = window_rows - rows
    factor = 1.0 / math.sqrt(HEAD_DIM)
    acc[...] = jnp.zeros_like(acc)
    for start, tile, low, high in row_tiles(rows, window_rows):
        allowed = tile_mask(own_ref, window_ref, start, tile, low, high, back)
        held = None
        for index, (base, group, inner) in enumerate(head_parts(width)):
            queries = pick(q_ref[start : start + tile, base : base + group], inner)
            cots = pick(cot_ref[start : start + tile, base : base + group], inner)
            keys = kv_ref[low:high, base : base + group]
            values = kv_ref[low:high, width + base : width + base + group]
            logs = lse_ref[start : start + tile, index : index + 1]
            scores = dot_rows(queries, keys) * factor
            probabilities = jnp.where(allowed, jnp.exp(scores - logs), 0.0)
            rounded = probabilities.astype(jnp.bfloat16)
            acc[low:high, width + base : width + base + group] += dot_tokens(rounded, cots)
            prob_cot = dot_rows(cots, values)
            inner_sum = jnp.sum(probabilities * prob_cot, axis=-1, keepdims=True)
            score_cot = (probabilities * (prob_cot - inner_sum) * factor).astype(jnp.bfloat16)
            acc[low:high, base : base + group] += dot_tokens(score_cot, queries)
            part = pick(jnp.dot(score_cot, keys, preferred_element_type=jnp.float32), inner)
            held = part if inner == 0 else held + part
            if inner + HEAD_DIM == group:
                dq_ref[start : start + tile, base : base + group] = held
    own_out[...] = acc[back:, :]
    back_out[...] = acc[:back, :].astype(jnp.bfloat16)


def in_vmem(count):
    return [pl.BlockSpec(memory_space=pltpu.VMEM)] * count


def attend_forward(queries, window_kv, own_marks, window_marks):
    rows, width = queries.shape
    return pl.pallas_call(
        forward_kernel,
        out_shape=(
            jax.ShapeDtypeStruct((rows, width), jnp.bfloat16),
            jax.ShapeDtypeStruct((rows, width // HEAD_DIM), jnp.float32),
        ),
        in_specs=in_vmem(4),
        out_specs=tuple(in_vmem(2)),
        compiler_params=pltpu.CompilerParams(vmem_limit_bytes=40 * 1024 * 1024),
        name="attend_forward",
    )(queries, window_kv, own_marks, window_marks)


def attend_backward(queries, window_kv, log_totals, out_cot, own_marks, window_marks):
    rows, width = queries.shape
    window_rows = window_kv.shape[0]
    return pl.pallas_call(
        backward_kernel,
        out_shape=(
            jax.ShapeDtypeStruct((rows, width), jnp.float32),
            jax.ShapeDtypeStruct((rows, 2 * width), jnp.float32),
            jax.ShapeDtypeStruct((window_rows - rows, 2 * width), jnp.bfloat16),
        ),
        in_specs=in_vmem(6),
        out_specs=tuple(in_vmem(3)),
        scratch_shapes=[pltpu.VMEM((window_rows, 2 * width), jnp.float32)],
        compiler_params=pltpu.CompilerParams(vmem_limit_bytes=48 * 1024 * 1024),
        name="attend_backward",
    )(queries, window_kv, log_totals, out_cot, own_marks, window_marks)


def line_kernel(chunks, x_ref, o_ref, from_near, from_mid, pair, total, near_send, mid_send, near_recv, mid_recv):
    place = lax.axis_index("tensor")
    near = place + 1 - 2 * lax.rem(place, 2)
    across = 3 - place
    is_end = (place == 0) | (place == 3)
    is_mid = (place == 1) | (place == 2)
    step = x_ref.shape[0] // chunks
    barrier = pltpu.get_barrier_semaphore()

    def part(ref, c):
        return ref.at[pl.ds(c * step, step)]

    def to_near(src, c):
        return pltpu.make_async_remote_copy(
            src_ref=part(src, c),
            dst_ref=part(from_near, c),
            send_sem=near_send.at[c],
            recv_sem=near_recv.at[c],
            device_id={"tensor": near},
            device_id_type=pl.DeviceIdType.MESH,
        )

    def to_mid(c):
        return pltpu.make_async_remote_copy(
            src_ref=part(pair, c),
            dst_ref=part(from_mid, c),
            send_sem=mid_send.at[c],
            recv_sem=mid_recv.at[c],
            device_id={"tensor": across},
            device_id_type=pl.DeviceIdType.MESH,
        )

    def added(left, right, c):
        rows = pl.ds(c * step, step)
        both = left[rows, :].astype(jnp.float32) + right[rows, :].astype(jnp.float32)
        return both.astype(jnp.bfloat16)

    pl.semaphore_signal(
        barrier, inc=1, device_id={"tensor": near}, device_id_type=pl.DeviceIdType.MESH
    )

    @pl.when(is_end)
    def _():
        pl.semaphore_wait(barrier, 1)
        for c in range(chunks):
            to_near(x_ref, c).start()
        for c in range(chunks):
            to_near(x_ref, c).wait_recv()
            rows = pl.ds(c * step, step)
            o_ref[rows, :] = from_near[rows, :]
        for c in range(chunks):
            to_near(x_ref, c).wait_send()

    @pl.when(is_mid)
    def _():
        pl.semaphore_signal(
            barrier, inc=1, device_id={"tensor": across}, device_id_type=pl.DeviceIdType.MESH
        )
        pl.semaphore_wait(barrier, 2)
        lag = 2
        for c in range(chunks + lag):
            if c < chunks:
                to_near(total, c).wait_recv()
                pair[pl.ds(c * step, step), :] = added(x_ref, from_near, c)
                to_mid(c).start()
            done = c - lag
            if done >= 0:
                to_mid(done).wait_recv()
                result = added(pair, from_mid, done)
                total[pl.ds(done * step, step), :] = result
                to_near(total, done).start()
                o_ref[pl.ds(done * step, step), :] = result
        for c in range(chunks):
            to_mid(c).wait_send()
            to_near(total, c).wait_send()


def tensor_total(partial_value):
    rounded = partial_value.astype(jnp.bfloat16)
    rows = rounded.shape[0]
    if lax.axis_size("tensor") != 4 or rows % 128:
        return lax.psum(rounded, "tensor").astype(jnp.float32)
    chunks = 8
    block = pltpu.VMEM(rounded.shape, jnp.bfloat16)
    summed = pl.pallas_call(
        functools.partial(line_kernel, chunks),
        out_shape=jax.ShapeDtypeStruct(rounded.shape, jnp.bfloat16),
        in_specs=in_vmem(1),
        out_specs=in_vmem(1)[0],
        scratch_shapes=[block] * 4 + [pltpu.SemaphoreType.DMA((chunks,))] * 4,
        compiler_params=pltpu.CompilerParams(
            collective_id=0, has_side_effects=True, vmem_limit_bytes=24 * 1024 * 1024
        ),
        name="line_total",
    )(rounded)
    return summed.astype(jnp.float32)


def forward_layer(hidden, params, marks, reach_back):
    attend_w, attend_b, output_w, branches, expand_w, expand_b, reduce_w, gains, offsets = params
    width = output_w.shape[0]
    own_marks, window_marks = marks
    normed_one = layer_norm(hidden, gains[0], offsets[0]).astype(jnp.bfloat16)
    projected = jnp.dot(normed_one, attend_w, preferred_element_type=jnp.float32)
    queries = (projected[:, :width] + attend_b[0]).astype(jnp.bfloat16)
    kv_bias = jnp.concatenate([jnp.zeros_like(attend_b[1]), attend_b[1]])
    kv_now = (projected[:, width:] + kv_bias).astype(jnp.bfloat16)
    kv_list = [passed_along(kv_now, "dp", hop) for hop in range(reach_back, 0, -1)]
    window_kv = jnp.concatenate(kv_list + [kv_now], axis=0)
    context, log_totals = attend_forward(queries, window_kv, own_marks, window_marks)
    attended = tensor_total(jnp.dot(context, output_w, preferred_element_type=jnp.float32))
    middle = hidden + (attended + branches[0])
    normed_two = layer_norm(middle, gains[1], offsets[1]).astype(jnp.bfloat16)
    pre_act = jnp.dot(normed_two, expand_w, preferred_element_type=jnp.float32) + expand_b
    activated = gelu_tanh(pre_act).astype(jnp.bfloat16)
    reduced = tensor_total(jnp.dot(activated, reduce_w, preferred_element_type=jnp.float32))
    output = middle + (reduced + branches[1])
    kept_state = (
        hidden,
        normed_one,
        queries,
        window_kv,
        context,
        log_totals,
        middle,
        normed_two,
        pre_act,
        activated,
    )
    return (output, kept_state)


def backward_layer(grad_out, params, kept_state, marks, reach_back):
    attend_w, attend_b, output_w, branches, expand_w, expand_b, reduce_w, gains, offsets = params
    (
        hidden,
        normed_one,
        queries,
        window_kv,
        context,
        log_totals,
        middle,
        normed_two,
        pre_act,
        activated,
    ) = kept_state
    own_marks, window_marks = marks
    rows = hidden.shape[0]
    width = output_w.shape[0]
    bias_two = jnp.sum(grad_out, axis=0)
    grad_rounded = grad_out.astype(jnp.bfloat16)
    act_cot = contract("td,fd->tf", grad_rounded, reduce_w)
    unused, gelu_pull = jax.vjp(gelu_tanh, pre_act)
    pre_cot = gelu_pull(act_cot)[0]
    expand_bias_grad = jnp.sum(pre_cot, axis=0)
    pre_rounded = pre_cot.astype(jnp.bfloat16)
    normed_cot = tensor_total(contract("tf,df->td", pre_rounded, expand_w))
    reduce_grad = contract("tf,td->fd", activated, grad_rounded).astype(jnp.bfloat16)
    expand_grad = contract("td,tf->df", normed_two, pre_rounded).astype(jnp.bfloat16)
    unused, norm_pull = jax.vjp(layer_norm, middle, gains[1], offsets[1])
    mid_part, gain_two, offset_two = norm_pull(normed_cot)
    mid_cot = grad_out + mid_part
    bias_one = jnp.sum(mid_cot, axis=0)
    mid_rounded = mid_cot.astype(jnp.bfloat16)
    output_grad = contract("tk,td->kd", context, mid_rounded).astype(jnp.bfloat16)
    context_cot = contract("td,kd->tk", mid_rounded, output_w).astype(jnp.bfloat16)
    context_cot, expand_grad, reduce_grad = lax.optimization_barrier(
        (context_cot, expand_grad, reduce_grad)
    )
    query_cot, kv_own, kv_back = attend_backward(
        queries, window_kv, log_totals, context_cot, own_marks, window_marks
    )
    for hop in range(1, reach_back + 1):
        begin = (reach_back - hop) * rows
        kv_own = kv_own + passed_along(kv_back[begin : begin + rows], "dp", -hop).astype(
            jnp.float32
        )
    attend_bias_grad = jnp.stack([jnp.sum(query_cot, axis=0), jnp.sum(kv_own[:, width:], axis=0)])
    proj_rounded = jnp.concatenate(
        [query_cot.astype(jnp.bfloat16), kv_own.astype(jnp.bfloat16)], axis=1
    )
    normed_cot_one = tensor_total(contract("tc,dc->td", proj_rounded, attend_w))
    attend_grad = contract("td,tc->dc", normed_one, proj_rounded).astype(jnp.bfloat16)
    unused, first_pull = jax.vjp(layer_norm, hidden, gains[0], offsets[0])
    hid_part, gain_one, offset_one = first_pull(normed_cot_one)
    in_cot = mid_cot + hid_part
    small = (
        attend_bias_grad,
        jnp.stack([bias_one, bias_two]),
        expand_bias_grad,
        jnp.stack([gain_one, gain_two]),
        jnp.stack([offset_one, offset_two]),
    )
    return (in_cot, expand_grad, reduce_grad, attend_grad, output_grad, small)


def scattered(block):
    return lax.psum_scatter(block, "dp", scatter_dimension=0, tiled=True)


def pack_output(block, model, share):
    part = model // lax.axis_size("dp")
    slabs = part // share
    owners = block.shape[0] // share
    return (
        block.reshape(owners, share, slabs, model // slabs)
        .transpose(0, 2, 1, 3)
        .reshape(owners * part, model // slabs)
    )


def unpack_output(block, model, share):
    part = model // lax.axis_size("dp")
    slabs = part // share
    owners = block.shape[0] // part
    return (
        block.reshape(owners, slabs, share, model // slabs)
        .transpose(0, 2, 1, 3)
        .reshape(owners * share, model)
    )


def split_owned(pieces, sizes, size):
    rows = [
        jnp.moveaxis(p.reshape(p.shape[:-1] + (size, p.shape[-1] // size)), -2, 0).reshape(size, -1)
        for p in pieces
    ]
    return jnp.concatenate(rows, axis=1)


GELU_SCALE = 0.7978845608028654
GELU_CUBIC = 0.044715
COLUMNS = 256


def column_blocks(width):
    size = min(COLUMNS, width)
    return [slice(start, start + size) for start in range(0, width, size)]


def norm_parts(values):
    center = values - jnp.mean(values, axis=-1, keepdims=True)
    inverse = lax.rsqrt(jnp.mean(center * center, axis=-1, keepdims=True) + 1e-05)
    return center * inverse, inverse


def norm_rows(values, gain_row, offset_row):
    return norm_parts(values)[0] * gain_row + offset_row


def norm_back(values, gain_row, cot):
    normal, inverse = norm_parts(values)
    scaled = cot * gain_row
    mean_one = jnp.mean(scaled, axis=-1, keepdims=True)
    mean_two = jnp.mean(scaled * normal, axis=-1, keepdims=True)
    return inverse * (scaled - mean_one - normal * mean_two), cot * normal


def gelu_value(values):
    bent = jnp.tanh(GELU_SCALE * (values + GELU_CUBIC * values * values * values))
    return 0.5 * values * (1.0 + bent), bent


def gelu_slope(values, bent):
    inner = GELU_SCALE * (1.0 + 3.0 * GELU_CUBIC * values * values)
    return 0.5 * (1.0 + bent) + 0.5 * values * (1.0 - bent * bent) * inner


class LineTotal:
    scratch_count = 7

    @staticmethod
    def scratch(rows, model, chunks):
        block = pltpu.VMEM((rows, model), jnp.bfloat16)
        return [block] * 3 + [pltpu.SemaphoreType.DMA((chunks,))] * 4

    def __init__(self, refs, chunks):
        self.own, self.near_buf, self.mid_buf = refs[:3]
        self.near_send, self.near_recv, self.mid_send, self.mid_recv = refs[3:]
        self.chunks = chunks
        self.step = self.own.shape[0] // chunks
        place = lax.axis_index("tensor")
        self.near = place + 1 - 2 * lax.rem(place, 2)
        self.across = 3 - place
        self.is_end = (place == 0) | (place == 3)
        self.is_mid = (place == 1) | (place == 2)

    def rows(self, c):
        return pl.ds(pl.multiple_of(c * self.step, self.step), self.step)

    def to_near(self, src, c):
        return pltpu.make_async_remote_copy(
            src_ref=src.at[self.rows(c)],
            dst_ref=self.near_buf.at[self.rows(c)],
            send_sem=self.near_send.at[c],
            recv_sem=self.near_recv.at[c],
            device_id={"tensor": self.near},
            device_id_type=pl.DeviceIdType.MESH,
        )

    def to_across(self, c):
        return pltpu.make_async_remote_copy(
            src_ref=self.own.at[self.rows(c)],
            dst_ref=self.mid_buf.at[self.rows(c)],
            send_sem=self.mid_send.at[c],
            recv_sem=self.mid_recv.at[c],
            device_id={"tensor": self.across},
            device_id_type=pl.DeviceIdType.MESH,
        )

    def greet(self):
        barrier = pltpu.get_barrier_semaphore()
        pl.semaphore_signal(
            barrier, inc=1, device_id={"tensor": self.near}, device_id_type=pl.DeviceIdType.MESH
        )

        @pl.when(self.is_end)
        def _():
            pl.semaphore_wait(barrier, 1)

        @pl.when(self.is_mid)
        def _():
            pl.semaphore_signal(
                barrier,
                inc=1,
                device_id={"tensor": self.across},
                device_id_type=pl.DeviceIdType.MESH,
            )
            pl.semaphore_wait(barrier, 2)

    def send(self, c):
        @pl.when(self.is_end)
        def _():
            self.to_near(self.own, c).start()

    def summed(self, left, right, c):
        rows = self.rows(c)
        both = left[rows, :].astype(jnp.float32) + right[rows, :].astype(jnp.float32)
        return both.astype(jnp.bfloat16)

    def join(self, c):
        @pl.when(self.is_mid)
        def _():
            self.to_near(self.near_buf, c).wait_recv()
            self.own[self.rows(c), :] = self.summed(self.own, self.near_buf, c)
            self.to_across(c).start()

    def finish(self, c):
        @pl.when(self.is_mid)
        def _():
            self.to_across(c).wait_recv()
            self.near_buf[self.rows(c), :] = self.summed(self.own, self.mid_buf, c)
            self.to_near(self.near_buf, c).start()

    def take(self, c):
        @pl.when(self.is_end)
        def _():
            self.to_near(self.own, c).wait_recv()

        return self.near_buf[self.rows(c), :].astype(jnp.float32)

    def drain(self, c):
        @pl.when(self.is_end)
        def _():
            self.to_near(self.own, c).wait_send()

        @pl.when(self.is_mid)
        def _():
            self.to_across(c).wait_send()
            self.to_near(self.near_buf, c).wait_send()


def run_stages(chunks, stages):
    def body(t, carry):
        for lag, stage in stages:
            c = t - lag

            @pl.when((c >= 0) & (c < chunks))
            def _(stage=stage, c=c):
                stage(c)

        return carry

    lax.fori_loop(0, chunks + max(lag for lag, _ in stages), body, 0)


def drain_all(chunks, lines):
    def body(c, carry):
        for line in lines:
            line.drain(c)
        return carry

    lax.fori_loop(0, chunks, body, 0)


def add_sums(sums_ref, row, values):
    width = values.shape[1]
    sums_ref[row : row + 1, :width] += jnp.sum(values, axis=0, keepdims=True)


def project_into(line, c, left, weight_ref):
    rows = line.rows(c)
    for cols in column_blocks(weight_ref.shape[1]):
        part = jnp.dot(left, weight_ref[:, cols], preferred_element_type=jnp.float32)
        line.own[rows, cols] = part.astype(jnp.bfloat16)
    line.send(c)


def project_back_into(line, c, left, weight_ref):
    rows = line.rows(c)
    for cols in column_blocks(weight_ref.shape[0]):
        part = dot_rows(left, weight_ref[cols, :])
        line.own[rows, cols] = part.astype(jnp.bfloat16)
    line.send(c)


def first_kernel(chunks, *refs):
    ins, outs, scratch = refs[:7], refs[7:15], refs[15:]
    o_ref, wo_ref, h_ref, vec_ref, we_ref, wr_ref, wa_ref = ins
    mid_ref, a2_ref, f_ref, u_ref, next_ref, a1_ref, q_ref, kv_ref = outs
    one = LineTotal(scratch[:7], chunks)
    two = LineTotal(scratch[7:14], chunks)
    width = q_ref.shape[1]
    one.greet()

    def start(c):
        project_into(one, c, o_ref[one.rows(c), :], wo_ref)

    def feed(c):
        rows = one.rows(c)
        middle = h_ref[rows, :] + (one.take(c) + vec_ref[0:1, :])
        mid_ref[rows, :] = middle
        a2 = norm_rows(middle, vec_ref[1:2, :], vec_ref[2:3, :]).astype(jnp.bfloat16)
        a2_ref[rows, :] = a2
        for cols in column_blocks(we_ref.shape[1]):
            f = jnp.dot(a2, we_ref[:, cols], preferred_element_type=jnp.float32)
            f = f + vec_ref[3:4, cols]
            f_ref[rows, cols] = f
            u_ref[rows, cols] = gelu_value(f)[0].astype(jnp.bfloat16)
        project_into(two, c, u_ref[rows, :], wr_ref)

    def end(c):
        rows = two.rows(c)
        following = mid_ref[rows, :] + (two.take(c) + vec_ref[4:5, :])
        next_ref[rows, :] = following
        a1 = norm_rows(following, vec_ref[5:6, :], vec_ref[6:7, :]).astype(jnp.bfloat16)
        a1_ref[rows, :] = a1
        for part in range(3):
            cols = slice(part * width, (part + 1) * width)
            value = jnp.dot(a1, wa_ref[:, cols], preferred_element_type=jnp.float32)
            value = (value + vec_ref[7:8, cols]).astype(jnp.bfloat16)
            if part == 0:
                q_ref[rows, :] = value
            else:
                kv_ref[rows, (part - 1) * width : part * width] = value

    run_stages(
        chunks,
        [
            (0, start),
            (1, one.join),
            (2, one.finish),
            (3, feed),
            (4, two.join),
            (5, two.finish),
            (6, end),
        ],
    )
    drain_all(chunks, [one, two])


def turn_kernel(chunks, *refs):
    ins, outs, scratch = refs[:8], refs[8:17], refs[17:]
    o_ref, wo_ref, h_ref, vec_ref, we_ref, wr_ref, e_ref, mid_ref = ins[:7] + (scratch[0],)
    a2_ref, u_ref, eb_ref, dfb_ref, dmid_ref, db_ref, do_ref, out_ref, sums_ref = outs
    wo_back_ref = ins[7]
    one = LineTotal(scratch[1:8], chunks)
    two = LineTotal(scratch[8:15], chunks)
    back = LineTotal(scratch[15:22], chunks)
    sums_ref[...] = jnp.zeros_like(sums_ref)
    one.greet()

    def start(c):
        project_into(one, c, o_ref[one.rows(c), :], wo_ref)

    def feed(c):
        rows = one.rows(c)
        middle = h_ref[rows, :] + (one.take(c) + vec_ref[0:1, :])
        mid_ref[rows, :] = middle
        a2 = norm_rows(middle, vec_ref[1:2, :], vec_ref[2:3, :]).astype(jnp.bfloat16)
        a2_ref[rows, :] = a2
        e = e_ref[rows, :]
        add_sums(sums_ref, 0, e)
        eb = e.astype(jnp.bfloat16)
        eb_ref[rows, :] = eb
        for cols in column_blocks(we_ref.shape[1]):
            f = jnp.dot(a2, we_ref[:, cols], preferred_element_type=jnp.float32)
            f = f + vec_ref[3:4, cols]
            u, bent = gelu_value(f)
            u_ref[rows, cols] = u.astype(jnp.bfloat16)
            df = dot_rows(eb, wr_ref[cols, :]) * gelu_slope(f, bent)
            sums_ref[1:2, cols] += jnp.sum(df, axis=0, keepdims=True)
            dfb_ref[rows, cols] = df.astype(jnp.bfloat16)
        project_back_into(back, c, dfb_ref[rows, :], we_ref)
        project_into(two, c, u_ref[rows, :], wr_ref)

    def turn(c):
        rows = back.rows(c)
        cot = back.take(c)
        part, gain_part = norm_back(mid_ref[rows, :], vec_ref[1:2, :], cot)
        dmid = e_ref[rows, :] + part
        dmid_ref[rows, :] = dmid
        add_sums(sums_ref, 2, gain_part)
        add_sums(sums_ref, 3, cot)
        add_sums(sums_ref, 4, dmid)
        db = dmid.astype(jnp.bfloat16)
        db_ref[rows, :] = db
        do_ref[rows, :] = dot_rows(db, wo_back_ref[...]).astype(jnp.bfloat16)

    def end(c):
        rows = two.rows(c)
        out_ref[rows, :] = mid_ref[rows, :] + (two.take(c) + vec_ref[4:5, :])

    run_stages(
        chunks,
        [
            (0, start),
            (1, one.join),
            (2, one.finish),
            (3, feed),
            (4, back.join),
            (4, two.join),
            (5, back.finish),
            (5, two.finish),
            (6, turn),
            (6, end),
        ],
    )
    drain_all(chunks, [one, two, back])


def cross_kernel(chunks, *refs):
    ins, outs, scratch = refs[:10], refs[10:16], refs[16:]
    dproj_ref, wa_ref, h_ref, dmid_in_ref, vec_ref, f_ref, mid_ref, we_ref, wr_ref, wo_ref = ins
    eb_ref, dfb_ref, dmid_ref, db_ref, do_ref, sums_ref = outs
    e_ref = scratch[0]
    one = LineTotal(scratch[1:8], chunks)
    back = LineTotal(scratch[8:15], chunks)
    sums_ref[...] = jnp.zeros_like(sums_ref)
    one.greet()

    def start(c):
        project_back_into(one, c, dproj_ref[one.rows(c), :], wa_ref)

    def feed(c):
        rows = one.rows(c)
        cot = one.take(c)
        part, gain_part = norm_back(h_ref[rows, :], vec_ref[0:1, :], cot)
        e = dmid_in_ref[rows, :] + part
        e_ref[rows, :] = e
        add_sums(sums_ref, 0, gain_part)
        add_sums(sums_ref, 1, cot)
        add_sums(sums_ref, 2, e)
        eb = e.astype(jnp.bfloat16)
        eb_ref[rows, :] = eb
        for cols in column_blocks(we_ref.shape[1]):
            f = f_ref[rows, cols]
            unused, bent = gelu_value(f)
            df = dot_rows(eb, wr_ref[cols, :]) * gelu_slope(f, bent)
            sums_ref[3:4, cols] += jnp.sum(df, axis=0, keepdims=True)
            dfb_ref[rows, cols] = df.astype(jnp.bfloat16)
        project_back_into(back, c, dfb_ref[rows, :], we_ref)

    def turn(c):
        rows = back.rows(c)
        cot = back.take(c)
        part, gain_part = norm_back(mid_ref[rows, :], vec_ref[1:2, :], cot)
        dmid = e_ref[rows, :] + part
        dmid_ref[rows, :] = dmid
        add_sums(sums_ref, 4, gain_part)
        add_sums(sums_ref, 5, cot)
        add_sums(sums_ref, 6, dmid)
        db = dmid.astype(jnp.bfloat16)
        db_ref[rows, :] = db
        do_ref[rows, :] = dot_rows(db, wo_ref[...]).astype(jnp.bfloat16)

    run_stages(
        chunks,
        [
            (0, start),
            (1, one.join),
            (2, one.finish),
            (3, feed),
            (4, back.join),
            (5, back.finish),
            (6, turn),
        ],
    )
    drain_all(chunks, [one, back])


def last_kernel(chunks, *refs):
    ins, outs, scratch = refs[:5], refs[5:7], refs[7:]
    dproj_ref, wa_ref, h_ref, dmid_ref, vec_ref = ins
    grad_ref, sums_ref = outs
    one = LineTotal(scratch[:7], chunks)
    sums_ref[...] = jnp.zeros_like(sums_ref)
    one.greet()

    def start(c):
        project_back_into(one, c, dproj_ref[one.rows(c), :], wa_ref)

    def end(c):
        rows = one.rows(c)
        cot = one.take(c)
        part, gain_part = norm_back(h_ref[rows, :], vec_ref[0:1, :], cot)
        grad_ref[rows, :] = dmid_ref[rows, :] + part
        add_sums(sums_ref, 0, gain_part)
        add_sums(sums_ref, 1, cot)

    run_stages(chunks, [(0, start), (1, one.join), (2, one.finish), (3, end)])
    drain_all(chunks, [one])


CHUNKS = 8
MEGA = 1024 * 1024


def line_call(kernel, name, number, out_shapes, extra, lines, span_us, args):
    rows, model = extra
    scratch = []
    if lines[0]:
        scratch.append(pltpu.VMEM((rows, model), jnp.float32))
    for _ in range(lines[1]):
        scratch += LineTotal.scratch(rows, model, CHUNKS)
    return pl.pallas_call(
        functools.partial(kernel, CHUNKS),
        out_shape=tuple(jax.ShapeDtypeStruct(shape, kind) for shape, kind in out_shapes),
        in_specs=in_vmem(len(args)),
        out_specs=tuple(in_vmem(len(out_shapes))),
        scratch_shapes=scratch,
        cost_estimate=pl.CostEstimate(
            flops=int(span_us * 1e9), bytes_accessed=0, transcendentals=0
        ),
        compiler_params=pltpu.CompilerParams(
            collective_id=number, has_side_effects=True, vmem_limit_bytes=56 * MEGA
        ),
        name=name,
    )(*args)


def stack_rows(model, rows):
    rows = [jnp.pad(r, (0, model - r.shape[0])) for r in rows]
    rows += [jnp.zeros((model,), jnp.float32)] * (-len(rows) % 8)
    return jnp.stack(rows)


def window_of(kv_now, reach_back):
    kv_list = [passed_along(kv_now, "dp", hop) for hop in range(reach_back, 0, -1)]
    return jnp.concatenate(kv_list + [kv_now], axis=0)


def attention_cots(queries, window_kv, log_totals, context_cot, marks, reach_back):
    rows, width = queries.shape
    query_cot, kv_own, kv_back = attend_backward(
        queries, window_kv, log_totals, context_cot, marks[0], marks[1]
    )
    for hop in range(1, reach_back + 1):
        begin = (reach_back - hop) * rows
        kv_own = kv_own + passed_along(kv_back[begin : begin + rows], "dp", -hop).astype(
            jnp.float32
        )
    bias_grad = jnp.stack([jnp.sum(query_cot, axis=0), jnp.sum(kv_own[:, width:], axis=0)])
    rounded = jnp.concatenate(
        [query_cot.astype(jnp.bfloat16), kv_own.astype(jnp.bfloat16)], axis=1
    )
    return rounded, bias_grad


def weight_grad(left, right):
    return dot_tokens(left, right).astype(jnp.bfloat16)


def tied(*values):
    return lax.optimization_barrier(values)


def pair_layers(hidden_in, out_grad, params, marks, reach_back, model_parts):
    share, unit_share, size, part = model_parts
    bf16, f32 = jnp.bfloat16, jnp.float32
    rows, model = hidden_in.shape
    aw0, ab0, ow0, br0, ew0, eb0, rw0, g0, c0 = params[0]
    aw1, ab1, ow1, br1, ew1, eb1, rw1, g1, c1 = params[1]
    width = ow0.shape[0]
    units = ew0.shape[1]
    extra = (rows, model)

    def proj_bias(bias):
        return jnp.concatenate([bias[0], jnp.zeros_like(bias[0]), bias[1]])

    a1_0 = layer_norm(hidden_in, g0[0], c0[0]).astype(bf16)
    projected = jnp.dot(a1_0, aw0, preferred_element_type=f32) + proj_bias(ab0)
    q_0 = projected[:, :width].astype(bf16)
    window_0 = window_of(projected[:, width:].astype(bf16), reach_back)
    o_0, lse_0 = attend_forward(q_0, window_0, marks[0], marks[1])

    vec = stack_rows(model, [br0[0], g0[1], c0[1], eb0, br0[1], g1[0], c1[0], proj_bias(ab1)])
    mid_0, a2_0, f_0, u_0, h_1, a1_1, q_1, kv_1 = line_call(
        first_kernel,
        "first_tail",
        1,
        [
            ((rows, model), f32),
            ((rows, model), bf16),
            ((rows, units), f32),
            ((rows, units), bf16),
            ((rows, model), f32),
            ((rows, model), bf16),
            ((rows, width), bf16),
            ((rows, 2 * width), bf16),
        ],
        extra,
        (0, 2),
        50,
        (o_0, ow0, hidden_in, vec, ew0, rw0, aw1),
    )
    window_1 = window_of(kv_1, reach_back)
    o_1, lse_1 = attend_forward(q_1, window_1, marks[0], marks[1])

    vec = stack_rows(model, [br1[0], g1[1], c1[1], eb1, br1[1]])
    a2_1, u_1, eb_1, dfb_1, dmid_1, db_1, do_1, hidden_out, sums_1 = line_call(
        turn_kernel,
        "turn_tail",
        2,
        [
            ((rows, model), bf16),
            ((rows, units), bf16),
            ((rows, model), bf16),
            ((rows, units), bf16),
            ((rows, model), f32),
            ((rows, model), bf16),
            ((rows, width), bf16),
            ((rows, model), f32),
            ((8, model), f32),
        ],
        extra,
        (1, 3),
        70,
        (o_1, ow1, h_1, vec, ew1, rw1, out_grad, ow1),
    )
    expand_1 = weight_grad(a2_1, dfb_1)
    reduce_1 = weight_grad(u_1, eb_1)
    hidden_pack = jnp.concatenate([expand_1, pack_output(reduce_1, model, unit_share)], axis=1)
    hidden_pack, do_1 = tied(hidden_pack, do_1)
    hidden_sum_1 = scattered(hidden_pack)
    dproj_1, attend_bias_1 = attention_cots(q_1, window_1, lse_1, do_1, marks, reach_back)
    attend_1 = weight_grad(a1_1, dproj_1)
    output_1 = weight_grad(o_1, db_1)
    attend_pack = jnp.concatenate([attend_1, pack_output(output_1, model, share)], axis=1)
    attend_pack, dproj_1 = tied(attend_pack, dproj_1)
    attend_sum_1 = scattered(attend_pack)

    vec = stack_rows(model, [g1[0], g0[1]])
    eb_0, dfb_0, dmid_0, db_0, do_0, sums_0 = line_call(
        cross_kernel,
        "cross_tail",
        3,
        [
            ((rows, model), bf16),
            ((rows, units), bf16),
            ((rows, model), f32),
            ((rows, model), bf16),
            ((rows, width), bf16),
            ((8, model), f32),
        ],
        extra,
        (1, 2),
        60,
        (dproj_1, aw1, h_1, dmid_1, vec, f_0, mid_0, ew0, rw0, ow0),
    )
    do_0, hidden_sum_1 = tied(do_0, hidden_sum_1)
    expand_0 = weight_grad(a2_0, dfb_0)
    reduce_0 = weight_grad(u_0, eb_0)
    hidden_pack = jnp.concatenate([expand_0, pack_output(reduce_0, model, unit_share)], axis=1)
    hidden_pack, do_0 = tied(hidden_pack, do_0)
    hidden_sum_0 = scattered(hidden_pack)
    dproj_0, attend_bias_0 = attention_cots(q_0, window_0, lse_0, do_0, marks, reach_back)
    attend_0 = weight_grad(a1_0, dproj_0)
    output_0 = weight_grad(o_0, db_0)
    blocks = [attend_0, pack_output(output_0, model, share)]
    zero = jnp.zeros((model,), f32)
    small = (
        jnp.stack([attend_bias_0, attend_bias_1]),
        jnp.stack([jnp.stack([sums_0[6], sums_0[2]]), jnp.stack([sums_1[4], sums_1[0]])]),
        jnp.stack([sums_0[3, :units], sums_1[1, :units]]),
        jnp.stack([jnp.stack([zero, sums_0[4]]), jnp.stack([sums_0[0], sums_1[2]])]),
        jnp.stack([jnp.stack([zero, sums_0[5]]), jnp.stack([sums_0[1], sums_1[3]])]),
    )
    flat_rows = split_owned(small, None, size).astype(bf16)
    count = flat_rows.shape[1]
    room = part * LANES * (-(-count // (part * LANES)))
    padded = jnp.pad(flat_rows, ((0, 0), (0, room - count)))
    blocks.append(padded.reshape(size * part, room // part))
    attend_pack = jnp.concatenate(blocks, axis=1)
    attend_pack, dproj_0, attend_sum_1 = tied(attend_pack, dproj_0, attend_sum_1)
    attend_sum_0 = scattered(attend_pack)

    vec = stack_rows(model, [g0[0]])
    in_grad, sums_in = line_call(
        last_kernel,
        "last_tail",
        4,
        [((rows, model), f32), ((8, model), f32)],
        extra,
        (0, 1),
        30,
        (dproj_0, aw0, hidden_in, dmid_0, vec),
    )
    late = lax.psum_scatter(sums_in[:2].astype(bf16), "dp", scatter_dimension=1, tiled=True)
    return (
        hidden_out,
        in_grad,
        [hidden_sum_0, hidden_sum_1],
        [attend_sum_0, attend_sum_1],
        late.astype(f32),
    )


def layer_by_layer(hidden_in, out_grad, params, marks, reach_back, model_parts):
    share, unit_share, size, part = model_parts
    model = hidden_in.shape[1]
    saved = []
    current = hidden_in
    for layer in range(len(params)):
        current, kept_state = forward_layer(current, params[layer], marks, reach_back)
        saved.append(kept_state)
    grad_now = out_grad
    hidden_list = [None] * len(params)
    attend_list = [None] * len(params)
    small_list = [None] * len(params)
    for layer in reversed(range(len(params))):
        grad_now, expand_grad, reduce_grad, attend_grad, output_grad, small = backward_layer(
            grad_now, params[layer], saved[layer], marks, reach_back
        )
        hidden_list[layer] = scattered(
            jnp.concatenate([expand_grad, pack_output(reduce_grad, model, unit_share)], axis=1)
        )
        small_list[layer] = small
        blocks = [attend_grad, pack_output(output_grad, model, share)]
        if layer == 0:
            stacked = [jnp.stack([entry[i] for entry in small_list]) for i in range(len(small))]
            flat_rows = split_owned(stacked, None, size).astype(jnp.bfloat16)
            count = flat_rows.shape[1]
            room = part * LANES * (-(-count // (part * LANES)))
            padded = jnp.pad(flat_rows, ((0, 0), (0, room - count)))
            blocks.append(padded.reshape(size * part, room // part))
        packed = jnp.concatenate(blocks, axis=1)
        if layer > 0:
            grad_now, packed = lax.optimization_barrier((grad_now, packed))
        attend_list[layer] = scattered(packed)
    return current, grad_now, hidden_list, attend_list


def local(
    hidden_in,
    doc_ids,
    attend_weight,
    attend_bias,
    output_weight,
    branch_bias,
    expand_weight,
    expand_bias,
    reduce_weight,
    norm_gain,
    norm_bias,
    out_grad,
):
    size = lax.axis_size("dp")
    layer_count, part, three, width = attend_weight.shape
    tok_rows, model = hidden_in.shape
    share = output_weight.shape[1]
    unit_share = reduce_weight.shape[1]
    hidden_units = expand_weight.shape[2]
    reach_back = (CTX + tok_rows - 2) // tok_rows
    own_row = doc_ids + 1
    mark_list = [passed_along(own_row, "dp", hop) for hop in range(reach_back, 0, -1)]
    marks = (own_row[:, None], jnp.concatenate(mark_list + [own_row])[None, :])

    small_in = (attend_bias, branch_bias, expand_bias, norm_gain, norm_bias)
    flat = jnp.concatenate([entry.reshape(-1) for entry in small_in])
    flat_all = lax.all_gather(flat[None], "dp", axis=0, tiled=True)
    small_full = []
    at = 0
    for entry in small_in:
        piece = flat_all[:, at : at + entry.size].reshape((size,) + entry.shape)
        at += entry.size
        piece = jnp.moveaxis(piece, 0, -2)
        small_full.append(
            piece.reshape(entry.shape[:-1] + (size * entry.shape[-1],)).astype(jnp.float32)
        )
    attend_b, branches, expand_b, gains, offsets = small_full

    params = []
    for layer in range(layer_count):
        first = lax.all_gather(
            jnp.concatenate(
                [
                    attend_weight[layer].reshape(part, three * width),
                    pack_output(output_weight[layer], model, share),
                ],
                axis=1,
            ),
            "dp",
            axis=0,
            tiled=True,
        )
        second = lax.all_gather(
            jnp.concatenate(
                [expand_weight[layer], pack_output(reduce_weight[layer], model, unit_share)],
                axis=1,
            ),
            "dp",
            axis=0,
            tiled=True,
        )
        params.append(
            (
                first[:, : three * width],
                attend_b[layer],
                unpack_output(first[:, three * width :], model, share),
                branches[layer],
                second[:, :hidden_units],
                expand_b[layer],
                unpack_output(second[:, hidden_units:], model, unit_share),
                gains[layer],
                offsets[layer],
            )
        )
    late = None
    if lax.axis_size("tensor") == 4 and layer_count == 2 and tok_rows % 128 == 0:
        current, grad_now, hidden_list, attend_list, late = pair_layers(
            hidden_in, out_grad, params, marks, reach_back, (share, unit_share, size, part)
        )
    else:
        current, grad_now, hidden_list, attend_list = layer_by_layer(
            hidden_in, out_grad, params, marks, reach_back, (share, unit_share, size, part)
        )
    hidden_out = [entry.astype(jnp.float32) for entry in hidden_list]
    attend_out = [entry.astype(jnp.float32) for entry in attend_list]
    fold = three * width
    slab = model * share // part
    tail = attend_out[0][:, fold + slab :].reshape(-1)
    small_out = []
    at = 0
    for entry in small_in:
        small_out.append(tail[at : at + entry.size].reshape(entry.shape))
        at += entry.size
    attend_bgrad, branch_bgrad, expand_bgrad, gain_grad, offset_grad = small_out
    if late is not None:
        gain_grad = gain_grad.at[0, 0].set(late[0])
        offset_grad = offset_grad.at[0, 0].set(late[1])
    return (
        current,
        grad_now,
        jnp.stack([entry[:, :fold].reshape(part, three, width) for entry in attend_out]),
        attend_bgrad,
        jnp.stack([unpack_output(entry[:, fold : fold + slab], model, share) for entry in attend_out]),
        branch_bgrad,
        jnp.stack([entry[:, :hidden_units] for entry in hidden_out]),
        expand_bgrad,
        jnp.stack(
            [unpack_output(entry[:, hidden_units:], model, unit_share) for entry in hidden_out]
        ),
        gain_grad,
        offset_grad,
    )


def solution(mesh):
    return jax.shard_map(
        local,
        mesh=mesh,
        in_specs=(
            P("dp", None),
            P("dp"),
            P(None, "dp", None, "tensor"),
            P(None, None, ("tensor", "dp")),
            P(None, ("tensor", "dp"), None),
            P(None, None, "dp"),
            P(None, "dp", "tensor"),
            P(None, ("tensor", "dp")),
            P(None, ("tensor", "dp"), None),
            P(None, None, "dp"),
            P(None, None, "dp"),
            P("dp", None),
        ),
        out_specs=(
            P("dp", None),
            P("dp", None),
            P(None, "dp", None, "tensor"),
            P(None, None, ("tensor", "dp")),
            P(None, ("tensor", "dp"), None),
            P(None, None, "dp"),
            P(None, "dp", "tensor"),
            P(None, ("tensor", "dp")),
            P(None, ("tensor", "dp"), None),
            P(None, None, "dp"),
            P(None, None, "dp"),
        ),
        check_vma=False,
    )
```

```python
import functools
import math

import jax
import jax.numpy as jnp
from jax import lax
from jax.experimental import pallas as pl
from jax.experimental.pallas import tpu as pltpu
from jax.sharding import PartitionSpec as P

HEAD_DIM = 64
CTX = 1024
LANES = 128
ROW_TILE = 256


def passed_along(block, axis, distance):
    devices = range(lax.axis_size(axis))
    route = [(i - distance, i) for i in devices if i - distance in devices]
    return lax.ppermute(block, axis, route)


def contract(pattern, left_side, right_side):
    return jnp.einsum(pattern, left_side, right_side, preferred_element_type=jnp.float32)


def layer_norm(values, gain_row, offset_row):
    center = values - jnp.mean(values, axis=-1, keepdims=True)
    spread = jnp.mean(center * center, axis=-1, keepdims=True)
    return center * lax.rsqrt(spread + 1e-05) * gain_row + offset_row


def gelu_tanh(values):
    return (
        0.5
        * values
        * (1.0 + jnp.tanh(0.7978845608028654 * (values + 0.044715 * values * values * values)))
    )


def dot_rows(left_side, right_side):
    return lax.dot_general(
        left_side, right_side, (((1,), (1,)), ((), ())), preferred_element_type=jnp.float32
    )


def dot_tokens(left_side, right_side):
    return lax.dot_general(
        left_side, right_side, (((0,), (0,)), ((), ())), preferred_element_type=jnp.float32
    )


def row_tiles(rows, window_rows):
    tile = min(ROW_TILE, rows)
    back = window_rows - rows
    for start in range(0, rows, tile):
        low = max(0, (back + start - CTX + 1) // LANES * LANES)
        yield start, tile, low, back + start + tile


def tile_mask(own_ref, window_ref, start, tile, low, high, back):
    own = own_ref[start : start + tile, :]
    window = window_ref[:, low:high]
    row = lax.broadcasted_iota(jnp.int32, (tile, high - low), 0) + (start + back)
    col = lax.broadcasted_iota(jnp.int32, (tile, high - low), 1) + low
    return (window == own) & (col <= row)


def head_parts(width):
    group = min(LANES, width)
    for base in range(0, width, group):
        for inner in range(0, group, HEAD_DIM):
            yield base, group, inner


def pick(block, inner):
    lane = lax.broadcasted_iota(jnp.int32, block.shape, 1)
    return jnp.where((lane >= inner) & (lane < inner + HEAD_DIM), block, jnp.zeros_like(block))


def forward_kernel(q_ref, kv_ref, own_ref, window_ref, o_ref, lse_ref):
    rows, width = q_ref.shape
    window_rows = kv_ref.shape[0]
    back = window_rows - rows
    factor = 1.0 / math.sqrt(HEAD_DIM)
    for start, tile, low, high in row_tiles(rows, window_rows):
        allowed = tile_mask(own_ref, window_ref, start, tile, low, high, back)
        held = None
        logs = []
        for base, group, inner in head_parts(width):
            queries = pick(q_ref[start : start + tile, base : base + group], inner)
            keys = kv_ref[low:high, base : base + group]
            values = kv_ref[low:high, width + base : width + base + group]
            unnormed = jnp.where(allowed, jnp.exp(dot_rows(queries, keys) * factor), 0.0)
            totals = jnp.sum(unnormed, axis=-1, keepdims=True)
            probabilities = (unnormed * (1.0 / totals)).astype(jnp.bfloat16)
            context = pick(
                jnp.dot(probabilities, values, preferred_element_type=jnp.float32), inner
            )
            held = context if inner == 0 else held + context
            logs.append(jnp.log(totals))
            if inner + HEAD_DIM == group:
                o_ref[start : start + tile, base : base + group] = held.astype(jnp.bfloat16)
        for index, entry in enumerate(logs):
            lse_ref[start : start + tile, index : index + 1] = entry


def backward_kernel(
    q_ref, kv_ref, lse_ref, cot_ref, own_ref, window_ref, dq_ref, own_out, back_out, acc
):
    rows, width = q_ref.shape
    window_rows = kv_ref.shape[0]
    back = window_rows - rows
    factor = 1.0 / math.sqrt(HEAD_DIM)
    acc[...] = jnp.zeros_like(acc)
    for start, tile, low, high in row_tiles(rows, window_rows):
        allowed = tile_mask(own_ref, window_ref, start, tile, low, high, back)
        held = None
        for index, (base, group, inner) in enumerate(head_parts(width)):
            queries = pick(q_ref[start : start + tile, base : base + group], inner)
            cots = pick(cot_ref[start : start + tile, base : base + group], inner)
            keys = kv_ref[low:high, base : base + group]
            values = kv_ref[low:high, width + base : width + base + group]
            logs = lse_ref[start : start + tile, index : index + 1]
            scores = dot_rows(queries, keys) * factor
            probabilities = jnp.where(allowed, jnp.exp(scores - logs), 0.0)
            rounded = probabilities.astype(jnp.bfloat16)
            acc[low:high, width + base : width + base + group] += dot_tokens(rounded, cots)
            prob_cot = dot_rows(cots, values)
            inner_sum = jnp.sum(probabilities * prob_cot, axis=-1, keepdims=True)
            score_cot = (probabilities * (prob_cot - inner_sum) * factor).astype(jnp.bfloat16)
            acc[low:high, base : base + group] += dot_tokens(score_cot, queries)
            part = pick(jnp.dot(score_cot, keys, preferred_element_type=jnp.float32), inner)
            held = part if inner == 0 else held + part
            if inner + HEAD_DIM == group:
                dq_ref[start : start + tile, base : base + group] = held
    own_out[...] = acc[back:, :]
    back_out[...] = acc[:back, :].astype(jnp.bfloat16)


def in_vmem(count):
    return [pl.BlockSpec(memory_space=pltpu.VMEM)] * count


def attend_forward(queries, window_kv, own_marks, window_marks):
    rows, width = queries.shape
    return pl.pallas_call(
        forward_kernel,
        out_shape=(
            jax.ShapeDtypeStruct((rows, width), jnp.bfloat16),
            jax.ShapeDtypeStruct((rows, width // HEAD_DIM), jnp.float32),
        ),
        in_specs=in_vmem(4),
        out_specs=tuple(in_vmem(2)),
        compiler_params=pltpu.CompilerParams(vmem_limit_bytes=40 * 1024 * 1024),
        name="attend_forward",
    )(queries, window_kv, own_marks, window_marks)


def attend_backward(queries, window_kv, log_totals, out_cot, own_marks, window_marks):
    rows, width = queries.shape
    window_rows = window_kv.shape[0]
    return pl.pallas_call(
        backward_kernel,
        out_shape=(
            jax.ShapeDtypeStruct((rows, width), jnp.float32),
            jax.ShapeDtypeStruct((rows, 2 * width), jnp.float32),
            jax.ShapeDtypeStruct((window_rows - rows, 2 * width), jnp.bfloat16),
        ),
        in_specs=in_vmem(6),
        out_specs=tuple(in_vmem(3)),
        scratch_shapes=[pltpu.VMEM((window_rows, 2 * width), jnp.float32)],
        compiler_params=pltpu.CompilerParams(vmem_limit_bytes=48 * 1024 * 1024),
        name="attend_backward",
    )(queries, window_kv, log_totals, out_cot, own_marks, window_marks)


def line_kernel(chunks, x_ref, o_ref, from_near, from_mid, pair, total, near_send, mid_send, near_recv, mid_recv):
    place = lax.axis_index("tensor")
    near = place + 1 - 2 * lax.rem(place, 2)
    across = 3 - place
    is_end = (place == 0) | (place == 3)
    is_mid = (place == 1) | (place == 2)
    step = x_ref.shape[0] // chunks
    barrier = pltpu.get_barrier_semaphore()

    def part(ref, c):
        return ref.at[pl.ds(c * step, step)]

    def to_near(src, c):
        return pltpu.make_async_remote_copy(
            src_ref=part(src, c),
            dst_ref=part(from_near, c),
            send_sem=near_send.at[c],
            recv_sem=near_recv.at[c],
            device_id={"tensor": near},
            device_id_type=pl.DeviceIdType.MESH,
        )

    def to_mid(c):
        return pltpu.make_async_remote_copy(
            src_ref=part(pair, c),
            dst_ref=part(from_mid, c),
            send_sem=mid_send.at[c],
            recv_sem=mid_recv.at[c],
            device_id={"tensor": across},
            device_id_type=pl.DeviceIdType.MESH,
        )

    def added(left, right, c):
        rows = pl.ds(c * step, step)
        both = left[rows, :].astype(jnp.float32) + right[rows, :].astype(jnp.float32)
        return both.astype(jnp.bfloat16)

    pl.semaphore_signal(
        barrier, inc=1, device_id={"tensor": near}, device_id_type=pl.DeviceIdType.MESH
    )

    @pl.when(is_end)
    def _():
        pl.semaphore_wait(barrier, 1)
        for c in range(chunks):
            to_near(x_ref, c).start()
        for c in range(chunks):
            to_near(x_ref, c).wait_recv()
            rows = pl.ds(c * step, step)
            o_ref[rows, :] = from_near[rows, :]
        for c in range(chunks):
            to_near(x_ref, c).wait_send()

    @pl.when(is_mid)
    def _():
        pl.semaphore_signal(
            barrier, inc=1, device_id={"tensor": across}, device_id_type=pl.DeviceIdType.MESH
        )
        pl.semaphore_wait(barrier, 2)
        lag = 2
        for c in range(chunks + lag):
            if c < chunks:
                to_near(total, c).wait_recv()
                pair[pl.ds(c * step, step), :] = added(x_ref, from_near, c)
                to_mid(c).start()
            done = c - lag
            if done >= 0:
                to_mid(done).wait_recv()
                result = added(pair, from_mid, done)
                total[pl.ds(done * step, step), :] = result
                to_near(total, done).start()
                o_ref[pl.ds(done * step, step), :] = result
        for c in range(chunks):
            to_mid(c).wait_send()
            to_near(total, c).wait_send()


def tensor_total(partial_value):
    rounded = partial_value.astype(jnp.bfloat16)
    rows = rounded.shape[0]
    if lax.axis_size("tensor") != 4 or rows % 128:
        return lax.psum(rounded, "tensor").astype(jnp.float32)
    chunks = 8
    block = pltpu.VMEM(rounded.shape, jnp.bfloat16)
    summed = pl.pallas_call(
        functools.partial(line_kernel, chunks),
        out_shape=jax.ShapeDtypeStruct(rounded.shape, jnp.bfloat16),
        in_specs=in_vmem(1),
        out_specs=in_vmem(1)[0],
        scratch_shapes=[block] * 4 + [pltpu.SemaphoreType.DMA((chunks,))] * 4,
        compiler_params=pltpu.CompilerParams(
            collective_id=0, has_side_effects=True, vmem_limit_bytes=24 * 1024 * 1024
        ),
        name="line_total",
    )(rounded)
    return summed.astype(jnp.float32)


def forward_layer(hidden, params, marks, reach_back):
    attend_w, attend_b, output_w, branches, expand_w, expand_b, reduce_w, gains, offsets = params
    width = output_w.shape[0]
    own_marks, window_marks = marks
    normed_one = layer_norm(hidden, gains[0], offsets[0]).astype(jnp.bfloat16)
    projected = jnp.dot(normed_one, attend_w, preferred_element_type=jnp.float32)
    queries = (projected[:, :width] + attend_b[0]).astype(jnp.bfloat16)
    kv_bias = jnp.concatenate([jnp.zeros_like(attend_b[1]), attend_b[1]])
    kv_now = (projected[:, width:] + kv_bias).astype(jnp.bfloat16)
    kv_list = [passed_along(kv_now, "dp", hop) for hop in range(reach_back, 0, -1)]
    window_kv = jnp.concatenate(kv_list + [kv_now], axis=0)
    context, log_totals = attend_forward(queries, window_kv, own_marks, window_marks)
    attended = tensor_total(jnp.dot(context, output_w, preferred_element_type=jnp.float32))
    middle = hidden + (attended + branches[0])
    normed_two = layer_norm(middle, gains[1], offsets[1]).astype(jnp.bfloat16)
    pre_act = jnp.dot(normed_two, expand_w, preferred_element_type=jnp.float32) + expand_b
    activated = gelu_tanh(pre_act).astype(jnp.bfloat16)
    reduced = tensor_total(jnp.dot(activated, reduce_w, preferred_element_type=jnp.float32))
    output = middle + (reduced + branches[1])
    kept_state = (
        hidden,
        normed_one,
        queries,
        window_kv,
        context,
        log_totals,
        middle,
        normed_two,
        pre_act,
        activated,
    )
    return (output, kept_state)


def backward_layer(grad_out, params, kept_state, marks, reach_back):
    attend_w, attend_b, output_w, branches, expand_w, expand_b, reduce_w, gains, offsets = params
    (
        hidden,
        normed_one,
        queries,
        window_kv,
        context,
        log_totals,
        middle,
        normed_two,
        pre_act,
        activated,
    ) = kept_state
    own_marks, window_marks = marks
    rows = hidden.shape[0]
    width = output_w.shape[0]
    bias_two = jnp.sum(grad_out, axis=0)
    grad_rounded = grad_out.astype(jnp.bfloat16)
    act_cot = contract("td,fd->tf", grad_rounded, reduce_w)
    unused, gelu_pull = jax.vjp(gelu_tanh, pre_act)
    pre_cot = gelu_pull(act_cot)[0]
    expand_bias_grad = jnp.sum(pre_cot, axis=0)
    pre_rounded = pre_cot.astype(jnp.bfloat16)
    normed_cot = tensor_total(contract("tf,df->td", pre_rounded, expand_w))
    reduce_grad = contract("tf,td->fd", activated, grad_rounded).astype(jnp.bfloat16)
    expand_grad = contract("td,tf->df", normed_two, pre_rounded).astype(jnp.bfloat16)
    unused, norm_pull = jax.vjp(layer_norm, middle, gains[1], offsets[1])
    mid_part, gain_two, offset_two = norm_pull(normed_cot)
    mid_cot = grad_out + mid_part
    bias_one = jnp.sum(mid_cot, axis=0)
    mid_rounded = mid_cot.astype(jnp.bfloat16)
    output_grad = contract("tk,td->kd", context, mid_rounded).astype(jnp.bfloat16)
    context_cot = contract("td,kd->tk", mid_rounded, output_w).astype(jnp.bfloat16)
    context_cot, expand_grad, reduce_grad = lax.optimization_barrier(
        (context_cot, expand_grad, reduce_grad)
    )
    query_cot, kv_own, kv_back = attend_backward(
        queries, window_kv, log_totals, context_cot, own_marks, window_marks
    )
    for hop in range(1, reach_back + 1):
        begin = (reach_back - hop) * rows
        kv_own = kv_own + passed_along(kv_back[begin : begin + rows], "dp", -hop).astype(
            jnp.float32
        )
    attend_bias_grad = jnp.stack([jnp.sum(query_cot, axis=0), jnp.sum(kv_own[:, width:], axis=0)])
    proj_rounded = jnp.concatenate(
        [query_cot.astype(jnp.bfloat16), kv_own.astype(jnp.bfloat16)], axis=1
    )
    normed_cot_one = tensor_total(contract("tc,dc->td", proj_rounded, attend_w))
    attend_grad = contract("td,tc->dc", normed_one, proj_rounded).astype(jnp.bfloat16)
    unused, first_pull = jax.vjp(layer_norm, hidden, gains[0], offsets[0])
    hid_part, gain_one, offset_one = first_pull(normed_cot_one)
    in_cot = mid_cot + hid_part
    small = (
        attend_bias_grad,
        jnp.stack([bias_one, bias_two]),
        expand_bias_grad,
        jnp.stack([gain_one, gain_two]),
        jnp.stack([offset_one, offset_two]),
    )
    return (in_cot, expand_grad, reduce_grad, attend_grad, output_grad, small)


def scattered(block):
    return lax.psum_scatter(block, "dp", scatter_dimension=0, tiled=True)


def pack_output(block, model, share):
    part = model // lax.axis_size("dp")
    slabs = part // share
    owners = block.shape[0] // share
    return (
        block.reshape(owners, share, slabs, model // slabs)
        .transpose(0, 2, 1, 3)
        .reshape(owners * part, model // slabs)
    )


def unpack_output(block, model, share):
    part = model // lax.axis_size("dp")
    slabs = part // share
    owners = block.shape[0] // part
    return (
        block.reshape(owners, slabs, share, model // slabs)
        .transpose(0, 2, 1, 3)
        .reshape(owners * share, model)
    )


def split_owned(pieces, sizes, size):
    rows = [
        jnp.moveaxis(p.reshape(p.shape[:-1] + (size, p.shape[-1] // size)), -2, 0).reshape(size, -1)
        for p in pieces
    ]
    return jnp.concatenate(rows, axis=1)


GELU_SCALE = 0.7978845608028654
GELU_CUBIC = 0.044715
COLUMNS = 256


def column_blocks(width):
    size = min(COLUMNS, width)
    return [slice(start, start + size) for start in range(0, width, size)]


def norm_parts(values):
    center = values - jnp.mean(values, axis=-1, keepdims=True)
    inverse = lax.rsqrt(jnp.mean(center * center, axis=-1, keepdims=True) + 1e-05)
    return center * inverse, inverse


def norm_rows(values, gain_row, offset_row):
    return norm_parts(values)[0] * gain_row + offset_row


def norm_back(values, gain_row, cot):
    normal, inverse = norm_parts(values)
    scaled = cot * gain_row
    mean_one = jnp.mean(scaled, axis=-1, keepdims=True)
    mean_two = jnp.mean(scaled * normal, axis=-1, keepdims=True)
    return inverse * (scaled - mean_one - normal * mean_two), cot * normal


def gelu_value(values):
    bent = jnp.tanh(GELU_SCALE * (values + GELU_CUBIC * values * values * values))
    return 0.5 * values * (1.0 + bent), bent


def gelu_slope(values, bent):
    inner = GELU_SCALE * (1.0 + 3.0 * GELU_CUBIC * values * values)
    return 0.5 * (1.0 + bent) + 0.5 * values * (1.0 - bent * bent) * inner


class LineTotal:
    scratch_count = 7

    @staticmethod
    def scratch(rows, model, chunks):
        block = pltpu.VMEM((rows, model), jnp.bfloat16)
        return [block] * 3 + [pltpu.SemaphoreType.DMA((chunks,))] * 4

    def __init__(self, refs, chunks):
        self.own, self.near_buf, self.mid_buf = refs[:3]
        self.near_send, self.near_recv, self.mid_send, self.mid_recv = refs[3:]
        self.chunks = chunks
        self.step = self.own.shape[0] // chunks
        place = lax.axis_index("tensor")
        self.near = place + 1 - 2 * lax.rem(place, 2)
        self.across = 3 - place
        self.is_end = (place == 0) | (place == 3)
        self.is_mid = (place == 1) | (place == 2)

    def rows(self, c):
        return pl.ds(pl.multiple_of(c * self.step, self.step), self.step)

    def to_near(self, src, c):
        return pltpu.make_async_remote_copy(
            src_ref=src.at[self.rows(c)],
            dst_ref=self.near_buf.at[self.rows(c)],
            send_sem=self.near_send.at[c],
            recv_sem=self.near_recv.at[c],
            device_id={"tensor": self.near},
            device_id_type=pl.DeviceIdType.MESH,
        )

    def to_across(self, c):
        return pltpu.make_async_remote_copy(
            src_ref=self.own.at[self.rows(c)],
            dst_ref=self.mid_buf.at[self.rows(c)],
            send_sem=self.mid_send.at[c],
            recv_sem=self.mid_recv.at[c],
            device_id={"tensor": self.across},
            device_id_type=pl.DeviceIdType.MESH,
        )

    def peers(self):
        return [
            (self.is_end | self.is_mid, "tensor", self.near),
            (self.is_mid, "tensor", self.across),
        ]

    def send(self, c):
        @pl.when(self.is_end)
        def _():
            self.to_near(self.own, c).start()

    def summed(self, left, right, c):
        rows = self.rows(c)
        both = left[rows, :].astype(jnp.float32) + right[rows, :].astype(jnp.float32)
        return both.astype(jnp.bfloat16)

    def join(self, c):
        @pl.when(self.is_mid)
        def _():
            self.to_near(self.near_buf, c).wait_recv()
            self.own[self.rows(c), :] = self.summed(self.own, self.near_buf, c)
            self.to_across(c).start()

    def finish(self, c):
        @pl.when(self.is_mid)
        def _():
            self.to_across(c).wait_recv()
            self.near_buf[self.rows(c), :] = self.summed(self.own, self.mid_buf, c)
            self.to_near(self.near_buf, c).start()

    def take(self, c):
        @pl.when(self.is_end)
        def _():
            self.to_near(self.own, c).wait_recv()

        return self.near_buf[self.rows(c), :].astype(jnp.float32)

    def drain(self, c):
        @pl.when(self.is_end)
        def _():
            self.to_near(self.own, c).wait_send()

        @pl.when(self.is_mid)
        def _():
            self.to_across(c).wait_send()
            self.to_near(self.near_buf, c).wait_send()


def flipped(place, bit):
    return place + bit - 2 * bit * lax.rem(lax.div(place, bit), 2)


def dp_copy(src, dst, send_sem, recv_sem, target):
    return pltpu.make_async_remote_copy(
        src_ref=src,
        dst_ref=dst,
        send_sem=send_sem,
        recv_sem=recv_sem,
        device_id={"dp": target},
        device_id_type=pl.DeviceIdType.MESH,
    )


def greet(targets):
    barrier = pltpu.get_barrier_semaphore()
    count = 0
    for known, axis, target in targets:
        count = count + jnp.where(known, 1, 0)

        @pl.when(known)
        def _(axis=axis, target=target):
            pl.semaphore_signal(
                barrier, inc=1, device_id={axis: target}, device_id_type=pl.DeviceIdType.MESH
            )

    pl.semaphore_wait(barrier, count)


def cube_targets():
    place = lax.axis_index("dp")
    return [(place >= 0, "dp", flipped(place, bit)) for bit in (1, 2, 4)]


def window_targets(hops):
    place = lax.axis_index("dp")
    size = lax.axis_size("dp")
    after = [(place + hop < size, "dp", place + hop) for hop in range(1, hops + 1)]
    return after + [(place - hop >= 0, "dp", place - hop) for hop in range(1, hops + 1)]


class Gather:
    copies = 8

    @staticmethod
    def scratch():
        return [pltpu.SemaphoreType.DMA((Gather.copies,))] * 2

    def __init__(self, own_ref, full_ref, sems):
        self.own, self.full = own_ref, full_ref
        self.send, self.recv = sems
        self.size = own_ref.shape[0]
        self.place = lax.axis_index("dp")

    def span(self, owner, part=None):
        size = self.size if part is None else self.size // 2
        first = owner * self.size + (0 if not part else size)
        return self.full.at[pl.ds(pl.multiple_of(first, size), size)]

    def copy(self, k):
        me = self.place
        fx, fy, sib = flipped(me, 2), flipped(me, 4), flipped(me, 1)
        src, dst, target = {
            0: lambda: (self.own, self.span(me), fx),
            1: lambda: (self.own, self.span(me), fy),
            2: lambda: (self.own, self.span(me), sib),
            3: lambda: (self.span(fx, 0), self.span(fx, 0), fy),
            4: lambda: (self.span(fy, 1), self.span(fy, 1), fx),
            5: lambda: (self.span(fx), self.span(fx), sib),
            6: lambda: (self.span(fy), self.span(fy), sib),
            7: lambda: (self.span(flipped(fx, 4)), self.span(flipped(fx, 4)), sib),
        }[k]()
        return dp_copy(src, dst, self.send.at[k], self.recv.at[k], target)

    def begin(self):
        first = pl.multiple_of(self.place * self.size, self.size)
        self.full[pl.ds(first, self.size), :] = self.own[...]
        for k in (0, 1, 2):
            self.copy(k).start()

    def relay(self):
        self.copy(0).wait_recv()
        self.copy(3).start()
        self.copy(5).start()
        self.copy(1).wait_recv()
        self.copy(4).start()
        self.copy(6).start()

    def pass_on(self):
        self.copy(3).wait_recv()
        self.copy(4).wait_recv()
        self.copy(7).start()

    def finish(self):
        for k in (2, 5, 6, 7):
            self.copy(k).wait_recv()

    def drain(self):
        for k in range(self.copies):
            self.copy(k).wait_send()


class Scatter:
    copies = 10
    refs = 7

    @staticmethod
    def scratch(rows, width):
        half = rows // 2
        return [
            pltpu.VMEM((4, rows, width), jnp.bfloat16),
            pltpu.VMEM((2, half, width), jnp.bfloat16),
            pltpu.VMEM((2, half, width), jnp.bfloat16),
            pltpu.VMEM((half, width), jnp.bfloat16),
            pltpu.VMEM((half, width), jnp.bfloat16),
            pltpu.SemaphoreType.DMA((Scatter.copies,)),
            pltpu.SemaphoreType.DMA((Scatter.copies,)),
        ]

    def __init__(self, grad_ref, out_ref, refs):
        self.grad, self.out = grad_ref, out_ref
        self.acc, self.x_one, self.y_one, self.x_two, self.y_two, self.send, self.recv = refs
        self.size = out_ref.shape[0]
        me = lax.axis_index("dp")
        self.core = lax.rem(me, 2)
        self.sib, self.fx, self.fy = flipped(me, 1), flipped(me, 2), flipped(me, 4)
        self.here, self.qx, self.qy = (lax.div(v, 2) for v in (me, self.fx, self.fy))
        self.qxy = lax.div(flipped(self.fx, 4), 2)

    def owner_rows(self, chip, core):
        first = (2 * chip + core) * self.size
        return pl.ds(pl.multiple_of(first, self.size), self.size)

    def half(self, which):
        count = self.size // 2
        return pl.ds(which * count, count)

    def to_core(self, chip):
        src = self.grad.at[self.owner_rows(chip, 1 - self.core)]
        return dp_copy(src, self.acc.at[chip], self.send.at[chip], self.recv.at[chip], self.sib)

    def copy(self, k):
        acc, low, high = self.acc, self.half(0), self.half(1)
        src, dst, target = {
            4: lambda: (acc.at[self.qx, low], self.x_one.at[0], self.fx),
            5: lambda: (acc.at[self.qxy, low], self.x_one.at[1], self.fx),
            6: lambda: (acc.at[self.qy, high], self.y_one.at[0], self.fy),
            7: lambda: (acc.at[self.qxy, high], self.y_one.at[1], self.fy),
            8: lambda: (acc.at[self.qy, low], self.y_two, self.fy),
            9: lambda: (acc.at[self.qx, high], self.x_two, self.fx),
        }[k]()
        return dp_copy(src, dst, self.send.at[k], self.recv.at[k], target)

    def begin(self):
        for chip in range(4):
            self.to_core(chip).start()

    def add_core(self, chip):
        self.to_core(chip).wait_recv()
        first = self.owner_rows(chip, self.core).start
        count = self.size // 2
        for which in (0, 1):
            rows = pl.ds(pl.multiple_of(first + which * count, count), count)
            total = self.acc[chip, self.half(which), :].astype(jnp.float32)
            total = total + self.grad[rows, :].astype(jnp.float32)
            self.acc[chip, self.half(which), :] = total.astype(jnp.bfloat16)

    def spread(self):
        self.add_core(self.qxy)
        self.copy(5).start()
        self.copy(7).start()
        self.add_core(self.qx)
        self.copy(4).start()
        self.add_core(self.qy)
        self.copy(6).start()
        self.add_core(self.here)

    def add_half(self, chip, which, other):
        total = self.acc[chip, self.half(which), :].astype(jnp.float32)
        self.acc[chip, self.half(which), :] = (total + other.astype(jnp.float32)).astype(
            jnp.bfloat16
        )

    def narrow(self):
        self.copy(5).wait_recv()
        self.add_half(self.qy, 0, self.x_one[1])
        self.copy(8).start()
        self.copy(7).wait_recv()
        self.add_half(self.qx, 1, self.y_one[1])
        self.copy(9).start()

    def close(self):
        for k in (4, 6, 8, 9):
            self.copy(k).wait_recv()
        pairs = ((self.x_one, self.y_two), (self.y_one, self.x_two))
        for which, (one, two) in enumerate(pairs):
            total = self.acc[self.here, self.half(which), :].astype(jnp.float32)
            total = total + one[0].astype(jnp.float32) + two[...].astype(jnp.float32)
            self.out[self.half(which), :] = total

    def drain(self):
        for chip in range(4):
            self.to_core(chip).wait_send()
        for k in range(4, self.copies):
            self.copy(k).wait_send()


def scatters_of(grads, outs, scratch):
    count = Scatter.refs
    return [
        Scatter(g, o, scratch[count * i : count * (i + 1)])
        for i, (g, o) in enumerate(zip(grads, outs))
    ]


class Window:
    @staticmethod
    def scratch(hops, chunks):
        return [pltpu.SemaphoreType.DMA((hops, chunks))] * 2

    def __init__(self, window_ref, rows, chunks, sems):
        self.window, self.total_rows, self.chunks = window_ref, rows, chunks
        self.step = rows // chunks
        self.hops = window_ref.shape[0] // rows - 1
        self.send, self.recv = sems
        self.place = lax.axis_index("dp")
        self.size = lax.axis_size("dp")

    def span(self, block, c):
        first = block * self.total_rows + c * self.step
        return pl.ds(pl.multiple_of(first, self.step), self.step)

    def copy(self, hop, c):
        return dp_copy(
            self.window.at[self.span(self.hops, c)],
            self.window.at[self.span(self.hops - hop, c)],
            self.send.at[hop - 1, c],
            self.recv.at[hop - 1, c],
            self.place + hop,
        )

    def clear(self):
        for hop in range(1, self.hops + 1):

            @pl.when(self.place - hop < 0)
            def _(hop=hop):
                first = (self.hops - hop) * self.total_rows
                shape = (self.total_rows, self.window.shape[1])
                self.window[first : first + self.total_rows, :] = jnp.zeros(shape, jnp.bfloat16)

    def start(self, c):
        for hop in range(1, self.hops + 1):

            @pl.when(self.place + hop < self.size)
            def _(hop=hop):
                self.copy(hop, c).start()

    def drain(self, c):
        for hop in range(1, self.hops + 1):

            @pl.when(self.place + hop < self.size)
            def _(hop=hop):
                self.copy(hop, c).wait_send()

            @pl.when(self.place - hop >= 0)
            def _(hop=hop):
                self.copy(hop, c).wait_recv()


def run_stages(chunks, stages, events=()):
    def body(t, carry):
        for when, event in events:
            pl.when(t == when)(event)
        for lag, stage in stages:
            c = t - LAG * lag

            @pl.when((c >= 0) & (c < chunks))
            def _(stage=stage, c=c):
                stage(c)

        return carry

    lax.fori_loop(0, chunks + LAG * max(lag for lag, _ in stages), body, 0)


def drain_all(chunks, lines):
    def body(c, carry):
        for line in lines:
            line.drain(c)
        return carry

    lax.fori_loop(0, chunks, body, 0)


def add_sums(sums_ref, row, values):
    width = values.shape[1]
    sums_ref[row : row + 1, :width] += jnp.sum(values, axis=0, keepdims=True)


def project_into(line, c, left, weight_ref):
    rows = line.rows(c)
    for cols in column_blocks(weight_ref.shape[1]):
        part = jnp.dot(left, weight_ref[:, cols], preferred_element_type=jnp.float32)
        line.own[rows, cols] = part.astype(jnp.bfloat16)
    line.send(c)


def project_back_into(line, c, left, weight_ref):
    rows = line.rows(c)
    for cols in column_blocks(weight_ref.shape[0]):
        part = dot_rows(left, weight_ref[cols, :])
        line.own[rows, cols] = part.astype(jnp.bfloat16)
    line.send(c)


def head_kernel(hops, *refs):
    ins, outs, scratch = refs[:6], refs[6:14], refs[14:]
    h_ref, small_own, wa_own, wo_own, we_own, wr_own = ins
    small_ref, wa_ref, wo_ref, we_ref, wr_ref, a1_ref, q_ref, window_ref = outs
    pairs = zip((small_own, wa_own, wo_own, we_own, wr_own), outs[:5])
    gathers = [Gather(o, f, scratch[2 * i : 2 * i + 2]) for i, (o, f) in enumerate(pairs)]
    small, wa, wo, we, wr = gathers
    rows, width = q_ref.shape
    chunks = 4
    window = Window(window_ref, rows, chunks, scratch[10:12])
    greet(cube_targets() + window_targets(hops))
    small.begin()
    wa.begin()
    window.clear()
    small.relay()
    small.pass_on()
    small.finish()
    values = small_ref[...].astype(jnp.float32)
    gain, offset = wide_row(values, GAIN_ROW), wide_row(values, OFFSET_ROW)
    bias_q, bias_v = narrow_row(values, width, 0), narrow_row(values, width, 1)
    step = rows // chunks

    def normalize(c, carry):
        at = pl.ds(pl.multiple_of(c * step, step), step)
        a1_ref[at, :] = norm_rows(h_ref[at, :], gain, offset).astype(jnp.bfloat16)
        return carry

    lax.fori_loop(0, chunks, normalize, 0)
    wa.relay()
    we.begin()
    wa.pass_on()
    wr.begin()
    wo.begin()
    wa.finish()

    def project(c, carry):
        at = pl.ds(pl.multiple_of(c * step, step), step)
        a1 = a1_ref[at, :]
        there = window.span(window.hops, c)
        for part in (1, 2):
            cols = slice(part * width, (part + 1) * width)
            value = jnp.dot(a1, wa_ref[:, cols], preferred_element_type=jnp.float32)
            value = value if part == 1 else value + bias_v
            window_ref[there, (part - 1) * width : part * width] = value.astype(jnp.bfloat16)
        window.start(c)
        value = jnp.dot(a1, wa_ref[:, :width], preferred_element_type=jnp.float32)
        q_ref[at, :] = (value + bias_q).astype(jnp.bfloat16)
        return carry

    lax.fori_loop(0, chunks, project, 0)
    for member in (we, wr, wo):
        member.relay()
    for member in (we, wr, wo):
        member.pass_on()
    for c in range(chunks):
        window.drain(c)
    for member in (we, wr, wo):
        member.finish()
    for member in gathers:
        member.drain()


SMALL_ROWS = 32
BRANCH_ROW, UNIT_ROW, GAIN_ROW, OFFSET_ROW, MARK_ROW = 8, 12, 14, 18, 22


def wide_row(values, row):
    owners = range(values.shape[0] // SMALL_ROWS)
    return jnp.concatenate(
        [values[o * SMALL_ROWS + row : o * SMALL_ROWS + row + 1, :] for o in owners], axis=1
    )


def narrow_row(values, width, index):
    owners = range(values.shape[0] // SMALL_ROWS)
    count = width // LANES
    parts = []
    for row in range(index * count, (index + 1) * count):
        total = values[row : row + 1, :]
        for o in owners[1:]:
            total = total + values[o * SMALL_ROWS + row : o * SMALL_ROWS + row + 1, :]
        parts.append(total)
    return jnp.concatenate(parts, axis=1)


def pack_small(small_in, marks, width):
    attend_bias, branch_bias, expand_bias, norm_gain, norm_bias = small_in
    place = lax.axis_index("dp")
    flat = attend_bias.reshape(-1, attend_bias.shape[-1])
    spread = jnp.zeros((flat.shape[0], width), jnp.bfloat16)
    spread = lax.dynamic_update_slice(spread, flat, (0, place * flat.shape[1]))
    rows = [spread.reshape(-1, LANES)]
    rows += [e.reshape(-1, LANES) for e in (branch_bias, expand_bias, norm_gain, norm_bias)]
    rows.append(marks.astype(jnp.bfloat16).reshape(-1, LANES))
    packed = jnp.concatenate(rows, axis=0)
    return jnp.pad(packed, ((0, SMALL_ROWS - packed.shape[0]), (0, 0)))


def unpack_small(small_all, rows, width, reach_back):
    size = small_all.shape[0] // SMALL_ROWS
    grid = small_all.reshape(size, SMALL_ROWS, LANES)
    wide = grid[:, BRANCH_ROW:MARK_ROW].astype(jnp.float32)
    wide = jnp.moveaxis(wide, 0, 1).reshape(MARK_ROW - BRANCH_ROW, size * LANES)
    branches, units = wide[:4].reshape(2, 2, -1), wide[4:6]
    gains, offsets = wide[6:10].reshape(2, 2, -1), wide[10:14].reshape(2, 2, -1)
    attend_b = jnp.sum(grid[:, :BRANCH_ROW].astype(jnp.float32), axis=0).reshape(2, 2, width)
    marks = grid[:, MARK_ROW : MARK_ROW + rows // LANES].astype(jnp.int32).reshape(-1)
    padded = jnp.concatenate([jnp.zeros((reach_back * rows,), jnp.int32), marks])
    begin = lax.axis_index("dp") * rows
    window = lax.dynamic_slice_in_dim(padded, begin, (reach_back + 1) * rows)
    return attend_b, branches, units, gains, offsets, (window[reach_back * rows :, None], window[None])


def first_kernel(chunks, *refs):
    ins, outs, scratch = refs[:10], refs[10:22], refs[22:]
    o_ref, wo_ref, h_ref, vec_ref, we_ref, wr_ref = ins[:6]
    mid_ref, a2_ref, f_ref, u_ref, next_ref, a1_ref, q_ref, window_ref = outs[:8]
    wa_ref = outs[8]
    one = LineTotal(scratch[:7], chunks)
    two = LineTotal(scratch[7:14], chunks)
    pairs = zip(ins[6:], outs[8:])
    gathers = [
        Gather(o, f, scratch[14 + 2 * i : 16 + 2 * i]) for i, (o, f) in enumerate(pairs)
    ]
    rows_all, width = q_ref.shape
    window = Window(window_ref, rows_all, chunks, scratch[22:24])
    greet(one.peers() + cube_targets() + window_targets(window.hops))
    window.clear()

    def start(c):
        project_into(one, c, o_ref[one.rows(c), :], wo_ref)

    def feed(c):
        rows = one.rows(c)
        middle = h_ref[rows, :] + (one.take(c) + vec_ref[0:1, :])
        mid_ref[rows, :] = middle
        a2 = norm_rows(middle, vec_ref[1:2, :], vec_ref[2:3, :]).astype(jnp.bfloat16)
        a2_ref[rows, :] = a2
        for cols in column_blocks(we_ref.shape[1]):
            f = jnp.dot(a2, we_ref[:, cols], preferred_element_type=jnp.float32)
            f = f + vec_ref[3:4, cols]
            f_ref[rows, cols] = f
            u_ref[rows, cols] = gelu_value(f)[0].astype(jnp.bfloat16)
        project_into(two, c, u_ref[rows, :], wr_ref)

    def end(c):
        rows = two.rows(c)
        following = mid_ref[rows, :] + (two.take(c) + vec_ref[4:5, :])
        next_ref[rows, :] = following
        a1 = norm_rows(following, vec_ref[5:6, :], vec_ref[6:7, :]).astype(jnp.bfloat16)
        a1_ref[rows, :] = a1
        there = window.span(window.hops, c)
        for part in (1, 2, 0):
            cols = slice(part * width, (part + 1) * width)
            value = jnp.dot(a1, wa_ref[:, cols], preferred_element_type=jnp.float32)
            value = (value + vec_ref[7:8, cols]).astype(jnp.bfloat16)
            if part == 0:
                q_ref[rows, :] = value
            else:
                window_ref[there, (part - 1) * width : part * width] = value
            if part == 2:
                window.start(c)

    wa, wo, we, wr = gathers
    last = chunks + LAG * 6 - 1
    run_stages(
        chunks,
        [
            (0, start),
            (1, one.join),
            (2, one.finish),
            (3, feed),
            (4, two.join),
            (5, two.finish),
            (6, end),
        ],
        [
            (0, wa.begin),
            (3, wa.relay),
            (3, we.begin),
            (5, wa.pass_on),
            (LAG * 6, wa.finish),
            (LAG * 6, we.relay),
            (LAG * 6, wr.begin),
            (LAG * 6, wo.begin),
            (LAG * 6 + 2, we.pass_on),
            (last - 2, wr.relay),
            (last - 2, wo.relay),
            (last, wr.pass_on),
            (last, wo.pass_on),
        ],
    )
    drain_all(chunks, [one, two, window])
    for member in (wo, we, wr):
        member.finish()
    for member in gathers:
        member.drain()


def turn_kernel(chunks, *refs):
    ins, outs, scratch = refs[:8], refs[8:17], refs[17:]
    o_ref, wo_ref, h_ref, vec_ref, we_ref, wr_ref, e_ref, mid_ref = ins[:7] + (scratch[0],)
    a2_ref, u_ref, eb_ref, dfb_ref, dmid_ref, db_ref, do_ref, out_ref, sums_ref = outs
    wo_back_ref = ins[7]
    one = LineTotal(scratch[1:8], chunks)
    two = LineTotal(scratch[8:15], chunks)
    back = LineTotal(scratch[15:22], chunks)
    sums_ref[...] = jnp.zeros_like(sums_ref)
    greet(one.peers())

    def start(c):
        project_into(one, c, o_ref[one.rows(c), :], wo_ref)

    def feed(c):
        rows = one.rows(c)
        middle = h_ref[rows, :] + (one.take(c) + vec_ref[0:1, :])
        mid_ref[rows, :] = middle
        a2 = norm_rows(middle, vec_ref[1:2, :], vec_ref[2:3, :]).astype(jnp.bfloat16)
        a2_ref[rows, :] = a2
        e = e_ref[rows, :]
        add_sums(sums_ref, 0, e)
        eb = e.astype(jnp.bfloat16)
        eb_ref[rows, :] = eb
        for cols in column_blocks(we_ref.shape[1]):
            f = jnp.dot(a2, we_ref[:, cols], preferred_element_type=jnp.float32)
            f = f + vec_ref[3:4, cols]
            u, bent = gelu_value(f)
            u_ref[rows, cols] = u.astype(jnp.bfloat16)
            df = dot_rows(eb, wr_ref[cols, :]) * gelu_slope(f, bent)
            sums_ref[1:2, cols] += jnp.sum(df, axis=0, keepdims=True)
            dfb_ref[rows, cols] = df.astype(jnp.bfloat16)
        project_back_into(back, c, dfb_ref[rows, :], we_ref)
        project_into(two, c, u_ref[rows, :], wr_ref)

    def turn(c):
        rows = back.rows(c)
        cot = back.take(c)
        part, gain_part = norm_back(mid_ref[rows, :], vec_ref[1:2, :], cot)
        dmid = e_ref[rows, :] + part
        dmid_ref[rows, :] = dmid
        add_sums(sums_ref, 2, gain_part)
        add_sums(sums_ref, 3, cot)
        add_sums(sums_ref, 4, dmid)
        db = dmid.astype(jnp.bfloat16)
        db_ref[rows, :] = db
        do_ref[rows, :] = dot_rows(db, wo_back_ref[...]).astype(jnp.bfloat16)

    def end(c):
        rows = two.rows(c)
        out_ref[rows, :] = mid_ref[rows, :] + (two.take(c) + vec_ref[4:5, :])

    run_stages(
        chunks,
        [
            (0, start),
            (1, one.join),
            (2, one.finish),
            (3, feed),
            (4, back.join),
            (4, two.join),
            (5, back.finish),
            (5, two.finish),
            (6, turn),
            (6, end),
        ],
    )
    drain_all(chunks, [one, two, back])


def cross_kernel(chunks, *refs):
    ins, outs, scratch = refs[:14], refs[14:24], refs[24:]
    dproj_ref, wa_ref, h_ref, dmid_in_ref, vec_ref, f_ref, mid_ref, we_ref, wr_ref, wo_ref = ins[:10]
    eb_ref, dfb_ref, dmid_ref, db_ref, do_ref, sums_ref = outs[:6]
    e_ref = scratch[0]
    one = LineTotal(scratch[1:8], chunks)
    back = LineTotal(scratch[8:15], chunks)
    scatters = scatters_of(ins[10:], outs[6:], scratch[15:])
    sums_ref[...] = jnp.zeros_like(sums_ref)
    greet(one.peers() + cube_targets())

    def start(c):
        project_back_into(one, c, dproj_ref[one.rows(c), :], wa_ref)

    def feed(c):
        rows = one.rows(c)
        cot = one.take(c)
        part, gain_part = norm_back(h_ref[rows, :], vec_ref[0:1, :], cot)
        e = dmid_in_ref[rows, :] + part
        e_ref[rows, :] = e
        add_sums(sums_ref, 0, gain_part)
        add_sums(sums_ref, 1, cot)
        add_sums(sums_ref, 2, e)
        eb = e.astype(jnp.bfloat16)
        eb_ref[rows, :] = eb
        for cols in column_blocks(we_ref.shape[1]):
            f = f_ref[rows, cols]
            unused, bent = gelu_value(f)
            df = dot_rows(eb, wr_ref[cols, :]) * gelu_slope(f, bent)
            sums_ref[3:4, cols] += jnp.sum(df, axis=0, keepdims=True)
            dfb_ref[rows, cols] = df.astype(jnp.bfloat16)
        project_back_into(back, c, dfb_ref[rows, :], we_ref)

    def turn(c):
        rows = back.rows(c)
        cot = back.take(c)
        part, gain_part = norm_back(mid_ref[rows, :], vec_ref[1:2, :], cot)
        dmid = e_ref[rows, :] + part
        dmid_ref[rows, :] = dmid
        add_sums(sums_ref, 4, gain_part)
        add_sums(sums_ref, 5, cot)
        add_sums(sums_ref, 6, dmid)
        db = dmid.astype(jnp.bfloat16)
        db_ref[rows, :] = db
        do_ref[rows, :] = dot_rows(db, wo_ref[...]).astype(jnp.bfloat16)

    run_stages(
        chunks,
        [
            (0, start),
            (1, one.join),
            (2, one.finish),
            (3, feed),
            (4, back.join),
            (5, back.finish),
            (6, turn),
        ],
        scatter_events(scatters, chunks + LAG * 6 - 1, 1, 2, 3, 3),
    )
    drain_all(chunks, [one, back])
    for member in scatters:
        member.drain()


def scatter_events(scatters, last, apart, wait_one, wait_two, wait_three):
    events = []
    for i, member in enumerate(scatters):
        at = i * apart
        events.append((min(at, last), member.begin))
        events.append((min(at + wait_one, last), member.spread))
        events.append((min(at + wait_one + wait_two, last), member.narrow))
        events.append((min(at + wait_one + wait_two + wait_three, last), member.close))
    return events


def last_kernel(chunks, *refs):
    ins, outs, scratch = refs[:10], refs[10:18], refs[18:]
    dproj_ref, wa_ref, h_ref, dmid_ref, vec_ref = ins[:5]
    grad_ref, late_ref, sums_ref = outs[0], outs[1], outs[2]
    one = LineTotal(scratch[:7], chunks)
    parts_ref, seen_ref, part_send, part_recv = scratch[7:11]
    scatters = scatters_of(ins[5:], outs[3:], scratch[11:])
    place, size = lax.axis_index("dp"), lax.axis_size("dp")
    sums_ref[...] = jnp.zeros_like(sums_ref)
    everyone = [(place >= 0, "dp", lax.rem(place + j, size)) for j in range(1, size)]
    greet(one.peers() + everyone)

    def start(c):
        project_back_into(one, c, dproj_ref[one.rows(c), :], wa_ref)

    def end(c):
        rows = one.rows(c)
        cot = one.take(c)
        part, gain_part = norm_back(h_ref[rows, :], vec_ref[0:1, :], cot)
        grad_ref[rows, :] = dmid_ref[rows, :] + part
        add_sums(sums_ref, 0, gain_part)
        add_sums(sums_ref, 1, cot)

    run_stages(
        chunks,
        [(0, start), (1, one.join), (2, one.finish), (3, end)],
        scatter_events(scatters, chunks + LAG * 3 - 1, 1, 1, 3, 3),
    )

    def part_copy(j):
        target = lax.rem(place + j, size)
        return dp_copy(
            parts_ref.at[target], seen_ref.at[j], part_send.at[j], part_recv.at[j], target
        )

    for owner in range(size):
        parts_ref[owner] = sums_ref[:, owner * LANES : (owner + 1) * LANES]
    for j in range(1, size):
        part_copy(j).start()
    drain_all(chunks, [one])
    total = parts_ref[place]
    for j in range(1, size):
        part_copy(j).wait_recv()
        total = total + seen_ref[j]
    late_ref[...] = total
    for j in range(1, size):
        part_copy(j).wait_send()
    for member in scatters:
        member.drain()


CHUNKS = 8
LAG = 1
MEGA = 1024 * 1024


def line_call(kernel, name, number, out_shapes, extra, lines, span_us, args, more=()):
    rows, model = extra
    scratch = []
    if lines[0]:
        scratch.append(pltpu.VMEM((rows, model), jnp.float32))
    for _ in range(lines[1]):
        scratch += LineTotal.scratch(rows, model, CHUNKS)
    scratch += list(more)
    return pl.pallas_call(
        functools.partial(kernel, CHUNKS),
        out_shape=tuple(jax.ShapeDtypeStruct(shape, kind) for shape, kind in out_shapes),
        in_specs=in_vmem(len(args)),
        out_specs=tuple(in_vmem(len(out_shapes))),
        scratch_shapes=scratch,
        cost_estimate=pl.CostEstimate(
            flops=int(span_us * 1e9), bytes_accessed=0, transcendentals=0
        ),
        compiler_params=pltpu.CompilerParams(
            collective_id=number, has_side_effects=True, vmem_limit_bytes=56 * MEGA
        ),
        name=name,
    )(*args)


def stack_rows(model, rows):
    rows = [jnp.pad(r, (0, model - r.shape[0])) for r in rows]
    rows += [jnp.zeros((model,), jnp.float32)] * (-len(rows) % 8)
    return jnp.stack(rows)


def window_of(kv_now, reach_back):
    kv_list = [passed_along(kv_now, "dp", hop) for hop in range(reach_back, 0, -1)]
    return jnp.concatenate(kv_list + [kv_now], axis=0)


def attention_cots(queries, window_kv, log_totals, context_cot, marks, reach_back):
    rows, width = queries.shape
    query_cot, kv_own, kv_back = attend_backward(
        queries, window_kv, log_totals, context_cot, marks[0], marks[1]
    )
    for hop in range(1, reach_back + 1):
        begin = (reach_back - hop) * rows
        kv_own = kv_own + passed_along(kv_back[begin : begin + rows], "dp", -hop).astype(
            jnp.float32
        )
    bias_grad = jnp.stack([jnp.sum(query_cot, axis=0), jnp.sum(kv_own[:, width:], axis=0)])
    rounded = jnp.concatenate(
        [query_cot.astype(jnp.bfloat16), kv_own.astype(jnp.bfloat16)], axis=1
    )
    return rounded, bias_grad


def weight_grad(left, right):
    return dot_tokens(left, right).astype(jnp.bfloat16)


def tied(*values):
    return lax.optimization_barrier(values)


def head_call(hidden_in, small, weights, width, hops):
    rows, model = hidden_in.shape
    size = lax.axis_size("dp")
    fulls = [jax.ShapeDtypeStruct((size * w.shape[0], w.shape[1]), w.dtype) for w in (small, *weights)]
    outs = fulls + [
        jax.ShapeDtypeStruct((rows, model), jnp.bfloat16),
        jax.ShapeDtypeStruct((rows, width), jnp.bfloat16),
        jax.ShapeDtypeStruct(((hops + 1) * rows, 2 * width), jnp.bfloat16),
    ]
    return pl.pallas_call(
        functools.partial(head_kernel, hops),
        out_shape=tuple(outs),
        in_specs=in_vmem(2 + len(weights)),
        out_specs=tuple(in_vmem(len(outs))),
        scratch_shapes=Gather.scratch() * 5 + Window.scratch(hops, 4),
        compiler_params=pltpu.CompilerParams(
            collective_id=5, has_side_effects=True, vmem_limit_bytes=40 * MEGA
        ),
        name="head",
    )(hidden_in, small, *weights)


def pair_layers(hidden_in, out_grad, shards, small_in, doc_marks, reach_back, model_parts):
    share, unit_share, size, part = model_parts
    bf16, f32 = jnp.bfloat16, jnp.float32
    rows, model = hidden_in.shape
    attend_weight, output_weight, expand_weight, reduce_weight = shards
    width, units = attend_weight.shape[3], expand_weight.shape[2]
    extra = (rows, model)

    def shards_of(layer):
        return (
            attend_weight[layer].reshape(part, 3 * width),
            output_weight[layer],
            expand_weight[layer],
            reduce_weight[layer],
        )

    def proj_bias(bias):
        return jnp.concatenate([bias[0], jnp.zeros_like(bias[0]), bias[1]])

    small_all, aw0, ow0, ew0, rw0, a1_0, q_0, window_0 = head_call(
        hidden_in, pack_small(small_in, doc_marks, width), shards_of(0), width, reach_back
    )
    attend_b, (br0, br1), (eb0, eb1), (g0, g1), (c0, c1), marks = unpack_small(
        small_all, rows, width, reach_back
    )
    o_0, lse_0 = attend_forward(q_0, window_0, marks[0], marks[1])

    vec = stack_rows(
        model, [br0[0], g0[1], c0[1], eb0, br0[1], g1[0], c1[0], proj_bias(attend_b[1])]
    )
    mid_0, a2_0, f_0, u_0, h_1, a1_1, q_1, window_1, aw1, ow1, ew1, rw1 = line_call(
        first_kernel,
        "first_tail",
        1,
        [
            ((rows, model), f32),
            ((rows, model), bf16),
            ((rows, units), f32),
            ((rows, units), bf16),
            ((rows, model), f32),
            ((rows, model), bf16),
            ((rows, width), bf16),
            (((reach_back + 1) * rows, 2 * width), bf16),
            ((model, 3 * width), bf16),
            ((width, model), bf16),
            ((model, units), bf16),
            ((units, model), bf16),
        ],
        extra,
        (0, 2),
        50,
        (o_0, ow0, hidden_in, vec, ew0, rw0, *shards_of(1)),
        Gather.scratch() * 4 + Window.scratch(reach_back, CHUNKS),
    )
    o_1, lse_1 = attend_forward(q_1, window_1, marks[0], marks[1])

    vec = stack_rows(model, [br1[0], g1[1], c1[1], eb1, br1[1]])
    a2_1, u_1, eb_1, dfb_1, dmid_1, db_1, do_1, hidden_out, sums_1 = line_call(
        turn_kernel,
        "turn_tail",
        2,
        [
            ((rows, model), bf16),
            ((rows, units), bf16),
            ((rows, model), bf16),
            ((rows, units), bf16),
            ((rows, model), f32),
            ((rows, model), bf16),
            ((rows, width), bf16),
            ((rows, model), f32),
            ((8, model), f32),
        ],
        extra,
        (1, 3),
        70,
        (o_1, ow1, h_1, vec, ew1, rw1, out_grad, ow1),
    )
    expand_1 = weight_grad(a2_1, dfb_1)
    reduce_1 = weight_grad(u_1, eb_1)
    output_1 = weight_grad(o_1, db_1)
    dproj_1, attend_bias_1 = attention_cots(q_1, window_1, lse_1, do_1, marks, reach_back)
    attend_1 = weight_grad(a1_1, dproj_1)
    grads_1 = (expand_1, reduce_1, attend_1, output_1)
    owned = [((g.shape[0] // size, g.shape[1]), f32) for g in grads_1]

    def scatter_scratch(pieces):
        return sum((Scatter.scratch(*shape) for shape, kind in pieces), [])

    vec = stack_rows(model, [g1[0], g0[1]])
    eb_0, dfb_0, dmid_0, db_0, do_0, sums_0, *sums_of_1 = line_call(
        cross_kernel,
        "cross_tail",
        3,
        [
            ((rows, model), bf16),
            ((rows, units), bf16),
            ((rows, model), f32),
            ((rows, model), bf16),
            ((rows, width), bf16),
            ((8, model), f32),
            *owned,
        ],
        extra,
        (1, 2),
        60,
        (dproj_1, aw1, h_1, dmid_1, vec, f_0, mid_0, ew0, rw0, ow0, *grads_1),
        scatter_scratch(owned),
    )
    expand_0 = weight_grad(a2_0, dfb_0)
    reduce_0 = weight_grad(u_0, eb_0)
    output_0 = weight_grad(o_0, db_0)
    dproj_0, attend_bias_0 = attention_cots(q_0, window_0, lse_0, do_0, marks, reach_back)
    attend_0 = weight_grad(a1_0, dproj_0)
    zero = jnp.zeros((model,), f32)
    wide = [
        sums_0[6], sums_0[2], sums_1[4], sums_1[0],
        sums_0[3], sums_1[1],
        zero, sums_0[4], sums_0[0], sums_1[2],
        zero, sums_0[5], sums_0[1], sums_1[3],
    ]
    wide = jnp.stack(wide).reshape(len(wide), size, LANES)
    narrow = jnp.concatenate([attend_bias_0, attend_bias_1]).reshape(4, size, width // size)
    narrow = jnp.moveaxis(narrow, 1, 0).reshape(size, 1, LANES)
    small = jnp.concatenate([narrow, jnp.moveaxis(wide, 1, 0)], axis=1).astype(bf16)
    small = jnp.pad(small, ((0, 0), (0, SMALL_ROWS - small.shape[1]), (0, 0)))
    grads_0 = (expand_0, reduce_0, attend_0, output_0, small.reshape(-1, LANES))
    owned = [((g.shape[0] // size, g.shape[1]), f32) for g in grads_0]

    vec = stack_rows(model, [g0[0]])
    in_grad, late, unused, *sums_of_0 = line_call(
        last_kernel,
        "last_tail",
        4,
        [((rows, model), f32), ((8, LANES), f32), ((8, model), f32), *owned],
        extra,
        (0, 1),
        30,
        (dproj_0, aw0, hidden_in, dmid_0, vec, *grads_0),
        [
            pltpu.VMEM((size, 8, LANES), f32),
            pltpu.VMEM((size, 8, LANES), f32),
            pltpu.SemaphoreType.DMA((size,)),
            pltpu.SemaphoreType.DMA((size,)),
            *scatter_scratch(owned),
        ],
    )
    small = sums_of_0[4]
    expand, reduced, attend, output = [jnp.stack(pair) for pair in zip(sums_of_0[:4], sums_of_1)]
    pieces = [small[1 + i : 1 + i + n] for i, n in ((0, 4), (4, 2), (6, 4), (10, 4))]
    branch, units_grad, gain, offset = pieces
    return (
        hidden_out,
        in_grad,
        attend.reshape(2, part, 3, width),
        small[0].reshape(2, 2, width // size),
        output,
        branch.reshape(2, 2, LANES),
        expand,
        units_grad,
        reduced,
        jnp.concatenate([late[0:1], gain[1:]]).reshape(2, 2, LANES),
        jnp.concatenate([late[1:2], offset[1:]]).reshape(2, 2, LANES),
    )


def layer_by_layer(hidden_in, out_grad, params, marks, reach_back, model_parts):
    share, unit_share, size, part = model_parts
    model = hidden_in.shape[1]
    saved = []
    current = hidden_in
    for layer in range(len(params)):
        current, kept_state = forward_layer(current, params[layer], marks, reach_back)
        saved.append(kept_state)
    grad_now = out_grad
    hidden_list = [None] * len(params)
    attend_list = [None] * len(params)
    small_list = [None] * len(params)
    for layer in reversed(range(len(params))):
        grad_now, expand_grad, reduce_grad, attend_grad, output_grad, small = backward_layer(
            grad_now, params[layer], saved[layer], marks, reach_back
        )
        hidden_list[layer] = scattered(
            jnp.concatenate([expand_grad, pack_output(reduce_grad, model, unit_share)], axis=1)
        )
        small_list[layer] = small
        blocks = [attend_grad, pack_output(output_grad, model, share)]
        if layer == 0:
            stacked = [jnp.stack([entry[i] for entry in small_list]) for i in range(len(small))]
            flat_rows = split_owned(stacked, None, size).astype(jnp.bfloat16)
            count = flat_rows.shape[1]
            room = part * LANES * (-(-count // (part * LANES)))
            padded = jnp.pad(flat_rows, ((0, 0), (0, room - count)))
            blocks.append(padded.reshape(size * part, room // part))
        packed = jnp.concatenate(blocks, axis=1)
        if layer > 0:
            grad_now, packed = lax.optimization_barrier((grad_now, packed))
        attend_list[layer] = scattered(packed)
    return current, grad_now, hidden_list, attend_list


def local(
    hidden_in,
    doc_ids,
    attend_weight,
    attend_bias,
    output_weight,
    branch_bias,
    expand_weight,
    expand_bias,
    reduce_weight,
    norm_gain,
    norm_bias,
    out_grad,
):
    size = lax.axis_size("dp")
    layer_count, part, three, width = attend_weight.shape
    tok_rows, model = hidden_in.shape
    share = output_weight.shape[1]
    unit_share = reduce_weight.shape[1]
    hidden_units = expand_weight.shape[2]
    reach_back = (CTX + tok_rows - 2) // tok_rows
    own_row = doc_ids + 1
    small_in = (attend_bias, branch_bias, expand_bias, norm_gain, norm_bias)
    on_cube = size == 8 and lax.axis_size("tensor") == 4 and layer_count == 2
    if on_cube and part == unit_share == LANES and tok_rows == 4 * LANES and width == 2 * LANES:
        return pair_layers(
            hidden_in,
            out_grad,
            (attend_weight, output_weight, expand_weight, reduce_weight),
            small_in,
            own_row,
            reach_back,
            (share, unit_share, size, part),
        )
    else:
        mark_list = [passed_along(own_row, "dp", hop) for hop in range(reach_back, 0, -1)]
        marks = (own_row[:, None], jnp.concatenate(mark_list + [own_row])[None, :])
        flat = jnp.concatenate([entry.reshape(-1) for entry in small_in])
        flat_all = lax.all_gather(flat[None], "dp", axis=0, tiled=True)
        small_full = []
        at = 0
        for entry in small_in:
            piece = flat_all[:, at : at + entry.size].reshape((size,) + entry.shape)
            at += entry.size
            piece = jnp.moveaxis(piece, 0, -2)
            small_full.append(
                piece.reshape(entry.shape[:-1] + (size * entry.shape[-1],)).astype(jnp.float32)
            )
        attend_b, branches, expand_b, gains, offsets = small_full

        params = []
        for layer in range(layer_count):
            first = lax.all_gather(
                jnp.concatenate(
                    [
                        attend_weight[layer].reshape(part, three * width),
                        pack_output(output_weight[layer], model, share),
                    ],
                    axis=1,
                ),
                "dp",
                axis=0,
                tiled=True,
            )
            second = lax.all_gather(
                jnp.concatenate(
                    [expand_weight[layer], pack_output(reduce_weight[layer], model, unit_share)],
                    axis=1,
                ),
                "dp",
                axis=0,
                tiled=True,
            )
            params.append(
                (
                    first[:, : three * width],
                    attend_b[layer],
                    unpack_output(first[:, three * width :], model, share),
                    branches[layer],
                    second[:, :hidden_units],
                    expand_b[layer],
                    unpack_output(second[:, hidden_units:], model, unit_share),
                    gains[layer],
                    offsets[layer],
                )
            )
        current, grad_now, hidden_list, attend_list = layer_by_layer(
            hidden_in, out_grad, params, marks, reach_back, (share, unit_share, size, part)
        )
    hidden_out = [entry.astype(jnp.float32) for entry in hidden_list]
    attend_out = [entry.astype(jnp.float32) for entry in attend_list]
    fold = three * width
    slab = model * share // part
    tail = attend_out[0][:, fold + slab :].reshape(-1)
    small_out = []
    at = 0
    for entry in small_in:
        small_out.append(tail[at : at + entry.size].reshape(entry.shape))
        at += entry.size
    attend_bgrad, branch_bgrad, expand_bgrad, gain_grad, offset_grad = small_out
    return (
        current,
        grad_now,
        jnp.stack([entry[:, :fold].reshape(part, three, width) for entry in attend_out]),
        attend_bgrad,
        jnp.stack([unpack_output(entry[:, fold : fold + slab], model, share) for entry in attend_out]),
        branch_bgrad,
        jnp.stack([entry[:, :hidden_units] for entry in hidden_out]),
        expand_bgrad,
        jnp.stack(
            [unpack_output(entry[:, hidden_units:], model, unit_share) for entry in hidden_out]
        ),
        gain_grad,
        offset_grad,
    )


def solution(mesh):
    return jax.shard_map(
        local,
        mesh=mesh,
        in_specs=(
            P("dp", None),
            P("dp"),
            P(None, "dp", None, "tensor"),
            P(None, None, ("tensor", "dp")),
            P(None, ("tensor", "dp"), None),
            P(None, None, "dp"),
            P(None, "dp", "tensor"),
            P(None, ("tensor", "dp")),
            P(None, ("tensor", "dp"), None),
            P(None, None, "dp"),
            P(None, None, "dp"),
            P("dp", None),
        ),
        out_specs=(
            P("dp", None),
            P("dp", None),
            P(None, "dp", None, "tensor"),
            P(None, None, ("tensor", "dp")),
            P(None, ("tensor", "dp"), None),
            P(None, None, "dp"),
            P(None, "dp", "tensor"),
            P(None, ("tensor", "dp")),
            P(None, ("tensor", "dp"), None),
            P(None, None, "dp"),
            P(None, None, "dp"),
        ),
        check_vma=False,
    )
```

```python
import functools
import math

import jax
import jax.numpy as jnp
from jax import lax
from jax.experimental import pallas as pl
from jax.experimental.pallas import tpu as pltpu
from jax.sharding import PartitionSpec as P

HEAD_DIM = 64
CTX = 1024
LANES = 128
ROW_TILE = 256


def passed_along(block, axis, distance):
    devices = range(lax.axis_size(axis))
    route = [(i - distance, i) for i in devices if i - distance in devices]
    return lax.ppermute(block, axis, route)


def contract(pattern, left_side, right_side):
    return jnp.einsum(pattern, left_side, right_side, preferred_element_type=jnp.float32)


def layer_norm(values, gain_row, offset_row):
    center = values - jnp.mean(values, axis=-1, keepdims=True)
    spread = jnp.mean(center * center, axis=-1, keepdims=True)
    return center * lax.rsqrt(spread + 1e-05) * gain_row + offset_row


def gelu_tanh(values):
    return (
        0.5
        * values
        * (1.0 + jnp.tanh(0.7978845608028654 * (values + 0.044715 * values * values * values)))
    )


def dot_rows(left_side, right_side):
    return lax.dot_general(
        left_side, right_side, (((1,), (1,)), ((), ())), preferred_element_type=jnp.float32
    )


def dot_tokens(left_side, right_side):
    return lax.dot_general(
        left_side, right_side, (((0,), (0,)), ((), ())), preferred_element_type=jnp.float32
    )


def row_tiles(rows, window_rows):
    tile = min(ROW_TILE, rows)
    back = window_rows - rows
    for start in range(0, rows, tile):
        low = max(0, (back + start - CTX + 1) // LANES * LANES)
        yield start, tile, low, back + start + tile


def tile_mask(own_ref, window_ref, start, tile, low, high, back):
    own = own_ref[start : start + tile, :]
    window = window_ref[:, low:high]
    row = lax.broadcasted_iota(jnp.int32, (tile, high - low), 0) + (start + back)
    col = lax.broadcasted_iota(jnp.int32, (tile, high - low), 1) + low
    return (window == own) & (col <= row)


def head_parts(width):
    group = min(LANES, width)
    for base in range(0, width, group):
        for inner in range(0, group, HEAD_DIM):
            yield base, group, inner


def pick(block, inner):
    lane = lax.broadcasted_iota(jnp.int32, block.shape, 1)
    return jnp.where((lane >= inner) & (lane < inner + HEAD_DIM), block, jnp.zeros_like(block))


def forward_kernel(q_ref, kv_ref, own_ref, window_ref, o_ref, lse_ref):
    rows, width = q_ref.shape
    window_rows = kv_ref.shape[0]
    back = window_rows - rows
    factor = 1.0 / math.sqrt(HEAD_DIM)
    for start, tile, low, high in row_tiles(rows, window_rows):
        allowed = tile_mask(own_ref, window_ref, start, tile, low, high, back)
        held = None
        logs = []
        for base, group, inner in head_parts(width):
            queries = pick(q_ref[start : start + tile, base : base + group], inner)
            keys = kv_ref[low:high, base : base + group]
            values = kv_ref[low:high, width + base : width + base + group]
            unnormed = jnp.where(allowed, jnp.exp(dot_rows(queries, keys) * factor), 0.0)
            totals = jnp.sum(unnormed, axis=-1, keepdims=True)
            probabilities = (unnormed * (1.0 / totals)).astype(jnp.bfloat16)
            context = pick(
                jnp.dot(probabilities, values, preferred_element_type=jnp.float32), inner
            )
            held = context if inner == 0 else held + context
            logs.append(jnp.log(totals))
            if inner + HEAD_DIM == group:
                o_ref[start : start + tile, base : base + group] = held.astype(jnp.bfloat16)
        for index, entry in enumerate(logs):
            lse_ref[start : start + tile, index : index + 1] = entry


def backward_kernel(
    q_ref, kv_ref, lse_ref, cot_ref, own_ref, window_ref, dq_ref, own_out, back_out, acc
):
    rows, width = q_ref.shape
    window_rows = kv_ref.shape[0]
    back = window_rows - rows
    factor = 1.0 / math.sqrt(HEAD_DIM)
    acc[...] = jnp.zeros_like(acc)
    for start, tile, low, high in row_tiles(rows, window_rows):
        allowed = tile_mask(own_ref, window_ref, start, tile, low, high, back)
        held = None
        for index, (base, group, inner) in enumerate(head_parts(width)):
            queries = pick(q_ref[start : start + tile, base : base + group], inner)
            cots = pick(cot_ref[start : start + tile, base : base + group], inner)
            keys = kv_ref[low:high, base : base + group]
            values = kv_ref[low:high, width + base : width + base + group]
            logs = lse_ref[start : start + tile, index : index + 1]
            scores = dot_rows(queries, keys) * factor
            probabilities = jnp.where(allowed, jnp.exp(scores - logs), 0.0)
            rounded = probabilities.astype(jnp.bfloat16)
            acc[low:high, width + base : width + base + group] += dot_tokens(rounded, cots)
            prob_cot = dot_rows(cots, values)
            inner_sum = jnp.sum(probabilities * prob_cot, axis=-1, keepdims=True)
            score_cot = (probabilities * (prob_cot - inner_sum) * factor).astype(jnp.bfloat16)
            acc[low:high, base : base + group] += dot_tokens(score_cot, queries)
            part = pick(jnp.dot(score_cot, keys, preferred_element_type=jnp.float32), inner)
            held = part if inner == 0 else held + part
            if inner + HEAD_DIM == group:
                dq_ref[start : start + tile, base : base + group] = held
    own_out[...] = acc[back:, :]
    back_out[...] = acc[:back, :].astype(jnp.bfloat16)


def in_vmem(count):
    return [pl.BlockSpec(memory_space=pltpu.VMEM)] * count


def attend_forward(queries, window_kv, own_marks, window_marks):
    rows, width = queries.shape
    return pl.pallas_call(
        forward_kernel,
        out_shape=(
            jax.ShapeDtypeStruct((rows, width), jnp.bfloat16),
            jax.ShapeDtypeStruct((rows, width // HEAD_DIM), jnp.float32),
        ),
        in_specs=in_vmem(4),
        out_specs=tuple(in_vmem(2)),
        compiler_params=pltpu.CompilerParams(vmem_limit_bytes=40 * 1024 * 1024),
        name="attend_forward",
    )(queries, window_kv, own_marks, window_marks)


def attend_backward(queries, window_kv, log_totals, out_cot, own_marks, window_marks):
    rows, width = queries.shape
    window_rows = window_kv.shape[0]
    return pl.pallas_call(
        backward_kernel,
        out_shape=(
            jax.ShapeDtypeStruct((rows, width), jnp.float32),
            jax.ShapeDtypeStruct((rows, 2 * width), jnp.float32),
            jax.ShapeDtypeStruct((window_rows - rows, 2 * width), jnp.bfloat16),
        ),
        in_specs=in_vmem(6),
        out_specs=tuple(in_vmem(3)),
        scratch_shapes=[pltpu.VMEM((window_rows, 2 * width), jnp.float32)],
        compiler_params=pltpu.CompilerParams(vmem_limit_bytes=48 * 1024 * 1024),
        name="attend_backward",
    )(queries, window_kv, log_totals, out_cot, own_marks, window_marks)


def line_kernel(chunks, x_ref, o_ref, from_near, from_mid, pair, total, near_send, mid_send, near_recv, mid_recv):
    place = lax.axis_index("tensor")
    near = place + 1 - 2 * lax.rem(place, 2)
    across = 3 - place
    is_end = (place == 0) | (place == 3)
    is_mid = (place == 1) | (place == 2)
    step = x_ref.shape[0] // chunks
    barrier = pltpu.get_barrier_semaphore()

    def part(ref, c):
        return ref.at[pl.ds(c * step, step)]

    def to_near(src, c):
        return pltpu.make_async_remote_copy(
            src_ref=part(src, c),
            dst_ref=part(from_near, c),
            send_sem=near_send.at[c],
            recv_sem=near_recv.at[c],
            device_id={"tensor": near},
            device_id_type=pl.DeviceIdType.MESH,
        )

    def to_mid(c):
        return pltpu.make_async_remote_copy(
            src_ref=part(pair, c),
            dst_ref=part(from_mid, c),
            send_sem=mid_send.at[c],
            recv_sem=mid_recv.at[c],
            device_id={"tensor": across},
            device_id_type=pl.DeviceIdType.MESH,
        )

    def added(left, right, c):
        rows = pl.ds(c * step, step)
        both = left[rows, :].astype(jnp.float32) + right[rows, :].astype(jnp.float32)
        return both.astype(jnp.bfloat16)

    pl.semaphore_signal(
        barrier, inc=1, device_id={"tensor": near}, device_id_type=pl.DeviceIdType.MESH
    )

    @pl.when(is_end)
    def _():
        pl.semaphore_wait(barrier, 1)
        for c in range(chunks):
            to_near(x_ref, c).start()
        for c in range(chunks):
            to_near(x_ref, c).wait_recv()
            rows = pl.ds(c * step, step)
            o_ref[rows, :] = from_near[rows, :]
        for c in range(chunks):
            to_near(x_ref, c).wait_send()

    @pl.when(is_mid)
    def _():
        pl.semaphore_signal(
            barrier, inc=1, device_id={"tensor": across}, device_id_type=pl.DeviceIdType.MESH
        )
        pl.semaphore_wait(barrier, 2)
        lag = 2
        for c in range(chunks + lag):
            if c < chunks:
                to_near(total, c).wait_recv()
                pair[pl.ds(c * step, step), :] = added(x_ref, from_near, c)
                to_mid(c).start()
            done = c - lag
            if done >= 0:
                to_mid(done).wait_recv()
                result = added(pair, from_mid, done)
                total[pl.ds(done * step, step), :] = result
                to_near(total, done).start()
                o_ref[pl.ds(done * step, step), :] = result
        for c in range(chunks):
            to_mid(c).wait_send()
            to_near(total, c).wait_send()


def tensor_total(partial_value):
    rounded = partial_value.astype(jnp.bfloat16)
    rows = rounded.shape[0]
    if lax.axis_size("tensor") != 4 or rows % 128:
        return lax.psum(rounded, "tensor").astype(jnp.float32)
    chunks = 8
    block = pltpu.VMEM(rounded.shape, jnp.bfloat16)
    summed = pl.pallas_call(
        functools.partial(line_kernel, chunks),
        out_shape=jax.ShapeDtypeStruct(rounded.shape, jnp.bfloat16),
        in_specs=in_vmem(1),
        out_specs=in_vmem(1)[0],
        scratch_shapes=[block] * 4 + [pltpu.SemaphoreType.DMA((chunks,))] * 4,
        compiler_params=pltpu.CompilerParams(
            collective_id=0, has_side_effects=True, vmem_limit_bytes=24 * 1024 * 1024
        ),
        name="line_total",
    )(rounded)
    return summed.astype(jnp.float32)


def forward_layer(hidden, params, marks, reach_back):
    attend_w, attend_b, output_w, branches, expand_w, expand_b, reduce_w, gains, offsets = params
    width = output_w.shape[0]
    own_marks, window_marks = marks
    normed_one = layer_norm(hidden, gains[0], offsets[0]).astype(jnp.bfloat16)
    projected = jnp.dot(normed_one, attend_w, preferred_element_type=jnp.float32)
    queries = (projected[:, :width] + attend_b[0]).astype(jnp.bfloat16)
    kv_bias = jnp.concatenate([jnp.zeros_like(attend_b[1]), attend_b[1]])
    kv_now = (projected[:, width:] + kv_bias).astype(jnp.bfloat16)
    kv_list = [passed_along(kv_now, "dp", hop) for hop in range(reach_back, 0, -1)]
    window_kv = jnp.concatenate(kv_list + [kv_now], axis=0)
    context, log_totals = attend_forward(queries, window_kv, own_marks, window_marks)
    attended = tensor_total(jnp.dot(context, output_w, preferred_element_type=jnp.float32))
    middle = hidden + (attended + branches[0])
    normed_two = layer_norm(middle, gains[1], offsets[1]).astype(jnp.bfloat16)
    pre_act = jnp.dot(normed_two, expand_w, preferred_element_type=jnp.float32) + expand_b
    activated = gelu_tanh(pre_act).astype(jnp.bfloat16)
    reduced = tensor_total(jnp.dot(activated, reduce_w, preferred_element_type=jnp.float32))
    output = middle + (reduced + branches[1])
    kept_state = (
        hidden,
        normed_one,
        queries,
        window_kv,
        context,
        log_totals,
        middle,
        normed_two,
        pre_act,
        activated,
    )
    return (output, kept_state)


def backward_layer(grad_out, params, kept_state, marks, reach_back):
    attend_w, attend_b, output_w, branches, expand_w, expand_b, reduce_w, gains, offsets = params
    (
        hidden,
        normed_one,
        queries,
        window_kv,
        context,
        log_totals,
        middle,
        normed_two,
        pre_act,
        activated,
    ) = kept_state
    own_marks, window_marks = marks
    rows = hidden.shape[0]
    width = output_w.shape[0]
    bias_two = jnp.sum(grad_out, axis=0)
    grad_rounded = grad_out.astype(jnp.bfloat16)
    act_cot = contract("td,fd->tf", grad_rounded, reduce_w)
    unused, gelu_pull = jax.vjp(gelu_tanh, pre_act)
    pre_cot = gelu_pull(act_cot)[0]
    expand_bias_grad = jnp.sum(pre_cot, axis=0)
    pre_rounded = pre_cot.astype(jnp.bfloat16)
    normed_cot = tensor_total(contract("tf,df->td", pre_rounded, expand_w))
    reduce_grad = contract("tf,td->fd", activated, grad_rounded).astype(jnp.bfloat16)
    expand_grad = contract("td,tf->df", normed_two, pre_rounded).astype(jnp.bfloat16)
    unused, norm_pull = jax.vjp(layer_norm, middle, gains[1], offsets[1])
    mid_part, gain_two, offset_two = norm_pull(normed_cot)
    mid_cot = grad_out + mid_part
    bias_one = jnp.sum(mid_cot, axis=0)
    mid_rounded = mid_cot.astype(jnp.bfloat16)
    output_grad = contract("tk,td->kd", context, mid_rounded).astype(jnp.bfloat16)
    context_cot = contract("td,kd->tk", mid_rounded, output_w).astype(jnp.bfloat16)
    context_cot, expand_grad, reduce_grad = lax.optimization_barrier(
        (context_cot, expand_grad, reduce_grad)
    )
    query_cot, kv_own, kv_back = attend_backward(
        queries, window_kv, log_totals, context_cot, own_marks, window_marks
    )
    for hop in range(1, reach_back + 1):
        begin = (reach_back - hop) * rows
        kv_own = kv_own + passed_along(kv_back[begin : begin + rows], "dp", -hop).astype(
            jnp.float32
        )
    attend_bias_grad = jnp.stack([jnp.sum(query_cot, axis=0), jnp.sum(kv_own[:, width:], axis=0)])
    proj_rounded = jnp.concatenate(
        [query_cot.astype(jnp.bfloat16), kv_own.astype(jnp.bfloat16)], axis=1
    )
    normed_cot_one = tensor_total(contract("tc,dc->td", proj_rounded, attend_w))
    attend_grad = contract("td,tc->dc", normed_one, proj_rounded).astype(jnp.bfloat16)
    unused, first_pull = jax.vjp(layer_norm, hidden, gains[0], offsets[0])
    hid_part, gain_one, offset_one = first_pull(normed_cot_one)
    in_cot = mid_cot + hid_part
    small = (
        attend_bias_grad,
        jnp.stack([bias_one, bias_two]),
        expand_bias_grad,
        jnp.stack([gain_one, gain_two]),
        jnp.stack([offset_one, offset_two]),
    )
    return (in_cot, expand_grad, reduce_grad, attend_grad, output_grad, small)


def scattered(block):
    return lax.psum_scatter(block, "dp", scatter_dimension=0, tiled=True)


def pack_output(block, model, share):
    part = model // lax.axis_size("dp")
    slabs = part // share
    owners = block.shape[0] // share
    return (
        block.reshape(owners, share, slabs, model // slabs)
        .transpose(0, 2, 1, 3)
        .reshape(owners * part, model // slabs)
    )


def unpack_output(block, model, share):
    part = model // lax.axis_size("dp")
    slabs = part // share
    owners = block.shape[0] // part
    return (
        block.reshape(owners, slabs, share, model // slabs)
        .transpose(0, 2, 1, 3)
        .reshape(owners * share, model)
    )


def split_owned(pieces, sizes, size):
    rows = [
        jnp.moveaxis(p.reshape(p.shape[:-1] + (size, p.shape[-1] // size)), -2, 0).reshape(size, -1)
        for p in pieces
    ]
    return jnp.concatenate(rows, axis=1)


GELU_SCALE = 0.7978845608028654
GELU_CUBIC = 0.044715
COLUMNS = 256


def column_blocks(width):
    size = min(COLUMNS, width)
    return [slice(start, start + size) for start in range(0, width, size)]


def norm_parts(values):
    center = values - jnp.mean(values, axis=-1, keepdims=True)
    inverse = lax.rsqrt(jnp.mean(center * center, axis=-1, keepdims=True) + 1e-05)
    return center * inverse, inverse


def norm_rows(values, gain_row, offset_row):
    return norm_parts(values)[0] * gain_row + offset_row


def norm_back(values, gain_row, cot):
    normal, inverse = norm_parts(values)
    scaled = cot * gain_row
    mean_one = jnp.mean(scaled, axis=-1, keepdims=True)
    mean_two = jnp.mean(scaled * normal, axis=-1, keepdims=True)
    return inverse * (scaled - mean_one - normal * mean_two), cot * normal


def gelu_value(values):
    bent = jnp.tanh(GELU_SCALE * (values + GELU_CUBIC * values * values * values))
    return 0.5 * values * (1.0 + bent), bent


def gelu_slope(values, bent):
    inner = GELU_SCALE * (1.0 + 3.0 * GELU_CUBIC * values * values)
    return 0.5 * (1.0 + bent) + 0.5 * values * (1.0 - bent * bent) * inner


class LineTotal:
    scratch_count = 7

    @staticmethod
    def scratch(rows, model, chunks):
        block = pltpu.VMEM((rows, model), jnp.bfloat16)
        return [block] * 3 + [pltpu.SemaphoreType.DMA((chunks,))] * 4

    def __init__(self, refs, chunks):
        self.own, self.near_buf, self.mid_buf = refs[:3]
        self.near_send, self.near_recv, self.mid_send, self.mid_recv = refs[3:]
        self.chunks = chunks
        self.step = self.own.shape[0] // chunks
        place = lax.axis_index("tensor")
        self.near = place + 1 - 2 * lax.rem(place, 2)
        self.across = 3 - place
        self.is_end = (place == 0) | (place == 3)
        self.is_mid = (place == 1) | (place == 2)

    def rows(self, c):
        return pl.ds(pl.multiple_of(c * self.step, self.step), self.step)

    def to_near(self, src, c):
        return pltpu.make_async_remote_copy(
            src_ref=src.at[self.rows(c)],
            dst_ref=self.near_buf.at[self.rows(c)],
            send_sem=self.near_send.at[c],
            recv_sem=self.near_recv.at[c],
            device_id={"tensor": self.near},
            device_id_type=pl.DeviceIdType.MESH,
        )

    def to_across(self, c):
        return pltpu.make_async_remote_copy(
            src_ref=self.own.at[self.rows(c)],
            dst_ref=self.mid_buf.at[self.rows(c)],
            send_sem=self.mid_send.at[c],
            recv_sem=self.mid_recv.at[c],
            device_id={"tensor": self.across},
            device_id_type=pl.DeviceIdType.MESH,
        )

    def peers(self):
        return [
            (self.is_end | self.is_mid, "tensor", self.near),
            (self.is_mid, "tensor", self.across),
        ]

    def send(self, c):
        @pl.when(self.is_end)
        def _():
            self.to_near(self.own, c).start()

    def summed(self, left, right, c):
        rows = self.rows(c)
        both = left[rows, :].astype(jnp.float32) + right[rows, :].astype(jnp.float32)
        return both.astype(jnp.bfloat16)

    def join(self, c):
        @pl.when(self.is_mid)
        def _():
            self.to_near(self.near_buf, c).wait_recv()
            self.own[self.rows(c), :] = self.summed(self.own, self.near_buf, c)
            self.to_across(c).start()

    def finish(self, c):
        @pl.when(self.is_mid)
        def _():
            self.to_across(c).wait_recv()
            self.near_buf[self.rows(c), :] = self.summed(self.own, self.mid_buf, c)
            self.to_near(self.near_buf, c).start()

    def take(self, c):
        @pl.when(self.is_end)
        def _():
            self.to_near(self.own, c).wait_recv()

        return self.near_buf[self.rows(c), :].astype(jnp.float32)

    def drain(self, c):
        @pl.when(self.is_end)
        def _():
            self.to_near(self.own, c).wait_send()

        @pl.when(self.is_mid)
        def _():
            self.to_across(c).wait_send()
            self.to_near(self.near_buf, c).wait_send()


def flipped(place, bit):
    return place + bit - 2 * bit * lax.rem(lax.div(place, bit), 2)


def dp_copy(src, dst, send_sem, recv_sem, target):
    return pltpu.make_async_remote_copy(
        src_ref=src,
        dst_ref=dst,
        send_sem=send_sem,
        recv_sem=recv_sem,
        device_id={"dp": target},
        device_id_type=pl.DeviceIdType.MESH,
    )


def greet(targets):
    barrier = pltpu.get_barrier_semaphore()
    count = 0
    for known, axis, target in targets:
        count = count + jnp.where(known, 1, 0)

        @pl.when(known)
        def _(axis=axis, target=target):
            pl.semaphore_signal(
                barrier, inc=1, device_id={axis: target}, device_id_type=pl.DeviceIdType.MESH
            )

    pl.semaphore_wait(barrier, count)


def cube_targets():
    place = lax.axis_index("dp")
    return [(place >= 0, "dp", flipped(place, bit)) for bit in (1, 2, 4)]


def window_targets(hops):
    place = lax.axis_index("dp")
    size = lax.axis_size("dp")
    after = [(place + hop < size, "dp", place + hop) for hop in range(1, hops + 1)]
    return after + [(place - hop >= 0, "dp", place - hop) for hop in range(1, hops + 1)]


class Gather:
    copies = 8

    @staticmethod
    def scratch():
        return [pltpu.SemaphoreType.DMA((Gather.copies,))] * 2

    def __init__(self, own_ref, full_ref, sems):
        self.own, self.full = own_ref, full_ref
        self.send, self.recv = sems
        self.size = own_ref.shape[0]
        self.place = lax.axis_index("dp")

    def span(self, owner, part=None):
        size = self.size if part is None else self.size // 2
        first = owner * self.size + (0 if not part else size)
        return self.full.at[pl.ds(pl.multiple_of(first, size), size)]

    def copy(self, k):
        me = self.place
        fx, fy, sib = flipped(me, 2), flipped(me, 4), flipped(me, 1)
        src, dst, target = {
            0: lambda: (self.own, self.span(me), fx),
            1: lambda: (self.own, self.span(me), fy),
            2: lambda: (self.own, self.span(me), sib),
            3: lambda: (self.span(fx, 0), self.span(fx, 0), fy),
            4: lambda: (self.span(fy, 1), self.span(fy, 1), fx),
            5: lambda: (self.span(fx), self.span(fx), sib),
            6: lambda: (self.span(fy), self.span(fy), sib),
            7: lambda: (self.span(flipped(fx, 4)), self.span(flipped(fx, 4)), sib),
        }[k]()
        return dp_copy(src, dst, self.send.at[k], self.recv.at[k], target)

    def begin(self):
        first = pl.multiple_of(self.place * self.size, self.size)
        self.full[pl.ds(first, self.size), :] = self.own[...]
        for k in (0, 1, 2):
            self.copy(k).start()

    def relay(self):
        self.copy(0).wait_recv()
        self.copy(3).start()
        self.copy(5).start()
        self.copy(1).wait_recv()
        self.copy(4).start()
        self.copy(6).start()

    def pass_on(self):
        self.copy(3).wait_recv()
        self.copy(4).wait_recv()
        self.copy(7).start()

    def finish(self):
        for k in (2, 5, 6, 7):
            self.copy(k).wait_recv()

    def drain(self):
        for k in range(self.copies):
            self.copy(k).wait_send()


class Scatter:
    copies = 10
    refs = 7

    @staticmethod
    def scratch(rows, width):
        half = rows // 2
        return [
            pltpu.VMEM((4, rows, width), jnp.bfloat16),
            pltpu.VMEM((2, half, width), jnp.bfloat16),
            pltpu.VMEM((2, half, width), jnp.bfloat16),
            pltpu.VMEM((half, width), jnp.bfloat16),
            pltpu.VMEM((half, width), jnp.bfloat16),
            pltpu.SemaphoreType.DMA((Scatter.copies,)),
            pltpu.SemaphoreType.DMA((Scatter.copies,)),
        ]

    def __init__(self, grad_ref, out_ref, refs):
        self.grad, self.out = grad_ref, out_ref
        self.acc, self.x_one, self.y_one, self.x_two, self.y_two, self.send, self.recv = refs
        self.size = out_ref.shape[0]
        me = lax.axis_index("dp")
        self.core = lax.rem(me, 2)
        self.sib, self.fx, self.fy = flipped(me, 1), flipped(me, 2), flipped(me, 4)
        self.here, self.qx, self.qy = (lax.div(v, 2) for v in (me, self.fx, self.fy))
        self.qxy = lax.div(flipped(self.fx, 4), 2)

    def owner_rows(self, chip, core):
        first = (2 * chip + core) * self.size
        return pl.ds(pl.multiple_of(first, self.size), self.size)

    def half(self, which):
        count = self.size // 2
        return pl.ds(which * count, count)

    def to_core(self, chip):
        src = self.grad.at[self.owner_rows(chip, 1 - self.core)]
        return dp_copy(src, self.acc.at[chip], self.send.at[chip], self.recv.at[chip], self.sib)

    def copy(self, k):
        acc, low, high = self.acc, self.half(0), self.half(1)
        src, dst, target = {
            4: lambda: (acc.at[self.qx, low], self.x_one.at[0], self.fx),
            5: lambda: (acc.at[self.qxy, low], self.x_one.at[1], self.fx),
            6: lambda: (acc.at[self.qy, high], self.y_one.at[0], self.fy),
            7: lambda: (acc.at[self.qxy, high], self.y_one.at[1], self.fy),
            8: lambda: (acc.at[self.qy, low], self.y_two, self.fy),
            9: lambda: (acc.at[self.qx, high], self.x_two, self.fx),
        }[k]()
        return dp_copy(src, dst, self.send.at[k], self.recv.at[k], target)

    def begin(self):
        for chip in range(4):
            self.to_core(chip).start()

    def add_core(self, chip):
        self.to_core(chip).wait_recv()
        first = self.owner_rows(chip, self.core).start
        count = self.size // 2
        for which in (0, 1):
            rows = pl.ds(pl.multiple_of(first + which * count, count), count)
            total = self.acc[chip, self.half(which), :].astype(jnp.float32)
            total = total + self.grad[rows, :].astype(jnp.float32)
            self.acc[chip, self.half(which), :] = total.astype(jnp.bfloat16)

    def spread(self):
        self.add_core(self.qxy)
        self.copy(5).start()
        self.copy(7).start()
        self.add_core(self.qx)
        self.copy(4).start()
        self.add_core(self.qy)
        self.copy(6).start()
        self.add_core(self.here)

    def add_half(self, chip, which, other):
        total = self.acc[chip, self.half(which), :].astype(jnp.float32)
        self.acc[chip, self.half(which), :] = (total + other.astype(jnp.float32)).astype(
            jnp.bfloat16
        )

    def narrow(self):
        self.copy(5).wait_recv()
        self.add_half(self.qy, 0, self.x_one[1])
        self.copy(8).start()
        self.copy(7).wait_recv()
        self.add_half(self.qx, 1, self.y_one[1])
        self.copy(9).start()

    def close(self):
        for k in (4, 6, 8, 9):
            self.copy(k).wait_recv()
        pairs = ((self.x_one, self.y_two), (self.y_one, self.x_two))
        for which, (one, two) in enumerate(pairs):
            total = self.acc[self.here, self.half(which), :].astype(jnp.float32)
            total = total + one[0].astype(jnp.float32) + two[...].astype(jnp.float32)
            self.out[self.half(which), :] = total

    def drain(self):
        for chip in range(4):
            self.to_core(chip).wait_send()
        for k in range(4, self.copies):
            self.copy(k).wait_send()


def scatters_of(grads, outs, scratch):
    count = Scatter.refs
    return [
        Scatter(g, o, scratch[count * i : count * (i + 1)])
        for i, (g, o) in enumerate(zip(grads, outs))
    ]


class LineGather:
    refs = 5

    @staticmethod
    def scratch(chunks):
        return [pltpu.SemaphoreType.DMA((3, chunks))] * 4

    def __init__(self, all_ref, chunks, sems):
        self.all, self.chunks = all_ref, chunks
        self.step = all_ref.shape[1] // chunks
        self.right_send, self.right_recv, self.left_send, self.left_recv = sems
        self.place = lax.axis_index("tensor")
        self.last = all_ref.shape[0] - 1

    def peers(self):
        return [
            (self.place < self.last, "tensor", self.place + 1),
            (self.place > 0, "tensor", self.place - 1),
        ]

    def rows(self, c):
        return pl.ds(pl.multiple_of(c * self.step, self.step), self.step)

    def copy(self, way, block, hop, c):
        send, recv = (
            (self.right_send, self.right_recv) if way > 0 else (self.left_send, self.left_recv)
        )
        return pltpu.make_async_remote_copy(
            src_ref=self.all.at[block, self.rows(c)],
            dst_ref=self.all.at[block, self.rows(c)],
            send_sem=send.at[hop, c],
            recv_sem=recv.at[hop, c],
            device_id={"tensor": self.place + way},
            device_id_type=pl.DeviceIdType.MESH,
        )

    def holds(self, way, hop):
        return (self.place >= hop) if way > 0 else (self.place + hop <= self.last)

    def passes(self, way, hop):
        open_end = (self.place < self.last) if way > 0 else (self.place > 0)
        return self.holds(way, hop) & open_end

    def hand(self, hop, c):
        for way in (1, -1):
            block = self.place - way * hop
            if hop > 0:

                @pl.when(self.holds(way, hop))
                def _(way=way, block=block):
                    self.copy(way, block, hop - 1, c).wait_recv()

            if hop < self.last:

                @pl.when(self.passes(way, hop))
                def _(way=way, block=block):
                    self.copy(way, block, hop, c).start()

    def drain(self, c):
        for way in (1, -1):
            for hop in range(self.last):

                @pl.when(self.passes(way, hop))
                def _(way=way, hop=hop):
                    self.copy(way, self.place - way * hop, hop, c).wait_send()


def project_groups(all_ref, rows, weights_ref):
    total = None
    for group in range(all_ref.shape[0]):
        part = jnp.dot(
            all_ref[group, rows, :], weights_ref[group], preferred_element_type=jnp.float32
        )
        total = part if total is None else total + part
    return total


class Window:
    @staticmethod
    def scratch(hops, chunks):
        return [pltpu.SemaphoreType.DMA((hops, chunks))] * 2

    def __init__(self, window_ref, rows, chunks, sems):
        self.window, self.total_rows, self.chunks = window_ref, rows, chunks
        self.step = rows // chunks
        self.hops = window_ref.shape[0] // rows - 1
        self.send, self.recv = sems
        self.place = lax.axis_index("dp")
        self.size = lax.axis_size("dp")

    def span(self, block, c):
        first = block * self.total_rows + c * self.step
        return pl.ds(pl.multiple_of(first, self.step), self.step)

    def copy(self, hop, c):
        return dp_copy(
            self.window.at[self.span(self.hops, c)],
            self.window.at[self.span(self.hops - hop, c)],
            self.send.at[hop - 1, c],
            self.recv.at[hop - 1, c],
            self.place + hop,
        )

    def clear(self):
        for hop in range(1, self.hops + 1):

            @pl.when(self.place - hop < 0)
            def _(hop=hop):
                first = (self.hops - hop) * self.total_rows
                shape = (self.total_rows, self.window.shape[1])
                self.window[first : first + self.total_rows, :] = jnp.zeros(shape, jnp.bfloat16)

    def start(self, c):
        for hop in range(1, self.hops + 1):

            @pl.when(self.place + hop < self.size)
            def _(hop=hop):
                self.copy(hop, c).start()

    def drain(self, c):
        for hop in range(1, self.hops + 1):

            @pl.when(self.place + hop < self.size)
            def _(hop=hop):
                self.copy(hop, c).wait_send()

            @pl.when(self.place - hop >= 0)
            def _(hop=hop):
                self.copy(hop, c).wait_recv()


def run_stages(chunks, stages, events=()):
    def body(t, carry):
        for when, event in events:
            pl.when(t == when)(event)
        for lag, stage in stages:
            c = t - LAG * lag

            @pl.when((c >= 0) & (c < chunks))
            def _(stage=stage, c=c):
                stage(c)

        return carry

    lax.fori_loop(0, chunks + LAG * max(lag for lag, _ in stages), body, 0)


def drain_all(chunks, lines):
    def body(c, carry):
        for line in lines:
            line.drain(c)
        return carry

    lax.fori_loop(0, chunks, body, 0)


def add_sums(sums_ref, row, values):
    width = values.shape[1]
    sums_ref[row : row + 1, :width] += jnp.sum(values, axis=0, keepdims=True)


def project_into(line, c, left, weight_ref):
    rows = line.rows(c)
    for cols in column_blocks(weight_ref.shape[1]):
        part = jnp.dot(left, weight_ref[:, cols], preferred_element_type=jnp.float32)
        line.own[rows, cols] = part.astype(jnp.bfloat16)
    line.send(c)


def project_back_into(line, c, left, weight_ref):
    rows = line.rows(c)
    for cols in column_blocks(weight_ref.shape[0]):
        part = dot_rows(left, weight_ref[cols, :])
        line.own[rows, cols] = part.astype(jnp.bfloat16)
    line.send(c)


def head_kernel(hops, *refs):
    ins, outs, scratch = refs[:6], refs[6:15], refs[15:]
    h_ref, small_own, wa_own, we_own, wr_own, wo_own = ins
    small_ref, wa_ref, we_ref, wr_ref, wo_ref, shard_ref, a1_ref, q_ref, window_ref = outs
    line = LineGather(shard_ref, 1, scratch[:4])
    groups, share = shard_ref.shape[0], shard_ref.shape[1] // 2
    pairs = list(zip((small_own, wa_own, we_own, wr_own), outs[:4]))
    pairs += [(shard_ref.at[g, pl.ds(0, share)], wo_ref.at[g]) for g in range(groups)]
    gathers = [
        Gather(o, f, scratch[4 + 2 * i : 6 + 2 * i]) for i, (o, f) in enumerate(pairs)
    ]
    small, wa, we, wr = gathers[:4]
    rows, width = q_ref.shape
    chunks = 4
    window = Window(window_ref, rows, chunks, scratch[-2:])
    shard_ref[line.place] = wo_own[...]
    greet(cube_targets() + window_targets(hops) + line.peers())
    small.begin()
    wa.begin()
    line.hand(0, 0)
    window.clear()
    small.relay()
    small.pass_on()
    small.finish()
    values = small_ref[...].astype(jnp.float32)
    gain, offset = wide_row(values, GAIN_ROW), wide_row(values, OFFSET_ROW)
    bias_q, bias_v = narrow_row(values, width, 0), narrow_row(values, width, 1)
    step = rows // chunks

    def normalize(c, carry):
        at = pl.ds(pl.multiple_of(c * step, step), step)
        a1_ref[at, :] = norm_rows(h_ref[at, :], gain, offset).astype(jnp.bfloat16)
        return carry

    line.hand(1, 0)
    lax.fori_loop(0, chunks, normalize, 0)
    line.hand(2, 0)
    wa.relay()
    we.begin()
    wa.pass_on()
    wr.begin()
    line.hand(3, 0)
    for member in gathers[4:]:
        member.begin()
    wa.finish()

    def project(c, carry):
        at = pl.ds(pl.multiple_of(c * step, step), step)
        a1 = a1_ref[at, :]
        there = window.span(window.hops, c)
        for part in (1, 2):
            cols = slice(part * width, (part + 1) * width)
            value = jnp.dot(a1, wa_ref[:, cols], preferred_element_type=jnp.float32)
            value = value if part == 1 else value + bias_v
            window_ref[there, (part - 1) * width : part * width] = value.astype(jnp.bfloat16)
        window.start(c)
        value = jnp.dot(a1, wa_ref[:, :width], preferred_element_type=jnp.float32)
        q_ref[at, :] = (value + bias_q).astype(jnp.bfloat16)
        return carry

    lax.fori_loop(0, chunks, project, 0)
    for member in gathers[2:]:
        member.relay()
    for member in gathers[2:]:
        member.pass_on()
    for c in range(chunks):
        window.drain(c)
    line.drain(0)
    for member in gathers[2:]:
        member.finish()
    for member in gathers:
        member.drain()


SMALL_ROWS = 32
BRANCH_ROW, UNIT_ROW, GAIN_ROW, OFFSET_ROW, MARK_ROW = 8, 12, 14, 18, 22


def wide_row(values, row):
    owners = range(values.shape[0] // SMALL_ROWS)
    return jnp.concatenate(
        [values[o * SMALL_ROWS + row : o * SMALL_ROWS + row + 1, :] for o in owners], axis=1
    )


def narrow_row(values, width, index):
    owners = range(values.shape[0] // SMALL_ROWS)
    count = width // LANES
    parts = []
    for row in range(index * count, (index + 1) * count):
        total = values[row : row + 1, :]
        for o in owners[1:]:
            total = total + values[o * SMALL_ROWS + row : o * SMALL_ROWS + row + 1, :]
        parts.append(total)
    return jnp.concatenate(parts, axis=1)


def pack_small(small_in, marks, width):
    attend_bias, branch_bias, expand_bias, norm_gain, norm_bias = small_in
    place = lax.axis_index("dp")
    flat = attend_bias.reshape(-1, attend_bias.shape[-1])
    spread = jnp.zeros((flat.shape[0], width), jnp.bfloat16)
    spread = lax.dynamic_update_slice(spread, flat, (0, place * flat.shape[1]))
    rows = [spread.reshape(-1, LANES)]
    rows += [e.reshape(-1, LANES) for e in (branch_bias, expand_bias, norm_gain, norm_bias)]
    rows.append(marks.astype(jnp.bfloat16).reshape(-1, LANES))
    packed = jnp.concatenate(rows, axis=0)
    return jnp.pad(packed, ((0, SMALL_ROWS - packed.shape[0]), (0, 0)))


def unpack_small(small_all, rows, width, reach_back):
    size = small_all.shape[0] // SMALL_ROWS
    grid = small_all.reshape(size, SMALL_ROWS, LANES)
    wide = grid[:, BRANCH_ROW:MARK_ROW].astype(jnp.float32)
    wide = jnp.moveaxis(wide, 0, 1).reshape(MARK_ROW - BRANCH_ROW, size * LANES)
    branches, units = wide[:4].reshape(2, 2, -1), wide[4:6]
    gains, offsets = wide[6:10].reshape(2, 2, -1), wide[10:14].reshape(2, 2, -1)
    attend_b = jnp.sum(grid[:, :BRANCH_ROW].astype(jnp.float32), axis=0).reshape(2, 2, width)
    marks = grid[:, MARK_ROW : MARK_ROW + rows // LANES].astype(jnp.int32).reshape(-1)
    padded = jnp.concatenate([jnp.zeros((reach_back * rows,), jnp.int32), marks])
    begin = lax.axis_index("dp") * rows
    window = lax.dynamic_slice_in_dim(padded, begin, (reach_back + 1) * rows)
    return attend_b, branches, units, gains, offsets, (window[reach_back * rows :, None], window[None])


def first_kernel(chunks, *refs):
    ins, outs, scratch = refs[:10], refs[10:22], refs[22:]
    o_ref, wo_ref, h_ref, vec_ref, we_ref, wr_ref = ins[:6]
    mid_ref, a2_ref, f_ref, u_ref, next_ref, a1_ref, q_ref, window_ref = outs[:8]
    wa_ref = outs[8]
    two = LineTotal(scratch[:7], chunks)
    all_ref = scratch[7]
    one = LineGather(all_ref, chunks, scratch[8:12])
    shard_ref = ins[9]
    groups, share = shard_ref.shape[0], shard_ref.shape[1] // 2
    pairs = list(zip(ins[6:9], outs[8:11]))
    pairs += [(shard_ref.at[g, pl.ds(share, share)], outs[11].at[g]) for g in range(groups)]
    gathers = [
        Gather(o, f, scratch[12 + 2 * i : 14 + 2 * i]) for i, (o, f) in enumerate(pairs)
    ]
    rows_all, width = q_ref.shape
    window = Window(window_ref, rows_all, chunks, scratch[-2:])
    all_ref[one.place] = o_ref[...]
    greet(one.peers() + two.peers() + cube_targets() + window_targets(window.hops))
    window.clear()

    def feed(c):
        rows = one.rows(c)
        one.hand(3, c)
        middle = h_ref[rows, :] + (project_groups(all_ref, rows, wo_ref) + vec_ref[0:1, :])
        mid_ref[rows, :] = middle
        a2 = norm_rows(middle, vec_ref[1:2, :], vec_ref[2:3, :]).astype(jnp.bfloat16)
        a2_ref[rows, :] = a2
        for cols in column_blocks(we_ref.shape[1]):
            f = jnp.dot(a2, we_ref[:, cols], preferred_element_type=jnp.float32)
            f = f + vec_ref[3:4, cols]
            f_ref[rows, cols] = f
            u_ref[rows, cols] = gelu_value(f)[0].astype(jnp.bfloat16)
        project_into(two, c, u_ref[rows, :], wr_ref)

    def end(c):
        rows = two.rows(c)
        following = mid_ref[rows, :] + (two.take(c) + vec_ref[4:5, :])
        next_ref[rows, :] = following
        a1 = norm_rows(following, vec_ref[5:6, :], vec_ref[6:7, :]).astype(jnp.bfloat16)
        a1_ref[rows, :] = a1
        there = window.span(window.hops, c)
        for part in (1, 2, 0):
            cols = slice(part * width, (part + 1) * width)
            value = jnp.dot(a1, wa_ref[:, cols], preferred_element_type=jnp.float32)
            value = (value + vec_ref[7:8, cols]).astype(jnp.bfloat16)
            if part == 0:
                q_ref[rows, :] = value
            else:
                window_ref[there, (part - 1) * width : part * width] = value
            if part == 2:
                window.start(c)

    wa, we, wr = gathers[:3]
    rest = gathers[3:]

    def every(name):
        def event():
            for member in rest:
                getattr(member, name)()

        return event

    last = chunks + LAG * 6 - 1
    run_stages(
        chunks,
        [
            (0, functools.partial(one.hand, 0)),
            (1, functools.partial(one.hand, 1)),
            (2, functools.partial(one.hand, 2)),
            (3, feed),
            (4, two.join),
            (5, two.finish),
            (6, end),
        ],
        [
            (0, wa.begin),
            (3, wa.relay),
            (3, we.begin),
            (5, wa.pass_on),
            (LAG * 6, wa.finish),
            (LAG * 6, we.relay),
            (LAG * 6, wr.begin),
            (LAG * 6, every("begin")),
            (LAG * 6 + 2, we.pass_on),
            (last - 2, wr.relay),
            (last - 2, every("relay")),
            (last, wr.pass_on),
            (last, every("pass_on")),
        ],
    )
    drain_all(chunks, [one, two, window])
    for member in gathers[1:]:
        member.finish()
    for member in gathers:
        member.drain()


def turn_kernel(chunks, *refs):
    ins, outs, scratch = refs[:7], refs[7:16], refs[16:]
    o_ref, wo_ref, h_ref, vec_ref, we_ref, wr_ref, e_ref = ins[:7]
    a2_ref, u_ref, eb_ref, dfb_ref, dmid_ref, db_ref, do_ref, mid_ref, sums_ref = outs
    back = LineTotal(scratch[:7], chunks)
    all_ref = scratch[7]
    one = LineGather(all_ref, chunks, scratch[8:12])
    all_ref[one.place] = o_ref[...]
    sums_ref[...] = jnp.zeros_like(sums_ref)
    greet(one.peers() + back.peers())

    def feed(c):
        rows = one.rows(c)
        one.hand(3, c)
        middle = h_ref[rows, :] + (project_groups(all_ref, rows, wo_ref) + vec_ref[0:1, :])
        mid_ref[rows, :] = middle
        a2 = norm_rows(middle, vec_ref[1:2, :], vec_ref[2:3, :]).astype(jnp.bfloat16)
        a2_ref[rows, :] = a2
        e = e_ref[rows, :]
        add_sums(sums_ref, 0, e)
        eb = e.astype(jnp.bfloat16)
        eb_ref[rows, :] = eb
        for cols in column_blocks(we_ref.shape[1]):
            f = jnp.dot(a2, we_ref[:, cols], preferred_element_type=jnp.float32)
            f = f + vec_ref[3:4, cols]
            u, bent = gelu_value(f)
            u_ref[rows, cols] = u.astype(jnp.bfloat16)
            df = dot_rows(eb, wr_ref[cols, :]) * gelu_slope(f, bent)
            sums_ref[1:2, cols] += jnp.sum(df, axis=0, keepdims=True)
            dfb_ref[rows, cols] = df.astype(jnp.bfloat16)
        project_back_into(back, c, dfb_ref[rows, :], we_ref)

    def turn(c):
        rows = back.rows(c)
        cot = back.take(c)
        part, gain_part = norm_back(mid_ref[rows, :], vec_ref[1:2, :], cot)
        dmid = e_ref[rows, :] + part
        dmid_ref[rows, :] = dmid
        add_sums(sums_ref, 2, gain_part)
        add_sums(sums_ref, 3, cot)
        add_sums(sums_ref, 4, dmid)
        db = dmid.astype(jnp.bfloat16)
        db_ref[rows, :] = db
        do_ref[rows, :] = dot_rows(db, wo_ref[one.place]).astype(jnp.bfloat16)

    run_stages(
        chunks,
        [
            (0, functools.partial(one.hand, 0)),
            (1, functools.partial(one.hand, 1)),
            (2, functools.partial(one.hand, 2)),
            (3, feed),
            (4, back.join),
            (5, back.finish),
            (6, turn),
        ],
    )
    drain_all(chunks, [one, back])


def cross_kernel(chunks, *refs):
    ins, outs, scratch = refs[:14], refs[14:24], refs[24:]
    dproj_ref, wa_ref, h_ref, dmid_in_ref, vec_ref, f_ref, mid_ref, we_ref, wr_ref, wo_ref = ins[:10]
    eb_ref, dfb_ref, dmid_ref, db_ref, do_ref, sums_ref = outs[:6]
    e_ref = scratch[0]
    one = LineTotal(scratch[1:8], chunks)
    back = LineTotal(scratch[8:15], chunks)
    scatters = scatters_of(ins[10:], outs[6:], scratch[15:])
    sums_ref[...] = jnp.zeros_like(sums_ref)
    greet(one.peers() + cube_targets())

    def start(c):
        project_back_into(one, c, dproj_ref[one.rows(c), :], wa_ref)

    def feed(c):
        rows = one.rows(c)
        cot = one.take(c)
        part, gain_part = norm_back(h_ref[rows, :], vec_ref[0:1, :], cot)
        e = dmid_in_ref[rows, :] + part
        e_ref[rows, :] = e
        add_sums(sums_ref, 0, gain_part)
        add_sums(sums_ref, 1, cot)
        add_sums(sums_ref, 2, e)
        eb = e.astype(jnp.bfloat16)
        eb_ref[rows, :] = eb
        for cols in column_blocks(we_ref.shape[1]):
            f = f_ref[rows, cols]
            unused, bent = gelu_value(f)
            df = dot_rows(eb, wr_ref[cols, :]) * gelu_slope(f, bent)
            sums_ref[3:4, cols] += jnp.sum(df, axis=0, keepdims=True)
            dfb_ref[rows, cols] = df.astype(jnp.bfloat16)
        project_back_into(back, c, dfb_ref[rows, :], we_ref)

    def turn(c):
        rows = back.rows(c)
        cot = back.take(c)
        part, gain_part = norm_back(mid_ref[rows, :], vec_ref[1:2, :], cot)
        dmid = e_ref[rows, :] + part
        dmid_ref[rows, :] = dmid
        add_sums(sums_ref, 4, gain_part)
        add_sums(sums_ref, 5, cot)
        add_sums(sums_ref, 6, dmid)
        db = dmid.astype(jnp.bfloat16)
        db_ref[rows, :] = db
        do_ref[rows, :] = dot_rows(db, wo_ref[lax.axis_index("tensor")]).astype(jnp.bfloat16)

    run_stages(
        chunks,
        [
            (0, start),
            (1, one.join),
            (2, one.finish),
            (3, feed),
            (4, back.join),
            (5, back.finish),
            (6, turn),
        ],
        scatter_events(scatters, chunks + LAG * 6 - 1, 1, 2, 3, 3),
    )
    drain_all(chunks, [one, back])
    for member in scatters:
        member.drain()


def scatter_events(scatters, last, apart, wait_one, wait_two, wait_three):
    events = []
    for i, member in enumerate(scatters):
        at = i * apart
        events.append((min(at, last), member.begin))
        events.append((min(at + wait_one, last), member.spread))
        events.append((min(at + wait_one + wait_two, last), member.narrow))
        events.append((min(at + wait_one + wait_two + wait_three, last), member.close))
    return events


def last_kernel(chunks, *refs):
    ins, outs, scratch = refs[:10], refs[10:18], refs[18:]
    dproj_ref, wa_ref, h_ref, dmid_ref, vec_ref = ins[:5]
    grad_ref, late_ref, sums_ref = outs[0], outs[1], outs[2]
    one = LineTotal(scratch[:7], chunks)
    parts_ref, seen_ref, part_send, part_recv = scratch[7:11]
    scatters = scatters_of(ins[5:], outs[3:], scratch[11:])
    place, size = lax.axis_index("dp"), lax.axis_size("dp")
    sums_ref[...] = jnp.zeros_like(sums_ref)
    everyone = [(place >= 0, "dp", lax.rem(place + j, size)) for j in range(1, size)]
    greet(one.peers() + everyone)

    def start(c):
        project_back_into(one, c, dproj_ref[one.rows(c), :], wa_ref)

    def end(c):
        rows = one.rows(c)
        cot = one.take(c)
        part, gain_part = norm_back(h_ref[rows, :], vec_ref[0:1, :], cot)
        grad_ref[rows, :] = dmid_ref[rows, :] + part
        add_sums(sums_ref, 0, gain_part)
        add_sums(sums_ref, 1, cot)

    run_stages(
        chunks,
        [(0, start), (1, one.join), (2, one.finish), (3, end)],
        scatter_events(scatters, chunks + LAG * 3 - 1, 1, 1, 3, 3),
    )

    def part_copy(j):
        target = lax.rem(place + j, size)
        return dp_copy(
            parts_ref.at[target], seen_ref.at[j], part_send.at[j], part_recv.at[j], target
        )

    for owner in range(size):
        parts_ref[owner] = sums_ref[:, owner * LANES : (owner + 1) * LANES]
    for j in range(1, size):
        part_copy(j).start()
    drain_all(chunks, [one])
    total = parts_ref[place]
    for j in range(1, size):
        part_copy(j).wait_recv()
        total = total + seen_ref[j]
    late_ref[...] = total
    for j in range(1, size):
        part_copy(j).wait_send()
    for member in scatters:
        member.drain()


CHUNKS = 8
LAG = 1
MEGA = 1024 * 1024


def line_call(kernel, name, number, out_shapes, extra, lines, span_us, args, more=()):
    rows, model = extra
    scratch = []
    if lines[0]:
        scratch.append(pltpu.VMEM((rows, model), jnp.float32))
    for _ in range(lines[1]):
        scratch += LineTotal.scratch(rows, model, CHUNKS)
    scratch += list(more)
    return pl.pallas_call(
        functools.partial(kernel, CHUNKS),
        out_shape=tuple(jax.ShapeDtypeStruct(shape, kind) for shape, kind in out_shapes),
        in_specs=in_vmem(len(args)),
        out_specs=tuple(in_vmem(len(out_shapes))),
        scratch_shapes=scratch,
        cost_estimate=pl.CostEstimate(
            flops=int(span_us * 1e9), bytes_accessed=0, transcendentals=0
        ),
        compiler_params=pltpu.CompilerParams(
            collective_id=number, has_side_effects=True, vmem_limit_bytes=56 * MEGA
        ),
        name=name,
    )(*args)


def stack_rows(model, rows):
    rows = [jnp.pad(r, (0, model - r.shape[0])) for r in rows]
    rows += [jnp.zeros((model,), jnp.float32)] * (-len(rows) % 8)
    return jnp.stack(rows)


def window_of(kv_now, reach_back):
    kv_list = [passed_along(kv_now, "dp", hop) for hop in range(reach_back, 0, -1)]
    return jnp.concatenate(kv_list + [kv_now], axis=0)


def grad_blocks(left_ref, right_ref, out_ref):
    for rows in column_blocks(left_ref.shape[1]):
        left = left_ref[:, rows]
        for cols in column_blocks(right_ref.shape[1]):
            out_ref[rows, cols] = dot_tokens(left, right_ref[:, cols]).astype(jnp.bfloat16)


class WindowBack:
    @staticmethod
    def scratch(hops, rows, width, pieces):
        return [
            pltpu.VMEM((hops * rows, width), jnp.bfloat16),
            pltpu.VMEM((hops * rows, width), jnp.bfloat16),
            pltpu.SemaphoreType.DMA((hops, pieces)),
            pltpu.SemaphoreType.DMA((hops, pieces)),
        ]

    def __init__(self, rows, refs):
        self.out, self.seen, self.send, self.recv = refs
        self.rows = rows
        self.hops = self.out.shape[0] // rows
        self.place, self.size = lax.axis_index("dp"), lax.axis_size("dp")

    def span(self, hop):
        return slice((self.hops - hop) * self.rows, (self.hops - hop + 1) * self.rows)

    def copy(self, hop, piece, cols):
        return dp_copy(
            self.out.at[self.span(hop), cols],
            self.seen.at[self.span(hop), cols],
            self.send.at[hop - 1, piece],
            self.recv.at[hop - 1, piece],
            self.place - hop,
        )

    def clear(self):
        for hop in range(1, self.hops + 1):

            @pl.when(self.place + hop >= self.size)
            def _(hop=hop):
                shape = (self.rows, self.seen.shape[1])
                self.seen[self.span(hop), :] = jnp.zeros(shape, jnp.bfloat16)

    def start(self, piece, cols):
        for hop in range(1, self.hops + 1):

            @pl.when(self.place - hop >= 0)
            def _(hop=hop):
                self.copy(hop, piece, cols).start()

    def take(self, piece, cols):
        total = None
        for hop in range(1, self.hops + 1):

            @pl.when(self.place + hop < self.size)
            def _(hop=hop):
                self.copy(hop, piece, cols).wait_recv()

            seen = self.seen[self.span(hop), cols].astype(jnp.float32)
            total = seen if total is None else total + seen
        return total

    def drain(self, piece, cols):
        for hop in range(1, self.hops + 1):

            @pl.when(self.place - hop >= 0)
            def _(hop=hop):
                self.copy(hop, piece, cols).wait_send()


def return_kernel(chunks, first, hops, *refs):
    ins, outs, scratch = refs[:17], refs[17:24], refs[24:]
    q_ref, kv_ref, lse_ref, cot_ref, own_ref, window_ref = ins[:6]
    a2_ref, dfb_ref, u_ref, eb_ref, o_ref, db_ref, a1_ref = ins[6:13]
    act_ref, wr_ref, mid_ref, bias_ref = ins[13:]
    dproj_ref, sums_ref, expand_ref, reduce_ref, output_ref, attend_ref, hidden_ref = outs
    acc = scratch[0]
    line = LineTotal(scratch[1:8], chunks)
    back_pass = WindowBack(q_ref.shape[0], scratch[8:12])
    rows, width = q_ref.shape
    window_rows = kv_ref.shape[0]
    back = window_rows - rows
    factor = 1.0 / math.sqrt(HEAD_DIM)
    sums_ref[...] = jnp.zeros_like(sums_ref)
    acc[...] = jnp.zeros_like(acc)
    greet(line.peers() + window_targets(hops))
    back_pass.clear()
    step = line.step

    def start(c):
        project_into(line, c, act_ref[first + c * step : first + (c + 1) * step, :], wr_ref)

    def end(c):
        middle = mid_ref[first + c * step : first + (c + 1) * step, :]
        hidden_ref[c * step : (c + 1) * step, :] = middle + (line.take(c) + bias_ref[0:1, :])

    stages = [start, line.join, line.finish, end]

    def line_step(t):
        for lag, stage in enumerate(stages):
            if 0 <= t - lag < chunks:
                stage(t - lag)

    groups = [(base, group) for base, group, inner in head_parts(width) if inner == 0]
    lines_done = 0
    for order, (base, group) in enumerate(groups):
        cols = slice(base, base + group)
        value_cols = slice(width + base, width + base + group)
        for start_row, tile, low, high in row_tiles(rows, window_rows):
            line_step(lines_done)
            lines_done += 1
            allowed = tile_mask(own_ref, window_ref, start_row, tile, low, high, back)
            at = slice(start_row, start_row + tile)
            held = None
            for inner in range(0, group, HEAD_DIM):
                index = (base + inner) // HEAD_DIM
                queries = pick(q_ref[at, cols], inner)
                cots = pick(cot_ref[at, cols], inner)
                keys = kv_ref[low:high, cols]
                values = kv_ref[low:high, value_cols]
                logs = lse_ref[at, index : index + 1]
                scores = dot_rows(queries, keys) * factor
                probabilities = jnp.where(allowed, jnp.exp(scores - logs), 0.0)
                rounded = probabilities.astype(jnp.bfloat16)
                acc[low:high, value_cols] += dot_tokens(rounded, cots)
                prob_cot = dot_rows(cots, values)
                inner_sum = jnp.sum(probabilities * prob_cot, axis=-1, keepdims=True)
                score_cot = (probabilities * (prob_cot - inner_sum) * factor).astype(jnp.bfloat16)
                acc[low:high, cols] += dot_tokens(score_cot, queries)
                part = pick(jnp.dot(score_cot, keys, preferred_element_type=jnp.float32), inner)
                held = part if held is None else held + part
            sums_ref[0:1, cols] += jnp.sum(held, axis=0, keepdims=True)
            dproj_ref[at, cols] = held.astype(jnp.bfloat16)
        for piece, part_cols in enumerate((cols, value_cols)):
            back_pass.out[:, part_cols] = acc[:back, part_cols].astype(jnp.bfloat16)
            back_pass.start(2 * order + piece, part_cols)

    line_step(lines_done)
    grad_blocks(a2_ref, dfb_ref, expand_ref)
    line_step(lines_done + 1)
    grad_blocks(u_ref, eb_ref, reduce_ref)
    line_step(lines_done + 2)
    grad_blocks(o_ref, db_ref, output_ref)
    for extra in range(lines_done + 3, chunks + 3):
        line_step(extra)
    for order, (base, group) in enumerate(groups):
        for piece, part_base in enumerate((base, width + base)):
            part_cols = slice(part_base, part_base + group)
            total = acc[back:, part_cols] + back_pass.take(2 * order + piece, part_cols)
            if piece == 1:
                sums_ref[1:2, base : base + group] = jnp.sum(total, axis=0, keepdims=True)
            dproj_ref[:, width + part_base : width + part_base + group] = total.astype(
                jnp.bfloat16
            )
    grad_blocks(a1_ref, dproj_ref, attend_ref)
    for c in range(chunks):
        line.drain(c)
    for order, (base, group) in enumerate(groups):
        for piece, part_base in enumerate((base, width + base)):
            back_pass.drain(2 * order + piece, slice(part_base, part_base + group))


RETURN_CHUNKS = 4


def return_call(name, number, first, hops, args):
    q, window, a2, dfb, o, a1 = args[0], args[1], args[6], args[7], args[10], args[12]
    rows, width = q.shape
    model, units = a2.shape[1], dfb.shape[1]
    count = rows // 2
    bf16, f32 = jnp.bfloat16, jnp.float32
    out_shapes = [
        ((rows, 3 * width), bf16),
        ((8, width), f32),
        ((model, units), bf16),
        ((units, model), bf16),
        ((width, model), bf16),
        ((model, 3 * width), bf16),
        ((count, model), f32),
    ]
    return pl.pallas_call(
        functools.partial(return_kernel, RETURN_CHUNKS, first, hops),
        out_shape=tuple(jax.ShapeDtypeStruct(shape, kind) for shape, kind in out_shapes),
        in_specs=in_vmem(len(args)),
        out_specs=tuple(in_vmem(len(out_shapes))),
        scratch_shapes=[
            pltpu.VMEM((window.shape[0], 2 * width), f32),
            *LineTotal.scratch(count, model, RETURN_CHUNKS),
            *WindowBack.scratch(hops, rows, 2 * width, 2 * max(1, width // LANES)),
        ],
        compiler_params=pltpu.CompilerParams(
            collective_id=number, has_side_effects=True, vmem_limit_bytes=56 * MEGA
        ),
        name=name,
    )(*args)


def head_call(hidden_in, small, weights, shards, width, hops):
    rows, model = hidden_in.shape
    size, groups = lax.axis_size("dp"), lax.axis_size("tensor")
    outs = [((size * w.shape[0], w.shape[1]), w.dtype) for w in (small, *weights)] + [
        ((groups, width, model), jnp.bfloat16),
        ((groups, *shards.shape), jnp.bfloat16),
        ((rows, model), jnp.bfloat16),
        ((rows, width), jnp.bfloat16),
        (((hops + 1) * rows, 2 * width), jnp.bfloat16),
    ]
    return pl.pallas_call(
        functools.partial(head_kernel, hops),
        out_shape=tuple(jax.ShapeDtypeStruct(shape, kind) for shape, kind in outs),
        in_specs=in_vmem(3 + len(weights)),
        out_specs=tuple(in_vmem(len(outs))),
        scratch_shapes=LineGather.scratch(1)
        + Gather.scratch() * (4 + groups)
        + Window.scratch(hops, 4),
        compiler_params=pltpu.CompilerParams(
            collective_id=5, has_side_effects=True, vmem_limit_bytes=40 * MEGA
        ),
        name="head",
    )(hidden_in, small, *weights, shards)


def pair_layers(hidden_in, out_grad, shards, small_in, doc_marks, reach_back, model_parts):
    share, unit_share, size, part = model_parts
    bf16, f32 = jnp.bfloat16, jnp.float32
    rows, model = hidden_in.shape
    attend_weight, output_weight, expand_weight, reduce_weight = shards
    width, units = attend_weight.shape[3], expand_weight.shape[2]
    extra = (rows, model)

    def shards_of(layer):
        return (
            attend_weight[layer].reshape(part, 3 * width),
            expand_weight[layer],
            reduce_weight[layer],
        )

    def proj_bias(bias):
        return jnp.concatenate([bias[0], jnp.zeros_like(bias[0]), bias[1]])

    groups = lax.axis_size("tensor")
    line_gather_scratch = [pltpu.VMEM((groups, rows, width), bf16), *LineGather.scratch(CHUNKS)]
    out_shards = output_weight.reshape(2 * share, model)
    small_all, aw0, ew0, rw0, ow0, line_shards, a1_0, q_0, window_0 = head_call(
        hidden_in,
        pack_small(small_in, doc_marks, width),
        shards_of(0),
        out_shards,
        width,
        reach_back,
    )
    attend_b, (br0, br1), (eb0, eb1), (g0, g1), (c0, c1), marks = unpack_small(
        small_all, rows, width, reach_back
    )
    o_0, lse_0 = attend_forward(q_0, window_0, marks[0], marks[1])

    vec = stack_rows(
        model, [br0[0], g0[1], c0[1], eb0, br0[1], g1[0], c1[0], proj_bias(attend_b[1])]
    )
    mid_0, a2_0, f_0, u_0, h_1, a1_1, q_1, window_1, aw1, ew1, rw1, ow1 = line_call(
        first_kernel,
        "first_tail",
        1,
        [
            ((rows, model), f32),
            ((rows, model), bf16),
            ((rows, units), f32),
            ((rows, units), bf16),
            ((rows, model), f32),
            ((rows, model), bf16),
            ((rows, width), bf16),
            (((reach_back + 1) * rows, 2 * width), bf16),
            ((model, 3 * width), bf16),
            ((model, units), bf16),
            ((units, model), bf16),
            ((groups, width, model), bf16),
        ],
        extra,
        (0, 1),
        50,
        (o_0, ow0, hidden_in, vec, ew0, rw0, *shards_of(1), line_shards),
        line_gather_scratch
        + Gather.scratch() * (3 + groups)
        + Window.scratch(reach_back, CHUNKS),
    )
    o_1, lse_1 = attend_forward(q_1, window_1, marks[0], marks[1])

    vec = stack_rows(model, [br1[0], g1[1], c1[1], eb1, br1[1]])
    a2_1, u_1, eb_1, dfb_1, dmid_1, db_1, do_1, mid_1, sums_1 = line_call(
        turn_kernel,
        "turn_tail",
        2,
        [
            ((rows, model), bf16),
            ((rows, units), bf16),
            ((rows, model), bf16),
            ((rows, units), bf16),
            ((rows, model), f32),
            ((rows, model), bf16),
            ((rows, width), bf16),
            ((rows, model), f32),
            ((8, model), f32),
        ],
        extra,
        (0, 1),
        60,
        (o_1, ow1, h_1, vec, ew1, rw1, out_grad),
        line_gather_scratch,
    )
    last_sum = (u_1, rw1, mid_1, stack_rows(model, [br1[1]]))
    dproj_1, attend_bias_1, expand_1, reduce_1, output_1, attend_1, low_out = return_call(
        "return_one",
        6,
        0,
        reach_back,
        (q_1, window_1, lse_1, do_1, *marks, a2_1, dfb_1, u_1, eb_1, o_1, db_1, a1_1, *last_sum),
    )
    grads_1 = (expand_1, reduce_1, attend_1, output_1)
    owned = [((g.shape[0] // size, g.shape[1]), f32) for g in grads_1]

    def scatter_scratch(pieces):
        return sum((Scatter.scratch(*shape) for shape, kind in pieces), [])

    vec = stack_rows(model, [g1[0], g0[1]])
    eb_0, dfb_0, dmid_0, db_0, do_0, sums_0, *sums_of_1 = line_call(
        cross_kernel,
        "cross_tail",
        3,
        [
            ((rows, model), bf16),
            ((rows, units), bf16),
            ((rows, model), f32),
            ((rows, model), bf16),
            ((rows, width), bf16),
            ((8, model), f32),
            *owned,
        ],
        extra,
        (1, 2),
        60,
        (dproj_1, aw1, h_1, dmid_1, vec, f_0, mid_0, ew0, rw0, ow0, *grads_1),
        scatter_scratch(owned),
    )
    dproj_0, attend_bias_0, expand_0, reduce_0, output_0, attend_0, high_out = return_call(
        "return_zero",
        7,
        rows // 2,
        reach_back,
        (q_0, window_0, lse_0, do_0, *marks, a2_0, dfb_0, u_0, eb_0, o_0, db_0, a1_0, *last_sum),
    )
    hidden_out = jnp.concatenate([low_out, high_out], axis=0)
    zero = jnp.zeros((model,), f32)
    wide = [
        sums_0[6], sums_0[2], sums_1[4], sums_1[0],
        sums_0[3], sums_1[1],
        zero, sums_0[4], sums_0[0], sums_1[2],
        zero, sums_0[5], sums_0[1], sums_1[3],
    ]
    wide = jnp.stack(wide).reshape(len(wide), size, LANES)
    narrow = jnp.concatenate([attend_bias_0[:2], attend_bias_1[:2]]).reshape(4, size, width // size)
    narrow = jnp.moveaxis(narrow, 1, 0).reshape(size, 1, LANES)
    small = jnp.concatenate([narrow, jnp.moveaxis(wide, 1, 0)], axis=1).astype(bf16)
    small = jnp.pad(small, ((0, 0), (0, SMALL_ROWS - small.shape[1]), (0, 0)))
    grads_0 = (expand_0, reduce_0, attend_0, output_0, small.reshape(-1, LANES))
    owned = [((g.shape[0] // size, g.shape[1]), f32) for g in grads_0]

    vec = stack_rows(model, [g0[0]])
    in_grad, late, unused, *sums_of_0 = line_call(
        last_kernel,
        "last_tail",
        4,
        [((rows, model), f32), ((8, LANES), f32), ((8, model), f32), *owned],
        extra,
        (0, 1),
        30,
        (dproj_0, aw0, hidden_in, dmid_0, vec, *grads_0),
        [
            pltpu.VMEM((size, 8, LANES), f32),
            pltpu.VMEM((size, 8, LANES), f32),
            pltpu.SemaphoreType.DMA((size,)),
            pltpu.SemaphoreType.DMA((size,)),
            *scatter_scratch(owned),
        ],
    )
    small = sums_of_0[4]
    expand, reduced, attend, output = [jnp.stack(pair) for pair in zip(sums_of_0[:4], sums_of_1)]
    pieces = [small[1 + i : 1 + i + n] for i, n in ((0, 4), (4, 2), (6, 4), (10, 4))]
    branch, units_grad, gain, offset = pieces
    return (
        hidden_out,
        in_grad,
        attend.reshape(2, part, 3, width),
        small[0].reshape(2, 2, width // size),
        output,
        branch.reshape(2, 2, LANES),
        expand,
        units_grad,
        reduced,
        jnp.concatenate([late[0:1], gain[1:]]).reshape(2, 2, LANES),
        jnp.concatenate([late[1:2], offset[1:]]).reshape(2, 2, LANES),
    )


def layer_by_layer(hidden_in, out_grad, params, marks, reach_back, model_parts):
    share, unit_share, size, part = model_parts
    model = hidden_in.shape[1]
    saved = []
    current = hidden_in
    for layer in range(len(params)):
        current, kept_state = forward_layer(current, params[layer], marks, reach_back)
        saved.append(kept_state)
    grad_now = out_grad
    hidden_list = [None] * len(params)
    attend_list = [None] * len(params)
    small_list = [None] * len(params)
    for layer in reversed(range(len(params))):
        grad_now, expand_grad, reduce_grad, attend_grad, output_grad, small = backward_layer(
            grad_now, params[layer], saved[layer], marks, reach_back
        )
        hidden_list[layer] = scattered(
            jnp.concatenate([expand_grad, pack_output(reduce_grad, model, unit_share)], axis=1)
        )
        small_list[layer] = small
        blocks = [attend_grad, pack_output(output_grad, model, share)]
        if layer == 0:
            stacked = [jnp.stack([entry[i] for entry in small_list]) for i in range(len(small))]
            flat_rows = split_owned(stacked, None, size).astype(jnp.bfloat16)
            count = flat_rows.shape[1]
            room = part * LANES * (-(-count // (part * LANES)))
            padded = jnp.pad(flat_rows, ((0, 0), (0, room - count)))
            blocks.append(padded.reshape(size * part, room // part))
        packed = jnp.concatenate(blocks, axis=1)
        if layer > 0:
            grad_now, packed = lax.optimization_barrier((grad_now, packed))
        attend_list[layer] = scattered(packed)
    return current, grad_now, hidden_list, attend_list


def local(
    hidden_in,
    doc_ids,
    attend_weight,
    attend_bias,
    output_weight,
    branch_bias,
    expand_weight,
    expand_bias,
    reduce_weight,
    norm_gain,
    norm_bias,
    out_grad,
):
    size = lax.axis_size("dp")
    layer_count, part, three, width = attend_weight.shape
    tok_rows, model = hidden_in.shape
    share = output_weight.shape[1]
    unit_share = reduce_weight.shape[1]
    hidden_units = expand_weight.shape[2]
    reach_back = (CTX + tok_rows - 2) // tok_rows
    own_row = doc_ids + 1
    small_in = (attend_bias, branch_bias, expand_bias, norm_gain, norm_bias)
    on_cube = size == 8 and lax.axis_size("tensor") == 4 and layer_count == 2
    if on_cube and part == unit_share == LANES and tok_rows == 4 * LANES and width == 2 * LANES:
        return pair_layers(
            hidden_in,
            out_grad,
            (attend_weight, output_weight, expand_weight, reduce_weight),
            small_in,
            own_row,
            reach_back,
            (share, unit_share, size, part),
        )
    else:
        mark_list = [passed_along(own_row, "dp", hop) for hop in range(reach_back, 0, -1)]
        marks = (own_row[:, None], jnp.concatenate(mark_list + [own_row])[None, :])
        flat = jnp.concatenate([entry.reshape(-1) for entry in small_in])
        flat_all = lax.all_gather(flat[None], "dp", axis=0, tiled=True)
        small_full = []
        at = 0
        for entry in small_in:
            piece = flat_all[:, at : at + entry.size].reshape((size,) + entry.shape)
            at += entry.size
            piece = jnp.moveaxis(piece, 0, -2)
            small_full.append(
                piece.reshape(entry.shape[:-1] + (size * entry.shape[-1],)).astype(jnp.float32)
            )
        attend_b, branches, expand_b, gains, offsets = small_full

        params = []
        for layer in range(layer_count):
            first = lax.all_gather(
                jnp.concatenate(
                    [
                        attend_weight[layer].reshape(part, three * width),
                        pack_output(output_weight[layer], model, share),
                    ],
                    axis=1,
                ),
                "dp",
                axis=0,
                tiled=True,
            )
            second = lax.all_gather(
                jnp.concatenate(
                    [expand_weight[layer], pack_output(reduce_weight[layer], model, unit_share)],
                    axis=1,
                ),
                "dp",
                axis=0,
                tiled=True,
            )
            params.append(
                (
                    first[:, : three * width],
                    attend_b[layer],
                    unpack_output(first[:, three * width :], model, share),
                    branches[layer],
                    second[:, :hidden_units],
                    expand_b[layer],
                    unpack_output(second[:, hidden_units:], model, unit_share),
                    gains[layer],
                    offsets[layer],
                )
            )
        current, grad_now, hidden_list, attend_list = layer_by_layer(
            hidden_in, out_grad, params, marks, reach_back, (share, unit_share, size, part)
        )
    hidden_out = [entry.astype(jnp.float32) for entry in hidden_list]
    attend_out = [entry.astype(jnp.float32) for entry in attend_list]
    fold = three * width
    slab = model * share // part
    tail = attend_out[0][:, fold + slab :].reshape(-1)
    small_out = []
    at = 0
    for entry in small_in:
        small_out.append(tail[at : at + entry.size].reshape(entry.shape))
        at += entry.size
    attend_bgrad, branch_bgrad, expand_bgrad, gain_grad, offset_grad = small_out
    return (
        current,
        grad_now,
        jnp.stack([entry[:, :fold].reshape(part, three, width) for entry in attend_out]),
        attend_bgrad,
        jnp.stack([unpack_output(entry[:, fold : fold + slab], model, share) for entry in attend_out]),
        branch_bgrad,
        jnp.stack([entry[:, :hidden_units] for entry in hidden_out]),
        expand_bgrad,
        jnp.stack(
            [unpack_output(entry[:, hidden_units:], model, unit_share) for entry in hidden_out]
        ),
        gain_grad,
        offset_grad,
    )


def solution(mesh):
    return jax.shard_map(
        local,
        mesh=mesh,
        in_specs=(
            P("dp", None),
            P("dp"),
            P(None, "dp", None, "tensor"),
            P(None, None, ("tensor", "dp")),
            P(None, ("tensor", "dp"), None),
            P(None, None, "dp"),
            P(None, "dp", "tensor"),
            P(None, ("tensor", "dp")),
            P(None, ("tensor", "dp"), None),
            P(None, None, "dp"),
            P(None, None, "dp"),
            P("dp", None),
        ),
        out_specs=(
            P("dp", None),
            P("dp", None),
            P(None, "dp", None, "tensor"),
            P(None, None, ("tensor", "dp")),
            P(None, ("tensor", "dp"), None),
            P(None, None, "dp"),
            P(None, "dp", "tensor"),
            P(None, ("tensor", "dp")),
            P(None, ("tensor", "dp"), None),
            P(None, None, "dp"),
            P(None, None, "dp"),
        ),
        check_vma=False,
    )
```

```python
import functools
import math

import jax
import jax.numpy as jnp
from jax import lax
from jax.experimental import pallas as pl
from jax.experimental.pallas import tpu as pltpu
from jax.sharding import PartitionSpec as P

HEAD_DIM = 64
CTX = 1024
LANES = 128
ROW_TILE = 256


def passed_along(block, axis, distance):
    devices = range(lax.axis_size(axis))
    route = [(i - distance, i) for i in devices if i - distance in devices]
    return lax.ppermute(block, axis, route)


def contract(pattern, left_side, right_side):
    return jnp.einsum(pattern, left_side, right_side, preferred_element_type=jnp.float32)


def layer_norm(values, gain_row, offset_row):
    center = values - jnp.mean(values, axis=-1, keepdims=True)
    spread = jnp.mean(center * center, axis=-1, keepdims=True)
    return center * lax.rsqrt(spread + 1e-05) * gain_row + offset_row


def gelu_tanh(values):
    return (
        0.5
        * values
        * (1.0 + jnp.tanh(0.7978845608028654 * (values + 0.044715 * values * values * values)))
    )


def dot_rows(left_side, right_side):
    return lax.dot_general(
        left_side, right_side, (((1,), (1,)), ((), ())), preferred_element_type=jnp.float32
    )


def dot_tokens(left_side, right_side):
    return lax.dot_general(
        left_side, right_side, (((0,), (0,)), ((), ())), preferred_element_type=jnp.float32
    )


def row_tiles(rows, window_rows):
    tile = min(ROW_TILE, rows)
    back = window_rows - rows
    for start in range(0, rows, tile):
        low = max(0, (back + start - CTX + 1) // LANES * LANES)
        yield start, tile, low, back + start + tile


def tile_mask(own_ref, window_ref, start, tile, low, high, back):
    own = own_ref[start : start + tile, :]
    window = window_ref[:, low:high]
    row = lax.broadcasted_iota(jnp.int32, (tile, high - low), 0) + (start + back)
    col = lax.broadcasted_iota(jnp.int32, (tile, high - low), 1) + low
    return (window == own) & (col <= row)


def head_parts(width):
    group = min(LANES, width)
    for base in range(0, width, group):
        for inner in range(0, group, HEAD_DIM):
            yield base, group, inner


def pick(block, inner):
    lane = lax.broadcasted_iota(jnp.int32, block.shape, 1)
    return jnp.where((lane >= inner) & (lane < inner + HEAD_DIM), block, jnp.zeros_like(block))


def forward_kernel(q_ref, kv_ref, own_ref, window_ref, o_ref, lse_ref):
    rows, width = q_ref.shape
    window_rows = kv_ref.shape[0]
    back = window_rows - rows
    factor = 1.0 / math.sqrt(HEAD_DIM)
    for start, tile, low, high in row_tiles(rows, window_rows):
        allowed = tile_mask(own_ref, window_ref, start, tile, low, high, back)
        held = None
        logs = []
        for base, group, inner in head_parts(width):
            queries = pick(q_ref[start : start + tile, base : base + group], inner)
            keys = kv_ref[low:high, base : base + group]
            values = kv_ref[low:high, width + base : width + base + group]
            unnormed = jnp.where(allowed, jnp.exp(dot_rows(queries, keys) * factor), 0.0)
            totals = jnp.sum(unnormed, axis=-1, keepdims=True)
            probabilities = (unnormed * (1.0 / totals)).astype(jnp.bfloat16)
            context = pick(
                jnp.dot(probabilities, values, preferred_element_type=jnp.float32), inner
            )
            held = context if inner == 0 else held + context
            logs.append(jnp.log(totals))
            if inner + HEAD_DIM == group:
                o_ref[start : start + tile, base : base + group] = held.astype(jnp.bfloat16)
        for index, entry in enumerate(logs):
            lse_ref[start : start + tile, index : index + 1] = entry


def backward_kernel(
    q_ref, kv_ref, lse_ref, cot_ref, own_ref, window_ref, dq_ref, own_out, back_out, acc
):
    rows, width = q_ref.shape
    window_rows = kv_ref.shape[0]
    back = window_rows - rows
    factor = 1.0 / math.sqrt(HEAD_DIM)
    acc[...] = jnp.zeros_like(acc)
    for start, tile, low, high in row_tiles(rows, window_rows):
        allowed = tile_mask(own_ref, window_ref, start, tile, low, high, back)
        held = None
        for index, (base, group, inner) in enumerate(head_parts(width)):
            queries = pick(q_ref[start : start + tile, base : base + group], inner)
            cots = pick(cot_ref[start : start + tile, base : base + group], inner)
            keys = kv_ref[low:high, base : base + group]
            values = kv_ref[low:high, width + base : width + base + group]
            logs = lse_ref[start : start + tile, index : index + 1]
            scores = dot_rows(queries, keys) * factor
            probabilities = jnp.where(allowed, jnp.exp(scores - logs), 0.0)
            rounded = probabilities.astype(jnp.bfloat16)
            acc[low:high, width + base : width + base + group] += dot_tokens(rounded, cots)
            prob_cot = dot_rows(cots, values)
            inner_sum = jnp.sum(probabilities * prob_cot, axis=-1, keepdims=True)
            score_cot = (probabilities * (prob_cot - inner_sum) * factor).astype(jnp.bfloat16)
            acc[low:high, base : base + group] += dot_tokens(score_cot, queries)
            part = pick(jnp.dot(score_cot, keys, preferred_element_type=jnp.float32), inner)
            held = part if inner == 0 else held + part
            if inner + HEAD_DIM == group:
                dq_ref[start : start + tile, base : base + group] = held
    own_out[...] = acc[back:, :]
    back_out[...] = acc[:back, :].astype(jnp.bfloat16)


def in_vmem(count):
    return [pl.BlockSpec(memory_space=pltpu.VMEM)] * count


def attend_forward(queries, window_kv, own_marks, window_marks):
    rows, width = queries.shape
    return pl.pallas_call(
        forward_kernel,
        out_shape=(
            jax.ShapeDtypeStruct((rows, width), jnp.bfloat16),
            jax.ShapeDtypeStruct((rows, width // HEAD_DIM), jnp.float32),
        ),
        in_specs=in_vmem(4),
        out_specs=tuple(in_vmem(2)),
        compiler_params=pltpu.CompilerParams(vmem_limit_bytes=40 * 1024 * 1024),
        name="attend_forward",
    )(queries, window_kv, own_marks, window_marks)


def attend_backward(queries, window_kv, log_totals, out_cot, own_marks, window_marks):
    rows, width = queries.shape
    window_rows = window_kv.shape[0]
    return pl.pallas_call(
        backward_kernel,
        out_shape=(
            jax.ShapeDtypeStruct((rows, width), jnp.float32),
            jax.ShapeDtypeStruct((rows, 2 * width), jnp.float32),
            jax.ShapeDtypeStruct((window_rows - rows, 2 * width), jnp.bfloat16),
        ),
        in_specs=in_vmem(6),
        out_specs=tuple(in_vmem(3)),
        scratch_shapes=[pltpu.VMEM((window_rows, 2 * width), jnp.float32)],
        compiler_params=pltpu.CompilerParams(vmem_limit_bytes=48 * 1024 * 1024),
        name="attend_backward",
    )(queries, window_kv, log_totals, out_cot, own_marks, window_marks)


def line_kernel(chunks, x_ref, o_ref, from_near, from_mid, pair, total, near_send, mid_send, near_recv, mid_recv):
    place = lax.axis_index("tensor")
    near = place + 1 - 2 * lax.rem(place, 2)
    across = 3 - place
    is_end = (place == 0) | (place == 3)
    is_mid = (place == 1) | (place == 2)
    step = x_ref.shape[0] // chunks
    barrier = pltpu.get_barrier_semaphore()

    def part(ref, c):
        return ref.at[pl.ds(c * step, step)]

    def to_near(src, c):
        return pltpu.make_async_remote_copy(
            src_ref=part(src, c),
            dst_ref=part(from_near, c),
            send_sem=near_send.at[c],
            recv_sem=near_recv.at[c],
            device_id={"tensor": near},
            device_id_type=pl.DeviceIdType.MESH,
        )

    def to_mid(c):
        return pltpu.make_async_remote_copy(
            src_ref=part(pair, c),
            dst_ref=part(from_mid, c),
            send_sem=mid_send.at[c],
            recv_sem=mid_recv.at[c],
            device_id={"tensor": across},
            device_id_type=pl.DeviceIdType.MESH,
        )

    def added(left, right, c):
        rows = pl.ds(c * step, step)
        both = left[rows, :].astype(jnp.float32) + right[rows, :].astype(jnp.float32)
        return both.astype(jnp.bfloat16)

    pl.semaphore_signal(
        barrier, inc=1, device_id={"tensor": near}, device_id_type=pl.DeviceIdType.MESH
    )

    @pl.when(is_end)
    def _():
        pl.semaphore_wait(barrier, 1)
        for c in range(chunks):
            to_near(x_ref, c).start()
        for c in range(chunks):
            to_near(x_ref, c).wait_recv()
            rows = pl.ds(c * step, step)
            o_ref[rows, :] = from_near[rows, :]
        for c in range(chunks):
            to_near(x_ref, c).wait_send()

    @pl.when(is_mid)
    def _():
        pl.semaphore_signal(
            barrier, inc=1, device_id={"tensor": across}, device_id_type=pl.DeviceIdType.MESH
        )
        pl.semaphore_wait(barrier, 2)
        lag = 2
        for c in range(chunks + lag):
            if c < chunks:
                to_near(total, c).wait_recv()
                pair[pl.ds(c * step, step), :] = added(x_ref, from_near, c)
                to_mid(c).start()
            done = c - lag
            if done >= 0:
                to_mid(done).wait_recv()
                result = added(pair, from_mid, done)
                total[pl.ds(done * step, step), :] = result
                to_near(total, done).start()
                o_ref[pl.ds(done * step, step), :] = result
        for c in range(chunks):
            to_mid(c).wait_send()
            to_near(total, c).wait_send()


def tensor_total(partial_value):
    rounded = partial_value.astype(jnp.bfloat16)
    rows = rounded.shape[0]
    if lax.axis_size("tensor") != 4 or rows % 128:
        return lax.psum(rounded, "tensor").astype(jnp.float32)
    chunks = 8
    block = pltpu.VMEM(rounded.shape, jnp.bfloat16)
    summed = pl.pallas_call(
        functools.partial(line_kernel, chunks),
        out_shape=jax.ShapeDtypeStruct(rounded.shape, jnp.bfloat16),
        in_specs=in_vmem(1),
        out_specs=in_vmem(1)[0],
        scratch_shapes=[block] * 4 + [pltpu.SemaphoreType.DMA((chunks,))] * 4,
        compiler_params=pltpu.CompilerParams(
            collective_id=0, has_side_effects=True, vmem_limit_bytes=24 * 1024 * 1024
        ),
        name="line_total",
    )(rounded)
    return summed.astype(jnp.float32)


def forward_layer(hidden, params, marks, reach_back):
    attend_w, attend_b, output_w, branches, expand_w, expand_b, reduce_w, gains, offsets = params
    width = output_w.shape[0]
    own_marks, window_marks = marks
    normed_one = layer_norm(hidden, gains[0], offsets[0]).astype(jnp.bfloat16)
    projected = jnp.dot(normed_one, attend_w, preferred_element_type=jnp.float32)
    queries = (projected[:, :width] + attend_b[0]).astype(jnp.bfloat16)
    kv_bias = jnp.concatenate([jnp.zeros_like(attend_b[1]), attend_b[1]])
    kv_now = (projected[:, width:] + kv_bias).astype(jnp.bfloat16)
    kv_list = [passed_along(kv_now, "dp", hop) for hop in range(reach_back, 0, -1)]
    window_kv = jnp.concatenate(kv_list + [kv_now], axis=0)
    context, log_totals = attend_forward(queries, window_kv, own_marks, window_marks)
    attended = tensor_total(jnp.dot(context, output_w, preferred_element_type=jnp.float32))
    middle = hidden + (attended + branches[0])
    normed_two = layer_norm(middle, gains[1], offsets[1]).astype(jnp.bfloat16)
    pre_act = jnp.dot(normed_two, expand_w, preferred_element_type=jnp.float32) + expand_b
    activated = gelu_tanh(pre_act).astype(jnp.bfloat16)
    reduced = tensor_total(jnp.dot(activated, reduce_w, preferred_element_type=jnp.float32))
    output = middle + (reduced + branches[1])
    kept_state = (
        hidden,
        normed_one,
        queries,
        window_kv,
        context,
        log_totals,
        middle,
        normed_two,
        pre_act,
        activated,
    )
    return (output, kept_state)


def backward_layer(grad_out, params, kept_state, marks, reach_back):
    attend_w, attend_b, output_w, branches, expand_w, expand_b, reduce_w, gains, offsets = params
    (
        hidden,
        normed_one,
        queries,
        window_kv,
        context,
        log_totals,
        middle,
        normed_two,
        pre_act,
        activated,
    ) = kept_state
    own_marks, window_marks = marks
    rows = hidden.shape[0]
    width = output_w.shape[0]
    bias_two = jnp.sum(grad_out, axis=0)
    grad_rounded = grad_out.astype(jnp.bfloat16)
    act_cot = contract("td,fd->tf", grad_rounded, reduce_w)
    unused, gelu_pull = jax.vjp(gelu_tanh, pre_act)
    pre_cot = gelu_pull(act_cot)[0]
    expand_bias_grad = jnp.sum(pre_cot, axis=0)
    pre_rounded = pre_cot.astype(jnp.bfloat16)
    normed_cot = tensor_total(contract("tf,df->td", pre_rounded, expand_w))
    reduce_grad = contract("tf,td->fd", activated, grad_rounded).astype(jnp.bfloat16)
    expand_grad = contract("td,tf->df", normed_two, pre_rounded).astype(jnp.bfloat16)
    unused, norm_pull = jax.vjp(layer_norm, middle, gains[1], offsets[1])
    mid_part, gain_two, offset_two = norm_pull(normed_cot)
    mid_cot = grad_out + mid_part
    bias_one = jnp.sum(mid_cot, axis=0)
    mid_rounded = mid_cot.astype(jnp.bfloat16)
    output_grad = contract("tk,td->kd", context, mid_rounded).astype(jnp.bfloat16)
    context_cot = contract("td,kd->tk", mid_rounded, output_w).astype(jnp.bfloat16)
    context_cot, expand_grad, reduce_grad = lax.optimization_barrier(
        (context_cot, expand_grad, reduce_grad)
    )
    query_cot, kv_own, kv_back = attend_backward(
        queries, window_kv, log_totals, context_cot, own_marks, window_marks
    )
    for hop in range(1, reach_back + 1):
        begin = (reach_back - hop) * rows
        kv_own = kv_own + passed_along(kv_back[begin : begin + rows], "dp", -hop).astype(
            jnp.float32
        )
    attend_bias_grad = jnp.stack([jnp.sum(query_cot, axis=0), jnp.sum(kv_own[:, width:], axis=0)])
    proj_rounded = jnp.concatenate(
        [query_cot.astype(jnp.bfloat16), kv_own.astype(jnp.bfloat16)], axis=1
    )
    normed_cot_one = tensor_total(contract("tc,dc->td", proj_rounded, attend_w))
    attend_grad = contract("td,tc->dc", normed_one, proj_rounded).astype(jnp.bfloat16)
    unused, first_pull = jax.vjp(layer_norm, hidden, gains[0], offsets[0])
    hid_part, gain_one, offset_one = first_pull(normed_cot_one)
    in_cot = mid_cot + hid_part
    small = (
        attend_bias_grad,
        jnp.stack([bias_one, bias_two]),
        expand_bias_grad,
        jnp.stack([gain_one, gain_two]),
        jnp.stack([offset_one, offset_two]),
    )
    return (in_cot, expand_grad, reduce_grad, attend_grad, output_grad, small)


def scattered(block):
    return lax.psum_scatter(block, "dp", scatter_dimension=0, tiled=True)


def pack_output(block, model, share):
    part = model // lax.axis_size("dp")
    slabs = part // share
    owners = block.shape[0] // share
    return (
        block.reshape(owners, share, slabs, model // slabs)
        .transpose(0, 2, 1, 3)
        .reshape(owners * part, model // slabs)
    )


def unpack_output(block, model, share):
    part = model // lax.axis_size("dp")
    slabs = part // share
    owners = block.shape[0] // part
    return (
        block.reshape(owners, slabs, share, model // slabs)
        .transpose(0, 2, 1, 3)
        .reshape(owners * share, model)
    )


def split_owned(pieces, sizes, size):
    rows = [
        jnp.moveaxis(p.reshape(p.shape[:-1] + (size, p.shape[-1] // size)), -2, 0).reshape(size, -1)
        for p in pieces
    ]
    return jnp.concatenate(rows, axis=1)


GELU_SCALE = 0.7978845608028654
GELU_CUBIC = 0.044715
COLUMNS = 256


def column_blocks(width):
    size = min(COLUMNS, width)
    return [slice(start, start + size) for start in range(0, width, size)]


def norm_parts(values):
    center = values - jnp.mean(values, axis=-1, keepdims=True)
    inverse = lax.rsqrt(jnp.mean(center * center, axis=-1, keepdims=True) + 1e-05)
    return center * inverse, inverse


def norm_rows(values, gain_row, offset_row):
    return norm_parts(values)[0] * gain_row + offset_row


def norm_back(values, gain_row, cot):
    normal, inverse = norm_parts(values)
    scaled = cot * gain_row
    mean_one = jnp.mean(scaled, axis=-1, keepdims=True)
    mean_two = jnp.mean(scaled * normal, axis=-1, keepdims=True)
    return inverse * (scaled - mean_one - normal * mean_two), cot * normal


def gelu_value(values):
    bent = jnp.tanh(GELU_SCALE * (values + GELU_CUBIC * values * values * values))
    return 0.5 * values * (1.0 + bent), bent


def gelu_slope(values, bent):
    inner = GELU_SCALE * (1.0 + 3.0 * GELU_CUBIC * values * values)
    return 0.5 * (1.0 + bent) + 0.5 * values * (1.0 - bent * bent) * inner


class LineTotal:
    scratch_count = 7

    @staticmethod
    def scratch(rows, model, chunks):
        block = pltpu.VMEM((rows, model), jnp.bfloat16)
        return [block] * 3 + [pltpu.SemaphoreType.DMA((chunks * SPLIT,))] * 4

    def __init__(self, refs, chunks):
        self.own, self.near_buf, self.mid_buf = refs[:3]
        self.near_send, self.near_recv, self.mid_send, self.mid_recv = refs[3:]
        self.chunks = chunks
        self.step = self.own.shape[0] // chunks
        self.piece = self.step // SPLIT
        place = lax.axis_index("tensor")
        self.near = place + 1 - 2 * lax.rem(place, 2)
        self.across = 3 - place
        self.is_end = (place == 0) | (place == 3)
        self.is_mid = (place == 1) | (place == 2)

    def rows(self, c):
        return pl.ds(pl.multiple_of(c * self.step, self.step), self.step)

    def piece_rows(self, i):
        return pl.ds(pl.multiple_of(i * self.piece, self.piece), self.piece)

    def pieces(self, c):
        return [c * SPLIT + j for j in range(SPLIT)]

    def to_near(self, src, c):
        return pltpu.make_async_remote_copy(
            src_ref=src.at[self.piece_rows(c)],
            dst_ref=self.near_buf.at[self.piece_rows(c)],
            send_sem=self.near_send.at[c],
            recv_sem=self.near_recv.at[c],
            device_id={"tensor": self.near},
            device_id_type=pl.DeviceIdType.MESH,
        )

    def to_across(self, c):
        return pltpu.make_async_remote_copy(
            src_ref=self.own.at[self.piece_rows(c)],
            dst_ref=self.mid_buf.at[self.piece_rows(c)],
            send_sem=self.mid_send.at[c],
            recv_sem=self.mid_recv.at[c],
            device_id={"tensor": self.across},
            device_id_type=pl.DeviceIdType.MESH,
        )

    def peers(self):
        return [
            (self.is_end | self.is_mid, "tensor", self.near),
            (self.is_mid, "tensor", self.across),
        ]

    def send(self, c):
        @pl.when(self.is_end)
        def _():
            for i in self.pieces(c):
                self.to_near(self.own, i).start()

    def summed(self, left, right, c):
        rows = self.piece_rows(c)
        both = left[rows, :].astype(jnp.float32) + right[rows, :].astype(jnp.float32)
        return both.astype(jnp.bfloat16)

    def join(self, c):
        @pl.when(self.is_mid)
        def _():
            for i in self.pieces(c):
                self.to_near(self.near_buf, i).wait_recv()
                self.own[self.piece_rows(i), :] = self.summed(self.own, self.near_buf, i)
                self.to_across(i).start()

    def finish(self, c):
        @pl.when(self.is_mid)
        def _():
            for i in self.pieces(c):
                self.to_across(i).wait_recv()
                self.near_buf[self.piece_rows(i), :] = self.summed(self.own, self.mid_buf, i)
                self.to_near(self.near_buf, i).start()

    def take(self, c):
        @pl.when(self.is_end)
        def _():
            for i in self.pieces(c):
                self.to_near(self.own, i).wait_recv()

        return self.near_buf[self.rows(c), :].astype(jnp.float32)

    def drain(self, c):
        @pl.when(self.is_end)
        def _():
            for i in self.pieces(c):
                self.to_near(self.own, i).wait_send()

        @pl.when(self.is_mid)
        def _():
            for i in self.pieces(c):
                self.to_across(i).wait_send()
                self.to_near(self.near_buf, i).wait_send()


def flipped(place, bit):
    return place + bit - 2 * bit * lax.rem(lax.div(place, bit), 2)


def dp_copy(src, dst, send_sem, recv_sem, target):
    return pltpu.make_async_remote_copy(
        src_ref=src,
        dst_ref=dst,
        send_sem=send_sem,
        recv_sem=recv_sem,
        device_id={"dp": target},
        device_id_type=pl.DeviceIdType.MESH,
    )


def greet(targets):
    barrier = pltpu.get_barrier_semaphore()
    count = 0
    for known, axis, target in targets:
        count = count + jnp.where(known, 1, 0)

        @pl.when(known)
        def _(axis=axis, target=target):
            pl.semaphore_signal(
                barrier, inc=1, device_id={axis: target}, device_id_type=pl.DeviceIdType.MESH
            )

    pl.semaphore_wait(barrier, count)


def cube_targets():
    place = lax.axis_index("dp")
    return [(place >= 0, "dp", flipped(place, bit)) for bit in (1, 2, 4)]


def window_targets(hops):
    place = lax.axis_index("dp")
    size = lax.axis_size("dp")
    after = [(place + hop < size, "dp", place + hop) for hop in range(1, hops + 1)]
    return after + [(place - hop >= 0, "dp", place - hop) for hop in range(1, hops + 1)]


class Gather:
    copies = 8

    @staticmethod
    def scratch():
        return [pltpu.SemaphoreType.DMA((Gather.copies,))] * 2

    def __init__(self, own_ref, full_ref, sems):
        self.own, self.full = own_ref, full_ref
        self.send, self.recv = sems
        self.size = own_ref.shape[0]
        self.place = lax.axis_index("dp")

    def span(self, owner, part=None):
        size = self.size if part is None else self.size // 2
        first = owner * self.size + (0 if not part else size)
        return self.full.at[pl.ds(pl.multiple_of(first, size), size)]

    def copy(self, k):
        me = self.place
        fx, fy, sib = flipped(me, 2), flipped(me, 4), flipped(me, 1)
        src, dst, target = {
            0: lambda: (self.own, self.span(me), fx),
            1: lambda: (self.own, self.span(me), fy),
            2: lambda: (self.own, self.span(me), sib),
            3: lambda: (self.span(fx, 0), self.span(fx, 0), fy),
            4: lambda: (self.span(fy, 1), self.span(fy, 1), fx),
            5: lambda: (self.span(fx), self.span(fx), sib),
            6: lambda: (self.span(fy), self.span(fy), sib),
            7: lambda: (self.span(flipped(fx, 4)), self.span(flipped(fx, 4)), sib),
        }[k]()
        return dp_copy(src, dst, self.send.at[k], self.recv.at[k], target)

    def begin(self):
        first = pl.multiple_of(self.place * self.size, self.size)
        self.full[pl.ds(first, self.size), :] = self.own[...]
        for k in (0, 1, 2):
            self.copy(k).start()

    def relay(self):
        self.copy(0).wait_recv()
        self.copy(3).start()
        self.copy(5).start()
        self.copy(1).wait_recv()
        self.copy(4).start()
        self.copy(6).start()

    def pass_on(self):
        self.copy(3).wait_recv()
        self.copy(4).wait_recv()
        self.copy(7).start()

    def finish(self):
        for k in (2, 5, 6, 7):
            self.copy(k).wait_recv()

    def drain(self):
        for k in range(self.copies):
            self.copy(k).wait_send()


class Scatter:
    copies = 10
    refs = 7

    @staticmethod
    def scratch(rows, width):
        half = rows // 2
        return [
            pltpu.VMEM((4, rows, width), jnp.bfloat16),
            pltpu.VMEM((2, half, width), jnp.bfloat16),
            pltpu.VMEM((2, half, width), jnp.bfloat16),
            pltpu.VMEM((half, width), jnp.bfloat16),
            pltpu.VMEM((half, width), jnp.bfloat16),
            pltpu.SemaphoreType.DMA((Scatter.copies,)),
            pltpu.SemaphoreType.DMA((Scatter.copies,)),
        ]

    def __init__(self, grad_ref, out_ref, refs):
        self.grad, self.out = grad_ref, out_ref
        self.acc, self.x_one, self.y_one, self.x_two, self.y_two, self.send, self.recv = refs
        self.size = out_ref.shape[0]
        me = lax.axis_index("dp")
        self.core = lax.rem(me, 2)
        self.sib, self.fx, self.fy = flipped(me, 1), flipped(me, 2), flipped(me, 4)
        self.here, self.qx, self.qy = (lax.div(v, 2) for v in (me, self.fx, self.fy))
        self.qxy = lax.div(flipped(self.fx, 4), 2)

    def owner_rows(self, chip, core):
        first = (2 * chip + core) * self.size
        return pl.ds(pl.multiple_of(first, self.size), self.size)

    def half(self, which):
        count = self.size // 2
        return pl.ds(which * count, count)

    def to_core(self, chip):
        src = self.grad.at[self.owner_rows(chip, 1 - self.core)]
        return dp_copy(src, self.acc.at[chip], self.send.at[chip], self.recv.at[chip], self.sib)

    def copy(self, k):
        acc, low, high = self.acc, self.half(0), self.half(1)
        src, dst, target = {
            4: lambda: (acc.at[self.qx, low], self.x_one.at[0], self.fx),
            5: lambda: (acc.at[self.qxy, low], self.x_one.at[1], self.fx),
            6: lambda: (acc.at[self.qy, high], self.y_one.at[0], self.fy),
            7: lambda: (acc.at[self.qxy, high], self.y_one.at[1], self.fy),
            8: lambda: (acc.at[self.qy, low], self.y_two, self.fy),
            9: lambda: (acc.at[self.qx, high], self.x_two, self.fx),
        }[k]()
        return dp_copy(src, dst, self.send.at[k], self.recv.at[k], target)

    def begin(self):
        for chip in range(4):
            self.to_core(chip).start()

    def add_core(self, chip):
        self.to_core(chip).wait_recv()
        first = self.owner_rows(chip, self.core).start
        count = self.size // 2
        for which in (0, 1):
            rows = pl.ds(pl.multiple_of(first + which * count, count), count)
            total = self.acc[chip, self.half(which), :].astype(jnp.float32)
            total = total + self.grad[rows, :].astype(jnp.float32)
            self.acc[chip, self.half(which), :] = total.astype(jnp.bfloat16)

    def spread(self):
        self.add_core(self.qxy)
        self.copy(5).start()
        self.copy(7).start()
        self.add_core(self.qx)
        self.copy(4).start()
        self.add_core(self.qy)
        self.copy(6).start()
        self.add_core(self.here)

    def add_half(self, chip, which, other):
        total = self.acc[chip, self.half(which), :].astype(jnp.float32)
        self.acc[chip, self.half(which), :] = (total + other.astype(jnp.float32)).astype(
            jnp.bfloat16
        )

    def narrow(self):
        self.copy(5).wait_recv()
        self.add_half(self.qy, 0, self.x_one[1])
        self.copy(8).start()
        self.copy(7).wait_recv()
        self.add_half(self.qx, 1, self.y_one[1])
        self.copy(9).start()

    def close(self):
        for k in (4, 6, 8, 9):
            self.copy(k).wait_recv()
        pairs = ((self.x_one, self.y_two), (self.y_one, self.x_two))
        for which, (one, two) in enumerate(pairs):
            total = self.acc[self.here, self.half(which), :].astype(jnp.float32)
            total = total + one[0].astype(jnp.float32) + two[...].astype(jnp.float32)
            self.out[self.half(which), :] = total

    def drain(self):
        for chip in range(4):
            self.to_core(chip).wait_send()
        for k in range(4, self.copies):
            self.copy(k).wait_send()


def scatters_of(grads, outs, scratch):
    count = Scatter.refs
    return [
        Scatter(g, o, scratch[count * i : count * (i + 1)])
        for i, (g, o) in enumerate(zip(grads, outs))
    ]


class LineGather:
    refs = 5

    @staticmethod
    def scratch(chunks):
        return [pltpu.SemaphoreType.DMA((3, chunks))] * 4

    def __init__(self, all_ref, chunks, sems):
        self.all, self.chunks = all_ref, chunks
        self.step = all_ref.shape[1] // chunks
        self.right_send, self.right_recv, self.left_send, self.left_recv = sems
        self.place = lax.axis_index("tensor")
        self.last = all_ref.shape[0] - 1

    def peers(self):
        return [
            (self.place < self.last, "tensor", self.place + 1),
            (self.place > 0, "tensor", self.place - 1),
        ]

    def rows(self, c):
        return pl.ds(pl.multiple_of(c * self.step, self.step), self.step)

    def copy(self, way, block, hop, c):
        send, recv = (
            (self.right_send, self.right_recv) if way > 0 else (self.left_send, self.left_recv)
        )
        return pltpu.make_async_remote_copy(
            src_ref=self.all.at[block, self.rows(c)],
            dst_ref=self.all.at[block, self.rows(c)],
            send_sem=send.at[hop, c],
            recv_sem=recv.at[hop, c],
            device_id={"tensor": self.place + way},
            device_id_type=pl.DeviceIdType.MESH,
        )

    def holds(self, way, hop):
        return (self.place >= hop) if way > 0 else (self.place + hop <= self.last)

    def passes(self, way, hop):
        open_end = (self.place < self.last) if way > 0 else (self.place > 0)
        return self.holds(way, hop) & open_end

    def hand(self, hop, c):
        for way in (1, -1):
            block = self.place - way * hop
            if hop > 0:

                @pl.when(self.holds(way, hop))
                def _(way=way, block=block):
                    self.copy(way, block, hop - 1, c).wait_recv()

            if hop < self.last:

                @pl.when(self.passes(way, hop))
                def _(way=way, block=block):
                    self.copy(way, block, hop, c).start()

    def drain(self, c):
        for way in (1, -1):
            for hop in range(self.last):

                @pl.when(self.passes(way, hop))
                def _(way=way, hop=hop):
                    self.copy(way, self.place - way * hop, hop, c).wait_send()


def project_groups(all_ref, rows, weights_ref):
    total = None
    for group in range(all_ref.shape[0]):
        part = jnp.dot(
            all_ref[group, rows, :], weights_ref[group], preferred_element_type=jnp.float32
        )
        total = part if total is None else total + part
    return total


class Window:
    @staticmethod
    def scratch(hops, chunks):
        return [pltpu.SemaphoreType.DMA((hops, chunks))] * 2

    def __init__(self, window_ref, rows, chunks, sems):
        self.window, self.total_rows, self.chunks = window_ref, rows, chunks
        self.step = rows // chunks
        self.hops = window_ref.shape[0] // rows - 1
        self.send, self.recv = sems
        self.place = lax.axis_index("dp")
        self.size = lax.axis_size("dp")

    def span(self, block, c):
        first = block * self.total_rows + c * self.step
        return pl.ds(pl.multiple_of(first, self.step), self.step)

    def copy(self, hop, c):
        return dp_copy(
            self.window.at[self.span(self.hops, c)],
            self.window.at[self.span(self.hops - hop, c)],
            self.send.at[hop - 1, c],
            self.recv.at[hop - 1, c],
            self.place + hop,
        )

    def clear(self):
        for hop in range(1, self.hops + 1):

            @pl.when(self.place - hop < 0)
            def _(hop=hop):
                first = (self.hops - hop) * self.total_rows
                shape = (self.total_rows, self.window.shape[1])
                self.window[first : first + self.total_rows, :] = jnp.zeros(shape, jnp.bfloat16)

    def start(self, c):
        for hop in range(1, self.hops + 1):

            @pl.when(self.place + hop < self.size)
            def _(hop=hop):
                self.copy(hop, c).start()

    def drain(self, c):
        for hop in range(1, self.hops + 1):

            @pl.when(self.place + hop < self.size)
            def _(hop=hop):
                self.copy(hop, c).wait_send()

            @pl.when(self.place - hop >= 0)
            def _(hop=hop):
                self.copy(hop, c).wait_recv()


def run_stages(chunks, stages, events=()):
    def body(t, carry):
        for when, event in events:
            pl.when(t == when)(event)
        for lag, stage in stages:
            c = t - LAG * lag

            @pl.when((c >= 0) & (c < chunks))
            def _(stage=stage, c=c):
                stage(c)

        return carry

    lax.fori_loop(0, chunks + LAG * max(lag for lag, _ in stages), body, 0)


def drain_all(chunks, lines):
    def body(c, carry):
        for line in lines:
            line.drain(c)
        return carry

    lax.fori_loop(0, chunks, body, 0)


def add_sums(sums_ref, row, values):
    width = values.shape[1]
    sums_ref[row : row + 1, :width] += jnp.sum(values, axis=0, keepdims=True)


def project_into(line, c, left, weight_ref):
    rows = line.rows(c)
    for cols in column_blocks(weight_ref.shape[1]):
        part = jnp.dot(left, weight_ref[:, cols], preferred_element_type=jnp.float32)
        line.own[rows, cols] = part.astype(jnp.bfloat16)
    line.send(c)


def project_back_into(line, c, left, weight_ref):
    rows = line.rows(c)
    for cols in column_blocks(weight_ref.shape[0]):
        part = dot_rows(left, weight_ref[cols, :])
        line.own[rows, cols] = part.astype(jnp.bfloat16)
    line.send(c)


def head_kernel(hops, *refs):
    ins, outs, scratch = refs[:6], refs[6:15], refs[15:]
    h_ref, small_own, wo_own = ins[0], ins[1], ins[5]
    wa_own, we_own, wr_own = (ref.at[0] for ref in ins[2:5])
    small_ref, wa_ref, we_ref, wr_ref, wo_ref, shard_ref, a1_ref, q_ref, window_ref = outs
    line = LineGather(shard_ref, 1, scratch[:4])
    groups, share = shard_ref.shape[0], shard_ref.shape[1] // 2
    pairs = list(zip((small_own, wa_own, we_own, wr_own), outs[:4]))
    pairs += [(shard_ref.at[g, pl.ds(0, share)], wo_ref.at[g]) for g in range(groups)]
    gathers = [
        Gather(o, f, scratch[4 + 2 * i : 6 + 2 * i]) for i, (o, f) in enumerate(pairs)
    ]
    small, wa, we, wr = gathers[:4]
    rows, width = q_ref.shape
    chunks = 4
    window = Window(window_ref, rows, chunks, scratch[-2:])
    shard_ref[line.place] = wo_own[...]
    greet(cube_targets() + window_targets(hops) + line.peers())
    small.begin()
    wa.begin()
    line.hand(0, 0)
    window.clear()
    small.relay()
    small.pass_on()
    small.finish()
    values = small_ref[...].astype(jnp.float32)
    gain, offset = wide_row(values, GAIN_ROW), wide_row(values, OFFSET_ROW)
    bias_q, bias_v = narrow_row(values, width, 0), narrow_row(values, width, 1)
    step = rows // chunks

    def normalize(c, carry):
        at = pl.ds(pl.multiple_of(c * step, step), step)
        a1_ref[at, :] = norm_rows(h_ref[at, :], gain, offset).astype(jnp.bfloat16)
        return carry

    line.hand(1, 0)
    lax.fori_loop(0, chunks, normalize, 0)
    line.hand(2, 0)
    wa.relay()
    we.begin()
    wa.pass_on()
    wr.begin()
    line.hand(3, 0)
    for member in gathers[4:]:
        member.begin()
    wa.finish()

    def project(c, carry):
        at = pl.ds(pl.multiple_of(c * step, step), step)
        a1 = a1_ref[at, :]
        there = window.span(window.hops, c)
        for part in (1, 2):
            cols = slice(part * width, (part + 1) * width)
            value = jnp.dot(a1, wa_ref[:, cols], preferred_element_type=jnp.float32)
            value = value if part == 1 else value + bias_v
            window_ref[there, (part - 1) * width : part * width] = value.astype(jnp.bfloat16)
        window.start(c)
        value = jnp.dot(a1, wa_ref[:, :width], preferred_element_type=jnp.float32)
        q_ref[at, :] = (value + bias_q).astype(jnp.bfloat16)
        return carry

    lax.fori_loop(0, chunks, project, 0)
    for member in gathers[2:]:
        member.relay()
    for member in gathers[2:]:
        member.pass_on()
    for c in range(chunks):
        window.drain(c)
    line.drain(0)
    for member in gathers[2:]:
        member.finish()
    for member in gathers:
        member.drain()


SMALL_ROWS = 32
BRANCH_ROW, UNIT_ROW, GAIN_ROW, OFFSET_ROW, MARK_ROW = 8, 12, 14, 18, 22


def wide_row(values, row):
    owners = range(values.shape[0] // SMALL_ROWS)
    return jnp.concatenate(
        [values[o * SMALL_ROWS + row : o * SMALL_ROWS + row + 1, :] for o in owners], axis=1
    )


def narrow_row(values, width, index):
    owners = range(values.shape[0] // SMALL_ROWS)
    count = width // LANES
    parts = []
    for row in range(index * count, (index + 1) * count):
        total = values[row : row + 1, :]
        for o in owners[1:]:
            total = total + values[o * SMALL_ROWS + row : o * SMALL_ROWS + row + 1, :]
        parts.append(total)
    return jnp.concatenate(parts, axis=1)


def pack_small(small_in, marks, width):
    attend_bias, branch_bias, expand_bias, norm_gain, norm_bias = small_in
    place = lax.axis_index("dp")
    flat = attend_bias.reshape(-1, attend_bias.shape[-1])
    spread = jnp.zeros((flat.shape[0], width), jnp.bfloat16)
    spread = lax.dynamic_update_slice(spread, flat, (0, place * flat.shape[1]))
    rows = [spread.reshape(-1, LANES)]
    rows += [e.reshape(-1, LANES) for e in (branch_bias, expand_bias, norm_gain, norm_bias)]
    rows.append(marks.astype(jnp.bfloat16).reshape(-1, LANES))
    packed = jnp.concatenate(rows, axis=0)
    return jnp.pad(packed, ((0, SMALL_ROWS - packed.shape[0]), (0, 0)))


def unpack_small(small_all, rows, width, reach_back):
    size = small_all.shape[0] // SMALL_ROWS
    grid = small_all.reshape(size, SMALL_ROWS, LANES)
    wide = grid[:, BRANCH_ROW:MARK_ROW].astype(jnp.float32)
    wide = jnp.moveaxis(wide, 0, 1).reshape(MARK_ROW - BRANCH_ROW, size * LANES)
    branches, units = wide[:4].reshape(2, 2, -1), wide[4:6]
    gains, offsets = wide[6:10].reshape(2, 2, -1), wide[10:14].reshape(2, 2, -1)
    attend_b = jnp.sum(grid[:, :BRANCH_ROW].astype(jnp.float32), axis=0).reshape(2, 2, width)
    marks = grid[:, MARK_ROW : MARK_ROW + rows // LANES].astype(jnp.int32).reshape(-1)
    padded = jnp.concatenate([jnp.zeros((reach_back * rows,), jnp.int32), marks])
    begin = lax.axis_index("dp") * rows
    window = lax.dynamic_slice_in_dim(padded, begin, (reach_back + 1) * rows)
    return attend_b, branches, units, gains, offsets, (window[reach_back * rows :, None], window[None])


def first_kernel(chunks, *refs):
    ins, outs, scratch = refs[:10], refs[10:22], refs[22:]
    o_ref, wo_ref, h_ref, vec_ref, we_ref, wr_ref = ins[:6]
    mid_ref, a2_ref, f_ref, u_ref, next_ref, a1_ref, q_ref, window_ref = outs[:8]
    wa_ref = outs[8]
    two = LineTotal(scratch[:7], chunks)
    all_ref = scratch[7]
    one = LineGather(all_ref, chunks, scratch[8:12])
    shard_ref = ins[9]
    groups, share = shard_ref.shape[0], shard_ref.shape[1] // 2
    pairs = list(zip((ref.at[1] for ref in ins[6:9]), outs[8:11]))
    pairs += [(shard_ref.at[g, pl.ds(share, share)], outs[11].at[g]) for g in range(groups)]
    gathers = [
        Gather(o, f, scratch[12 + 2 * i : 14 + 2 * i]) for i, (o, f) in enumerate(pairs)
    ]
    rows_all, width = q_ref.shape
    window = Window(window_ref, rows_all, chunks, scratch[-2:])
    all_ref[one.place] = o_ref[...]
    greet(one.peers() + two.peers() + cube_targets() + window_targets(window.hops))
    window.clear()

    def feed(c):
        rows = one.rows(c)
        one.hand(3, c)
        middle = h_ref[rows, :] + (project_groups(all_ref, rows, wo_ref) + vec_ref[0:1, :])
        mid_ref[rows, :] = middle
        a2 = norm_rows(middle, vec_ref[1:2, :], vec_ref[2:3, :]).astype(jnp.bfloat16)
        a2_ref[rows, :] = a2
        for cols in column_blocks(we_ref.shape[1]):
            f = jnp.dot(a2, we_ref[:, cols], preferred_element_type=jnp.float32)
            f = f + vec_ref[3:4, cols]
            f_ref[rows, cols] = f
            u_ref[rows, cols] = gelu_value(f)[0].astype(jnp.bfloat16)
        project_into(two, c, u_ref[rows, :], wr_ref)

    def end(c):
        rows = two.rows(c)
        following = mid_ref[rows, :] + (two.take(c) + vec_ref[4:5, :])
        next_ref[rows, :] = following
        a1 = norm_rows(following, vec_ref[5:6, :], vec_ref[6:7, :]).astype(jnp.bfloat16)
        a1_ref[rows, :] = a1
        there = window.span(window.hops, c)
        for part in (1, 2, 0):
            cols = slice(part * width, (part + 1) * width)
            value = jnp.dot(a1, wa_ref[:, cols], preferred_element_type=jnp.float32)
            value = (value + vec_ref[7:8, cols]).astype(jnp.bfloat16)
            if part == 0:
                q_ref[rows, :] = value
            else:
                window_ref[there, (part - 1) * width : part * width] = value
            if part == 2:
                window.start(c)

    wa, we, wr = gathers[:3]
    rest = gathers[3:]

    def every(name):
        def event():
            for member in rest:
                getattr(member, name)()

        return event

    last = chunks + LAG * 6 - 1
    run_stages(
        chunks,
        [
            (0, functools.partial(one.hand, 0)),
            (1, functools.partial(one.hand, 1)),
            (2, functools.partial(one.hand, 2)),
            (3, feed),
            (4, two.join),
            (5, two.finish),
            (6, end),
        ],
        [
            (0, wa.begin),
            (3, wa.relay),
            (3, we.begin),
            (5, wa.pass_on),
            (LAG * 6, wa.finish),
            (LAG * 6, we.relay),
            (LAG * 6, wr.begin),
            (LAG * 6, every("begin")),
            (LAG * 6 + 2, we.pass_on),
            (last - 2, wr.relay),
            (last - 2, every("relay")),
            (last, wr.pass_on),
            (last, every("pass_on")),
        ],
    )
    drain_all(chunks, [one, two, window])
    for member in gathers[1:]:
        member.finish()
    for member in gathers:
        member.drain()


def turn_kernel(chunks, *refs):
    ins, outs, scratch = refs[:7], refs[7:16], refs[16:]
    o_ref, wo_ref, h_ref, vec_ref, we_ref, wr_ref, e_ref = ins[:7]
    a2_ref, u_ref, eb_ref, dfb_ref, dmid_ref, db_ref, do_ref, mid_ref, sums_ref = outs
    back = LineTotal(scratch[:7], chunks)
    all_ref = scratch[7]
    one = LineGather(all_ref, chunks, scratch[8:12])
    all_ref[one.place] = o_ref[...]
    sums_ref[...] = jnp.zeros_like(sums_ref)
    greet(one.peers() + back.peers())

    def feed(c):
        rows = one.rows(c)
        one.hand(3, c)
        middle = h_ref[rows, :] + (project_groups(all_ref, rows, wo_ref) + vec_ref[0:1, :])
        mid_ref[rows, :] = middle
        a2 = norm_rows(middle, vec_ref[1:2, :], vec_ref[2:3, :]).astype(jnp.bfloat16)
        a2_ref[rows, :] = a2
        e = e_ref[rows, :]
        add_sums(sums_ref, 0, e)
        eb = e.astype(jnp.bfloat16)
        eb_ref[rows, :] = eb
        for cols in column_blocks(we_ref.shape[1]):
            f = jnp.dot(a2, we_ref[:, cols], preferred_element_type=jnp.float32)
            f = f + vec_ref[3:4, cols]
            u, bent = gelu_value(f)
            u_ref[rows, cols] = u.astype(jnp.bfloat16)
            df = dot_rows(eb, wr_ref[cols, :]) * gelu_slope(f, bent)
            sums_ref[1:2, cols] += jnp.sum(df, axis=0, keepdims=True)
            dfb_ref[rows, cols] = df.astype(jnp.bfloat16)
        project_back_into(back, c, dfb_ref[rows, :], we_ref)

    def turn(c):
        rows = back.rows(c)
        cot = back.take(c)
        part, gain_part = norm_back(mid_ref[rows, :], vec_ref[1:2, :], cot)
        dmid = e_ref[rows, :] + part
        dmid_ref[rows, :] = dmid
        add_sums(sums_ref, 2, gain_part)
        add_sums(sums_ref, 3, cot)
        add_sums(sums_ref, 4, dmid)
        db = dmid.astype(jnp.bfloat16)
        db_ref[rows, :] = db
        do_ref[rows, :] = dot_rows(db, wo_ref[one.place]).astype(jnp.bfloat16)

    run_stages(
        chunks,
        [
            (0, functools.partial(one.hand, 0)),
            (1, functools.partial(one.hand, 1)),
            (2, functools.partial(one.hand, 2)),
            (3, feed),
            (4, back.join),
            (5, back.finish),
            (6, turn),
        ],
    )
    drain_all(chunks, [one, back])


def cross_kernel(chunks, *refs):
    ins, outs, scratch = refs[:14], refs[14:24], refs[24:]
    dproj_ref, wa_ref, h_ref, dmid_in_ref, vec_ref, f_ref, mid_ref, we_ref, wr_ref, wo_ref = ins[:10]
    eb_ref, dfb_ref, dmid_ref, db_ref, do_ref, sums_ref = outs[:6]
    e_ref = scratch[0]
    one = LineTotal(scratch[1:8], chunks)
    back = LineTotal(scratch[8:15], chunks)
    scatters = scatters_of(ins[10:], outs[6:], scratch[15:])
    sums_ref[...] = jnp.zeros_like(sums_ref)
    greet(one.peers() + cube_targets())

    def start(c):
        project_back_into(one, c, dproj_ref[one.rows(c), :], wa_ref)

    def feed(c):
        rows = one.rows(c)
        cot = one.take(c)
        part, gain_part = norm_back(h_ref[rows, :], vec_ref[0:1, :], cot)
        e = dmid_in_ref[rows, :] + part
        e_ref[rows, :] = e
        add_sums(sums_ref, 0, gain_part)
        add_sums(sums_ref, 1, cot)
        add_sums(sums_ref, 2, e)
        eb = e.astype(jnp.bfloat16)
        eb_ref[rows, :] = eb
        for cols in column_blocks(we_ref.shape[1]):
            f = f_ref[rows, cols]
            unused, bent = gelu_value(f)
            df = dot_rows(eb, wr_ref[cols, :]) * gelu_slope(f, bent)
            sums_ref[3:4, cols] += jnp.sum(df, axis=0, keepdims=True)
            dfb_ref[rows, cols] = df.astype(jnp.bfloat16)
        project_back_into(back, c, dfb_ref[rows, :], we_ref)

    def turn(c):
        rows = back.rows(c)
        cot = back.take(c)
        part, gain_part = norm_back(mid_ref[rows, :], vec_ref[1:2, :], cot)
        dmid = e_ref[rows, :] + part
        dmid_ref[rows, :] = dmid
        add_sums(sums_ref, 4, gain_part)
        add_sums(sums_ref, 5, cot)
        add_sums(sums_ref, 6, dmid)
        db = dmid.astype(jnp.bfloat16)
        db_ref[rows, :] = db
        do_ref[rows, :] = dot_rows(db, wo_ref[lax.axis_index("tensor")]).astype(jnp.bfloat16)

    run_stages(
        chunks,
        [
            (0, start),
            (1, one.join),
            (2, one.finish),
            (3, feed),
            (4, back.join),
            (5, back.finish),
            (6, turn),
        ],
        scatter_events(scatters, chunks + LAG * 6 - 1, 1, 2, 3, 3),
    )
    drain_all(chunks, [one, back])
    for member in scatters:
        member.drain()


def scatter_events(scatters, last, apart, wait_one, wait_two, wait_three):
    events = []
    for i, member in enumerate(scatters):
        at = i * apart
        events.append((min(at, last), member.begin))
        events.append((min(at + wait_one, last), member.spread))
        events.append((min(at + wait_one + wait_two, last), member.narrow))
        events.append((min(at + wait_one + wait_two + wait_three, last), member.close))
    return events


def last_kernel(chunks, *refs):
    ins, outs, scratch = refs[:10], refs[10:18], refs[18:]
    dproj_ref, wa_ref, h_ref, dmid_ref, vec_ref = ins[:5]
    grad_ref, late_ref, sums_ref = outs[0], outs[1], outs[2]
    one = LineTotal(scratch[:7], chunks)
    parts_ref, seen_ref, part_send, part_recv = scratch[7:11]
    scatters = scatters_of(ins[5:], outs[3:], scratch[11:])
    place, size = lax.axis_index("dp"), lax.axis_size("dp")
    sums_ref[...] = jnp.zeros_like(sums_ref)
    everyone = [(place >= 0, "dp", lax.rem(place + j, size)) for j in range(1, size)]
    greet(one.peers() + everyone)

    def start(c):
        project_back_into(one, c, dproj_ref[one.rows(c), :], wa_ref)

    def end(c):
        rows = one.rows(c)
        cot = one.take(c)
        part, gain_part = norm_back(h_ref[rows, :], vec_ref[0:1, :], cot)
        grad_ref[rows, :] = dmid_ref[rows, :] + part
        add_sums(sums_ref, 0, gain_part)
        add_sums(sums_ref, 1, cot)

    run_stages(
        chunks,
        [(0, start), (1, one.join), (2, one.finish), (3, end)],
        scatter_events(scatters, chunks + LAG * 3 - 1, 1, 1, 3, 3),
    )

    def part_copy(j):
        target = lax.rem(place + j, size)
        return dp_copy(
            parts_ref.at[target], seen_ref.at[j], part_send.at[j], part_recv.at[j], target
        )

    for owner in range(size):
        parts_ref[owner] = sums_ref[:, owner * LANES : (owner + 1) * LANES]
    for j in range(1, size):
        part_copy(j).start()
    drain_all(chunks, [one])
    total = parts_ref[place]
    for j in range(1, size):
        part_copy(j).wait_recv()
        total = total + seen_ref[j]
    late_ref[...] = total
    for j in range(1, size):
        part_copy(j).wait_send()
    for member in scatters:
        member.drain()


CHUNKS = 8
SPLIT = 2
LAG = 1
MEGA = 1024 * 1024


def line_call(kernel, name, number, out_shapes, extra, lines, span_us, args, more=()):
    rows, model = extra
    scratch = []
    if lines[0]:
        scratch.append(pltpu.VMEM((rows, model), jnp.float32))
    for _ in range(lines[1]):
        scratch += LineTotal.scratch(rows, model, CHUNKS)
    scratch += list(more)
    return pl.pallas_call(
        functools.partial(kernel, CHUNKS),
        out_shape=tuple(jax.ShapeDtypeStruct(shape, kind) for shape, kind in out_shapes),
        in_specs=in_vmem(len(args)),
        out_specs=tuple(in_vmem(len(out_shapes))),
        scratch_shapes=scratch,
        cost_estimate=pl.CostEstimate(
            flops=int(span_us * 1e9), bytes_accessed=0, transcendentals=0
        ),
        compiler_params=pltpu.CompilerParams(
            collective_id=number, has_side_effects=True, vmem_limit_bytes=56 * MEGA
        ),
        name=name,
    )(*args)


def stack_rows(model, rows):
    rows = [jnp.pad(r, (0, model - r.shape[0])) for r in rows]
    rows += [jnp.zeros((model,), jnp.float32)] * (-len(rows) % 8)
    return jnp.stack(rows)


def window_of(kv_now, reach_back):
    kv_list = [passed_along(kv_now, "dp", hop) for hop in range(reach_back, 0, -1)]
    return jnp.concatenate(kv_list + [kv_now], axis=0)


def grad_blocks(left_ref, right_ref, out_ref):
    for rows in column_blocks(left_ref.shape[1]):
        left = left_ref[:, rows]
        for cols in column_blocks(right_ref.shape[1]):
            out_ref[rows, cols] = dot_tokens(left, right_ref[:, cols]).astype(jnp.bfloat16)


class WindowBack:
    @staticmethod
    def scratch(hops, rows, width, pieces):
        return [
            pltpu.VMEM((hops * rows, width), jnp.bfloat16),
            pltpu.VMEM((hops * rows, width), jnp.bfloat16),
            pltpu.SemaphoreType.DMA((hops, pieces)),
            pltpu.SemaphoreType.DMA((hops, pieces)),
        ]

    def __init__(self, rows, refs):
        self.out, self.seen, self.send, self.recv = refs
        self.rows = rows
        self.hops = self.out.shape[0] // rows
        self.place, self.size = lax.axis_index("dp"), lax.axis_size("dp")

    def span(self, hop):
        return slice((self.hops - hop) * self.rows, (self.hops - hop + 1) * self.rows)

    def copy(self, hop, piece, cols):
        return dp_copy(
            self.out.at[self.span(hop), cols],
            self.seen.at[self.span(hop), cols],
            self.send.at[hop - 1, piece],
            self.recv.at[hop - 1, piece],
            self.place - hop,
        )

    def clear(self):
        for hop in range(1, self.hops + 1):

            @pl.when(self.place + hop >= self.size)
            def _(hop=hop):
                shape = (self.rows, self.seen.shape[1])
                self.seen[self.span(hop), :] = jnp.zeros(shape, jnp.bfloat16)

    def start(self, piece, cols):
        for hop in range(1, self.hops + 1):

            @pl.when(self.place - hop >= 0)
            def _(hop=hop):
                self.copy(hop, piece, cols).start()

    def take(self, piece, cols):
        total = None
        for hop in range(1, self.hops + 1):

            @pl.when(self.place + hop < self.size)
            def _(hop=hop):
                self.copy(hop, piece, cols).wait_recv()

            seen = self.seen[self.span(hop), cols].astype(jnp.float32)
            total = seen if total is None else total + seen
        return total

    def drain(self, piece, cols):
        for hop in range(1, self.hops + 1):

            @pl.when(self.place - hop >= 0)
            def _(hop=hop):
                self.copy(hop, piece, cols).wait_send()


def return_kernel(chunks, first, hops, *refs):
    ins, outs, scratch = refs[:17], refs[17:24], refs[24:]
    q_ref, kv_ref, lse_ref, cot_ref, own_ref, window_ref = ins[:6]
    a2_ref, dfb_ref, u_ref, eb_ref, o_ref, db_ref, a1_ref = ins[6:13]
    act_ref, wr_ref, mid_ref, bias_ref = ins[13:]
    dproj_ref, sums_ref, expand_ref, reduce_ref, output_ref, attend_ref, hidden_ref = outs
    acc = scratch[0]
    line = LineTotal(scratch[1:8], chunks)
    back_pass = WindowBack(q_ref.shape[0], scratch[8:12])
    rows, width = q_ref.shape
    window_rows = kv_ref.shape[0]
    back = window_rows - rows
    factor = 1.0 / math.sqrt(HEAD_DIM)
    sums_ref[...] = jnp.zeros_like(sums_ref)
    acc[...] = jnp.zeros_like(acc)
    greet(line.peers() + window_targets(hops))
    back_pass.clear()
    step = line.step

    def start(c):
        project_into(line, c, act_ref[first + c * step : first + (c + 1) * step, :], wr_ref)

    def end(c):
        middle = mid_ref[first + c * step : first + (c + 1) * step, :]
        hidden_ref[c * step : (c + 1) * step, :] = middle + (line.take(c) + bias_ref[0:1, :])

    stages = [start, line.join, line.finish, end]

    def line_step(t):
        for lag, stage in enumerate(stages):
            if 0 <= t - lag < chunks:
                stage(t - lag)

    groups = [(base, group) for base, group, inner in head_parts(width) if inner == 0]
    lines_done = 0
    for order, (base, group) in enumerate(groups):
        cols = slice(base, base + group)
        value_cols = slice(width + base, width + base + group)
        for start_row, tile, low, high in row_tiles(rows, window_rows):
            line_step(lines_done)
            lines_done += 1
            allowed = tile_mask(own_ref, window_ref, start_row, tile, low, high, back)
            at = slice(start_row, start_row + tile)
            held = None
            for inner in range(0, group, HEAD_DIM):
                index = (base + inner) // HEAD_DIM
                queries = pick(q_ref[at, cols], inner)
                cots = pick(cot_ref[at, cols], inner)
                keys = kv_ref[low:high, cols]
                values = kv_ref[low:high, value_cols]
                logs = lse_ref[at, index : index + 1]
                scores = dot_rows(queries, keys) * factor
                probabilities = jnp.where(allowed, jnp.exp(scores - logs), 0.0)
                rounded = probabilities.astype(jnp.bfloat16)
                acc[low:high, value_cols] += dot_tokens(rounded, cots)
                prob_cot = dot_rows(cots, values)
                inner_sum = jnp.sum(probabilities * prob_cot, axis=-1, keepdims=True)
                score_cot = (probabilities * (prob_cot - inner_sum) * factor).astype(jnp.bfloat16)
                acc[low:high, cols] += dot_tokens(score_cot, queries)
                part = pick(jnp.dot(score_cot, keys, preferred_element_type=jnp.float32), inner)
                held = part if held is None else held + part
            sums_ref[0:1, cols] += jnp.sum(held, axis=0, keepdims=True)
            dproj_ref[at, cols] = held.astype(jnp.bfloat16)
        for piece, part_cols in enumerate((cols, value_cols)):
            back_pass.out[:, part_cols] = acc[:back, part_cols].astype(jnp.bfloat16)
            back_pass.start(2 * order + piece, part_cols)

    line_step(lines_done)
    grad_blocks(a2_ref, dfb_ref, expand_ref)
    line_step(lines_done + 1)
    grad_blocks(u_ref, eb_ref, reduce_ref)
    line_step(lines_done + 2)
    grad_blocks(o_ref, db_ref, output_ref)
    for extra in range(lines_done + 3, chunks + 3):
        line_step(extra)
    for order, (base, group) in enumerate(groups):
        for piece, part_base in enumerate((base, width + base)):
            part_cols = slice(part_base, part_base + group)
            total = acc[back:, part_cols] + back_pass.take(2 * order + piece, part_cols)
            if piece == 1:
                sums_ref[1:2, base : base + group] = jnp.sum(total, axis=0, keepdims=True)
            dproj_ref[:, width + part_base : width + part_base + group] = total.astype(
                jnp.bfloat16
            )
    grad_blocks(a1_ref, dproj_ref, attend_ref)
    for c in range(chunks):
        line.drain(c)
    for order, (base, group) in enumerate(groups):
        for piece, part_base in enumerate((base, width + base)):
            back_pass.drain(2 * order + piece, slice(part_base, part_base + group))


RETURN_CHUNKS = 4


def return_call(name, number, first, hops, args):
    q, window, a2, dfb, o, a1 = args[0], args[1], args[6], args[7], args[10], args[12]
    rows, width = q.shape
    model, units = a2.shape[1], dfb.shape[1]
    count = rows // 2
    bf16, f32 = jnp.bfloat16, jnp.float32
    out_shapes = [
        ((rows, 3 * width), bf16),
        ((8, width), f32),
        ((model, units), bf16),
        ((units, model), bf16),
        ((width, model), bf16),
        ((model, 3 * width), bf16),
        ((count, model), f32),
    ]
    return pl.pallas_call(
        functools.partial(return_kernel, RETURN_CHUNKS, first, hops),
        out_shape=tuple(jax.ShapeDtypeStruct(shape, kind) for shape, kind in out_shapes),
        in_specs=in_vmem(len(args)),
        out_specs=tuple(in_vmem(len(out_shapes))),
        scratch_shapes=[
            pltpu.VMEM((window.shape[0], 2 * width), f32),
            *LineTotal.scratch(count, model, RETURN_CHUNKS),
            *WindowBack.scratch(hops, rows, 2 * width, 2 * max(1, width // LANES)),
        ],
        compiler_params=pltpu.CompilerParams(
            collective_id=number, has_side_effects=True, vmem_limit_bytes=56 * MEGA
        ),
        name=name,
    )(*args)


def head_call(hidden_in, small, weights, shards, width, hops):
    rows, model = hidden_in.shape
    size, groups = lax.axis_size("dp"), lax.axis_size("tensor")
    outs = [((size * small.shape[0], small.shape[1]), small.dtype)]
    outs += [((size * w.shape[1], w.shape[2]), w.dtype) for w in weights]
    outs += [
        ((groups, width, model), jnp.bfloat16),
        ((groups, *shards.shape), jnp.bfloat16),
        ((rows, model), jnp.bfloat16),
        ((rows, width), jnp.bfloat16),
        (((hops + 1) * rows, 2 * width), jnp.bfloat16),
    ]
    return pl.pallas_call(
        functools.partial(head_kernel, hops),
        out_shape=tuple(jax.ShapeDtypeStruct(shape, kind) for shape, kind in outs),
        in_specs=in_vmem(3 + len(weights)),
        out_specs=tuple(in_vmem(len(outs))),
        scratch_shapes=LineGather.scratch(1)
        + Gather.scratch() * (4 + groups)
        + Window.scratch(hops, 4),
        compiler_params=pltpu.CompilerParams(
            collective_id=5, has_side_effects=True, vmem_limit_bytes=40 * MEGA
        ),
        name="head",
    )(hidden_in, small, *weights, shards)


def pair_layers(hidden_in, out_grad, weights, small_in, doc_marks, reach_back, model_parts):
    share, unit_share, size, part = model_parts
    bf16, f32 = jnp.bfloat16, jnp.float32
    rows, model = hidden_in.shape
    attend_weight, output_weight, expand_weight, reduce_weight = weights
    width, units = attend_weight.shape[3], expand_weight.shape[2]
    extra = (rows, model)

    shards = (attend_weight.reshape(2, part, 3 * width), expand_weight, reduce_weight)

    def proj_bias(bias):
        return jnp.concatenate([bias[0], jnp.zeros_like(bias[0]), bias[1]])

    groups = lax.axis_size("tensor")
    line_gather_scratch = [pltpu.VMEM((groups, rows, width), bf16), *LineGather.scratch(CHUNKS)]
    out_shards = output_weight.reshape(2 * share, model)
    small_all, aw0, ew0, rw0, ow0, line_shards, a1_0, q_0, window_0 = head_call(
        hidden_in,
        pack_small(small_in, doc_marks, width),
        shards,
        out_shards,
        width,
        reach_back,
    )
    attend_b, (br0, br1), (eb0, eb1), (g0, g1), (c0, c1), marks = unpack_small(
        small_all, rows, width, reach_back
    )
    o_0, lse_0 = attend_forward(q_0, window_0, marks[0], marks[1])

    vec = stack_rows(
        model, [br0[0], g0[1], c0[1], eb0, br0[1], g1[0], c1[0], proj_bias(attend_b[1])]
    )
    mid_0, a2_0, f_0, u_0, h_1, a1_1, q_1, window_1, aw1, ew1, rw1, ow1 = line_call(
        first_kernel,
        "first_tail",
        1,
        [
            ((rows, model), f32),
            ((rows, model), bf16),
            ((rows, units), f32),
            ((rows, units), bf16),
            ((rows, model), f32),
            ((rows, model), bf16),
            ((rows, width), bf16),
            (((reach_back + 1) * rows, 2 * width), bf16),
            ((model, 3 * width), bf16),
            ((model, units), bf16),
            ((units, model), bf16),
            ((groups, width, model), bf16),
        ],
        extra,
        (0, 1),
        50,
        (o_0, ow0, hidden_in, vec, ew0, rw0, *shards, line_shards),
        line_gather_scratch
        + Gather.scratch() * (3 + groups)
        + Window.scratch(reach_back, CHUNKS),
    )
    o_1, lse_1 = attend_forward(q_1, window_1, marks[0], marks[1])

    vec = stack_rows(model, [br1[0], g1[1], c1[1], eb1, br1[1]])
    a2_1, u_1, eb_1, dfb_1, dmid_1, db_1, do_1, mid_1, sums_1 = line_call(
        turn_kernel,
        "turn_tail",
        2,
        [
            ((rows, model), bf16),
            ((rows, units), bf16),
            ((rows, model), bf16),
            ((rows, units), bf16),
            ((rows, model), f32),
            ((rows, model), bf16),
            ((rows, width), bf16),
            ((rows, model), f32),
            ((8, model), f32),
        ],
        extra,
        (0, 1),
        60,
        (o_1, ow1, h_1, vec, ew1, rw1, out_grad),
        line_gather_scratch,
    )
    last_sum = (u_1, rw1, mid_1, stack_rows(model, [br1[1]]))
    dproj_1, attend_bias_1, expand_1, reduce_1, output_1, attend_1, low_out = return_call(
        "return_one",
        6,
        0,
        reach_back,
        (q_1, window_1, lse_1, do_1, *marks, a2_1, dfb_1, u_1, eb_1, o_1, db_1, a1_1, *last_sum),
    )
    grads_1 = (expand_1, reduce_1, attend_1, output_1)
    owned = [((g.shape[0] // size, g.shape[1]), f32) for g in grads_1]

    def scatter_scratch(pieces):
        return sum((Scatter.scratch(*shape) for shape, kind in pieces), [])

    vec = stack_rows(model, [g1[0], g0[1]])
    eb_0, dfb_0, dmid_0, db_0, do_0, sums_0, *sums_of_1 = line_call(
        cross_kernel,
        "cross_tail",
        3,
        [
            ((rows, model), bf16),
            ((rows, units), bf16),
            ((rows, model), f32),
            ((rows, model), bf16),
            ((rows, width), bf16),
            ((8, model), f32),
            *owned,
        ],
        extra,
        (1, 2),
        60,
        (dproj_1, aw1, h_1, dmid_1, vec, f_0, mid_0, ew0, rw0, ow0, *grads_1),
        scatter_scratch(owned),
    )
    dproj_0, attend_bias_0, expand_0, reduce_0, output_0, attend_0, high_out = return_call(
        "return_zero",
        7,
        rows // 2,
        reach_back,
        (q_0, window_0, lse_0, do_0, *marks, a2_0, dfb_0, u_0, eb_0, o_0, db_0, a1_0, *last_sum),
    )
    hidden_out = jnp.concatenate([low_out, high_out], axis=0)
    zero = jnp.zeros((model,), f32)
    wide = [
        sums_0[6], sums_0[2], sums_1[4], sums_1[0],
        sums_0[3], sums_1[1],
        zero, sums_0[4], sums_0[0], sums_1[2],
        zero, sums_0[5], sums_0[1], sums_1[3],
    ]
    wide = jnp.stack(wide).reshape(len(wide), size, LANES)
    narrow = jnp.concatenate([attend_bias_0[:2], attend_bias_1[:2]]).reshape(4, size, width // size)
    narrow = jnp.moveaxis(narrow, 1, 0).reshape(size, 1, LANES)
    small = jnp.concatenate([narrow, jnp.moveaxis(wide, 1, 0)], axis=1).astype(bf16)
    small = jnp.pad(small, ((0, 0), (0, SMALL_ROWS - small.shape[1]), (0, 0)))
    grads_0 = (expand_0, reduce_0, attend_0, output_0, small.reshape(-1, LANES))
    owned = [((g.shape[0] // size, g.shape[1]), f32) for g in grads_0]

    vec = stack_rows(model, [g0[0]])
    in_grad, late, unused, *sums_of_0 = line_call(
        last_kernel,
        "last_tail",
        4,
        [((rows, model), f32), ((8, LANES), f32), ((8, model), f32), *owned],
        extra,
        (0, 1),
        30,
        (dproj_0, aw0, hidden_in, dmid_0, vec, *grads_0),
        [
            pltpu.VMEM((size, 8, LANES), f32),
            pltpu.VMEM((size, 8, LANES), f32),
            pltpu.SemaphoreType.DMA((size,)),
            pltpu.SemaphoreType.DMA((size,)),
            *scatter_scratch(owned),
        ],
    )
    small = sums_of_0[4]
    expand, reduced, attend, output = [jnp.stack(pair) for pair in zip(sums_of_0[:4], sums_of_1)]
    pieces = [small[1 + i : 1 + i + n] for i, n in ((0, 4), (4, 2), (6, 4), (10, 4))]
    branch, units_grad, gain, offset = pieces
    return (
        hidden_out,
        in_grad,
        attend.reshape(2, part, 3, width),
        small[0].reshape(2, 2, width // size),
        output,
        branch.reshape(2, 2, LANES),
        expand,
        units_grad,
        reduced,
        jnp.concatenate([late[0:1], gain[1:]]).reshape(2, 2, LANES),
        jnp.concatenate([late[1:2], offset[1:]]).reshape(2, 2, LANES),
    )


def layer_by_layer(hidden_in, out_grad, params, marks, reach_back, model_parts):
    share, unit_share, size, part = model_parts
    model = hidden_in.shape[1]
    saved = []
    current = hidden_in
    for layer in range(len(params)):
        current, kept_state = forward_layer(current, params[layer], marks, reach_back)
        saved.append(kept_state)
    grad_now = out_grad
    hidden_list = [None] * len(params)
    attend_list = [None] * len(params)
    small_list = [None] * len(params)
    for layer in reversed(range(len(params))):
        grad_now, expand_grad, reduce_grad, attend_grad, output_grad, small = backward_layer(
            grad_now, params[layer], saved[layer], marks, reach_back
        )
        hidden_list[layer] = scattered(
            jnp.concatenate([expand_grad, pack_output(reduce_grad, model, unit_share)], axis=1)
        )
        small_list[layer] = small
        blocks = [attend_grad, pack_output(output_grad, model, share)]
        if layer == 0:
            stacked = [jnp.stack([entry[i] for entry in small_list]) for i in range(len(small))]
            flat_rows = split_owned(stacked, None, size).astype(jnp.bfloat16)
            count = flat_rows.shape[1]
            room = part * LANES * (-(-count // (part * LANES)))
            padded = jnp.pad(flat_rows, ((0, 0), (0, room - count)))
            blocks.append(padded.reshape(size * part, room // part))
        packed = jnp.concatenate(blocks, axis=1)
        if layer > 0:
            grad_now, packed = lax.optimization_barrier((grad_now, packed))
        attend_list[layer] = scattered(packed)
    return current, grad_now, hidden_list, attend_list


def local(
    hidden_in,
    doc_ids,
    attend_weight,
    attend_bias,
    output_weight,
    branch_bias,
    expand_weight,
    expand_bias,
    reduce_weight,
    norm_gain,
    norm_bias,
    out_grad,
):
    size = lax.axis_size("dp")
    layer_count, part, three, width = attend_weight.shape
    tok_rows, model = hidden_in.shape
    share = output_weight.shape[1]
    unit_share = reduce_weight.shape[1]
    hidden_units = expand_weight.shape[2]
    reach_back = (CTX + tok_rows - 2) // tok_rows
    own_row = doc_ids + 1
    small_in = (attend_bias, branch_bias, expand_bias, norm_gain, norm_bias)
    on_cube = size == 8 and lax.axis_size("tensor") == 4 and layer_count == 2
    if on_cube and part == unit_share == LANES and tok_rows == 4 * LANES and width == 2 * LANES:
        return pair_layers(
            hidden_in,
            out_grad,
            (attend_weight, output_weight, expand_weight, reduce_weight),
            small_in,
            own_row,
            reach_back,
            (share, unit_share, size, part),
        )
    else:
        mark_list = [passed_along(own_row, "dp", hop) for hop in range(reach_back, 0, -1)]
        marks = (own_row[:, None], jnp.concatenate(mark_list + [own_row])[None, :])
        flat = jnp.concatenate([entry.reshape(-1) for entry in small_in])
        flat_all = lax.all_gather(flat[None], "dp", axis=0, tiled=True)
        small_full = []
        at = 0
        for entry in small_in:
            piece = flat_all[:, at : at + entry.size].reshape((size,) + entry.shape)
            at += entry.size
            piece = jnp.moveaxis(piece, 0, -2)
            small_full.append(
                piece.reshape(entry.shape[:-1] + (size * entry.shape[-1],)).astype(jnp.float32)
            )
        attend_b, branches, expand_b, gains, offsets = small_full

        params = []
        for layer in range(layer_count):
            first = lax.all_gather(
                jnp.concatenate(
                    [
                        attend_weight[layer].reshape(part, three * width),
                        pack_output(output_weight[layer], model, share),
                    ],
                    axis=1,
                ),
                "dp",
                axis=0,
                tiled=True,
            )
            second = lax.all_gather(
                jnp.concatenate(
                    [expand_weight[layer], pack_output(reduce_weight[layer], model, unit_share)],
                    axis=1,
                ),
                "dp",
                axis=0,
                tiled=True,
            )
            params.append(
                (
                    first[:, : three * width],
                    attend_b[layer],
                    unpack_output(first[:, three * width :], model, share),
                    branches[layer],
                    second[:, :hidden_units],
                    expand_b[layer],
                    unpack_output(second[:, hidden_units:], model, unit_share),
                    gains[layer],
                    offsets[layer],
                )
            )
        current, grad_now, hidden_list, attend_list = layer_by_layer(
            hidden_in, out_grad, params, marks, reach_back, (share, unit_share, size, part)
        )
    hidden_out = [entry.astype(jnp.float32) for entry in hidden_list]
    attend_out = [entry.astype(jnp.float32) for entry in attend_list]
    fold = three * width
    slab = model * share // part
    tail = attend_out[0][:, fold + slab :].reshape(-1)
    small_out = []
    at = 0
    for entry in small_in:
        small_out.append(tail[at : at + entry.size].reshape(entry.shape))
        at += entry.size
    attend_bgrad, branch_bgrad, expand_bgrad, gain_grad, offset_grad = small_out
    return (
        current,
        grad_now,
        jnp.stack([entry[:, :fold].reshape(part, three, width) for entry in attend_out]),
        attend_bgrad,
        jnp.stack([unpack_output(entry[:, fold : fold + slab], model, share) for entry in attend_out]),
        branch_bgrad,
        jnp.stack([entry[:, :hidden_units] for entry in hidden_out]),
        expand_bgrad,
        jnp.stack(
            [unpack_output(entry[:, hidden_units:], model, unit_share) for entry in hidden_out]
        ),
        gain_grad,
        offset_grad,
    )


def solution(mesh):
    return jax.shard_map(
        local,
        mesh=mesh,
        in_specs=(
            P("dp", None),
            P("dp"),
            P(None, "dp", None, "tensor"),
            P(None, None, ("tensor", "dp")),
            P(None, ("tensor", "dp"), None),
            P(None, None, "dp"),
            P(None, "dp", "tensor"),
            P(None, ("tensor", "dp")),
            P(None, ("tensor", "dp"), None),
            P(None, None, "dp"),
            P(None, None, "dp"),
            P("dp", None),
        ),
        out_specs=(
            P("dp", None),
            P("dp", None),
            P(None, "dp", None, "tensor"),
            P(None, None, ("tensor", "dp")),
            P(None, ("tensor", "dp"), None),
            P(None, None, "dp"),
            P(None, "dp", "tensor"),
            P(None, ("tensor", "dp")),
            P(None, ("tensor", "dp"), None),
            P(None, None, "dp"),
            P(None, None, "dp"),
        ),
        check_vma=False,
    )
```
